256 devices in a mesh: dp: 16 (over z, core), expert: 16 (over y, x).
Axes of the slice: x: 4, y: 4, z: 8, core: 2. Of those that a mesh axis runs over, the one named last changes fastest.
Arguments:
- gen_rows: bfloat16 [32768, 2048], P(('dp', 'expert')), may hold values from -6 to 6
- gen_lengths: int32 [16, 16, 8], P('dp', 'expert'), may hold values from 1 to 16, as said below
- gen_adv: bfloat16 [16, 16, 8], P('dp', 'expert'), may hold values from -4 to 4
- destination: int32 [16, 16, 8], P('dp', 'expert'), may hold values from 0 to 15, as said below
- expert_ids: int32 [32768, 2], P(('dp', 'expert')), may hold values from 0 to 15, all different within a row; in each aligned block of 128 rows (0 to 127, 128 to 255, ...) at most 32 rows name the same one
- gate_values: float32 [32768, 2], P(('dp', 'expert')), may hold values from 0.1 to 1
- cotangent: bfloat16 [32768, 2048], P(('dp', 'expert')), may hold values from -6 to 6
- w_gate: bfloat16 [16, 2048, 768], P('expert'), may hold values from -0.125 to 0.125
- w_up: bfloat16 [16, 2048, 768], P('expert'), may hold values from -0.125 to 0.125
- w_down: bfloat16 [16, 768, 2048], P('expert'), may hold values from -0.21875 to 0.21875
Outputs:
- layer_out: bfloat16 [32768, 2048], P(('dp', 'expert'))
- input_grad: bfloat16 [32768, 2048], P(('dp', 'expert'))
- grad_gate: bfloat16 [16, 2048, 768], P('expert', 'dp')
- grad_up: bfloat16 [16, 2048, 768], P('expert', 'dp')
- grad_down: bfloat16 [16, 768, 2048], P('expert', 'dp')
The draws below stay inside these ranges and needn't reach their ends.
Inputs may be any that keep to these rules, and one draw needn't show every extreme that they name: `gen_lengths`: every device holds a sequence of exactly 16 tokens. `destination`: the sequences of one generation device go to distinct trainer ranks, and each trainer device receives exactly 8 sequences. `expert_ids`: within the rows of one device, no expert is named more than 32 times, a bound that some block reaches.
All inputs are finite; a program needn't handle non-finite values.
Results may differ from the reference program's by a relative error of at most 0.017.
Values may be sent and summed in bfloat16 or wider, within the bound.
A program may use at most 128 MiB of HBM per device.

```python
import math
import jax
import jax.numpy as jnp
import numpy as np
from jax import lax

D = 2048
FF = 768
TOP = 2
SEQ_DEV = 8
SLOT = 16
EXPERTS = 16
CAPE = 32
ROWS = 32768
N_DP = 16
N_EXPERT = 16


def draw_gen_lengths(key, part):
    subkeys = jax.random.split(key, 2)
    lengths = jax.random.randint(subkeys[0], (N_DP, N_EXPERT, SEQ_DEV), 1, SLOT + 1)
    longest = jax.random.randint(subkeys[1], (N_DP, N_EXPERT, 1), 0, SEQ_DEV)
    places = jnp.arange(SEQ_DEV, dtype=jnp.int32)[None, None, :]
    return jnp.where(places == longest, SLOT, lengths).astype(jnp.int32)


def draw_destination(key, part):
    subkeys = jax.random.split(key, 3)
    first_perm = jax.vmap(lambda k: jax.random.permutation(k, N_DP))(jax.random.split(subkeys[0], N_EXPERT))
    second_perm = jax.vmap(lambda k: jax.random.permutation(k, N_DP))(jax.random.split(subkeys[1], N_EXPERT))
    rotation = jax.random.randint(subkeys[2], (N_DP, N_EXPERT), 0, SEQ_DEV)
    offset = (jnp.arange(SEQ_DEV, dtype=jnp.int32)[None, None, :] + rotation[:, :, None]) % SEQ_DEV
    circle = (first_perm.T[:, :, None] + offset) % N_DP
    trainer = second_perm[jnp.arange(N_EXPERT, dtype=jnp.int32)[None, :, None], circle]
    return trainer.astype(jnp.int32)


def levels(stream_key, extent, cuts, smallest, high):
    loudness, own = 1.0, jax.random.fold_in(stream_key, 6)
    for dim, shards_of in cuts:
        heights = jnp.exp(jax.random.uniform(jax.random.fold_in(own, dim), (shards_of,), jnp.float32, smallest / len(cuts), high / len(cuts)))
        loudness = loudness * jnp.repeat(heights, extent[dim] // shards_of).reshape([-1 if axis == dim else 1 for axis in range(len(extent))])
    return loudness


def deal_out(own_key, own, number, rows, count, top, bound, lean):
    sequence = jax.random.permutation(own_key, count)
    crowded, common = load_shares(count, rows * top, bound, lean, True), load_shares(count, rows * top, bound, lean, False)
    places = jnp.arange(count)

    def named(sizes, turn):
        used = int((sizes > 0).sum())
        fixed = max(1, used // 4)
        passed = fixed + (places - fixed + turn * (used - fixed)) % max(1, count - fixed)
        return jnp.zeros((count,), jnp.int32).at[sequence[jnp.where(places < fixed, places, passed)]].set(jnp.asarray(sizes, jnp.int32))

    sizes = jnp.where(number % 4 == 0, named(crowded, number // 4), named(common, number - number // 4 - 1))
    mixed = jax.random.permutation(jax.random.fold_in(own, 3), count)
    giver, receiver = mixed[0:count // 2 * 2:2], mixed[1:count // 2 * 2:2]
    room = jnp.minimum(sizes[giver] - 1, bound - sizes[receiver]) // 2
    room = jnp.where((giver == sequence[0]) | (receiver == sequence[0]) | (sizes[receiver] == 0), 0, jnp.maximum(room, 0))
    passed = jax.random.randint(jax.random.fold_in(own, 4), (count // 2,), 0, 1 << 20) % (room + 1)
    sizes = sizes.at[giver].add(-passed).at[receiver].add(passed)
    items = jnp.searchsorted(jnp.cumsum(sizes), jnp.arange(rows * top), side="right").astype(jnp.int32)
    table = items.reshape(top, rows).T
    table = table[jax.random.permutation(jax.random.fold_in(own, 1), rows)]
    turn = jax.random.randint(jax.random.fold_in(own, 2), (rows, 1), 0, top)
    return jnp.take_along_axis(table, (jnp.arange(top)[None, :] + turn) % top, axis=1)


def load_shares(number_of, total, limit, skew, full):
    portions = [(1 << 20) // math.isqrt(standing ** skew) + 1 for standing in range(1, number_of + 1)]
    largest = limit if full else min(limit, max(-(-total // number_of), total * portions[0] // sum(portions)))
    least = 1 if total - largest >= number_of - 1 else 0
    counts, spare = [largest] + [least] * (number_of - 1), total - largest - least * (number_of - 1)
    while spare > 0:
        movable = [i for i in range(1, number_of) if counts[i] < largest] or [i for i in range(1, number_of) if counts[i] < limit]
        whole, budget = sum([portions[i] for i in movable]), spare
        for i in movable:
            addition = min(limit - counts[i], max(1, budget * portions[i] // whole), spare)
            counts[i] = counts[i] + addition
            spare = spare - addition
    return np.array(counts)


def scatter_about(stream_key, dims, deviation, bound, cuts=(), held_as=jnp.bfloat16):
    values = jax.random.normal(stream_key, dims, jnp.float32) * deviation
    if len(cuts) > 0:
        values = levels(stream_key, dims, cuts, -0.22, 0.18) * values
    return jnp.clip(values, min=-bound, max=bound).astype(held_as)


def setup_inputs(seed: int = 0) -> dict:
    seeds = jax.random.split(jax.random.key(seed), 11)
    gen_rows = scatter_about(seeds[0], (ROWS, D), 1.0, 6.0, ((0, 256),))
    gen_lengths = draw_gen_lengths(jax.random.fold_in(seeds[10], 71), 0)
    gen_adv = scatter_about(seeds[2], (N_DP, N_EXPERT, SEQ_DEV), 1.0, 4.0, ((0, 16), (1, 16)))
    destination = draw_destination(jax.random.fold_in(seeds[10], 71), 0)
    expert_ids_keys = jax.random.split(jax.random.fold_in(seeds[4], 1), ROWS // (SEQ_DEV * SLOT))
    expert_ids_turns = jax.random.permutation(jax.random.fold_in(seeds[4], 3), ROWS // (SEQ_DEV * SLOT))
    expert_ids = jax.vmap(lambda own, number: deal_out(jax.random.fold_in(seeds[4], 2), own, number, SEQ_DEV * SLOT, EXPERTS, TOP, CAPE, 2))(expert_ids_keys, expert_ids_turns).reshape((ROWS, TOP))
    gate_values = jnp.clip(0.1 + 0.9 * jax.random.uniform(seeds[5], (ROWS, TOP), jnp.float32) ** levels(seeds[5], (ROWS, TOP), ((0, 256),), -0.2, 0.2), 0.1, 1.0)
    cotangent = scatter_about(seeds[6], (ROWS, D), 1.0, 6.0, ((0, 256),))
    w_gate = scatter_about(seeds[7], (EXPERTS, D, FF), D ** -0.5, 0.125, ((0, 16),))
    w_up = scatter_about(seeds[8], (EXPERTS, D, FF), D ** -0.5, 0.125, ((0, 16),))
    w_down = scatter_about(seeds[9], (EXPERTS, FF, D), FF ** -0.5, 0.21875, ((0, 16),))
    return dict(gen_rows=gen_rows, gen_lengths=gen_lengths, gen_adv=gen_adv, destination=destination, expert_ids=expert_ids, gate_values=gate_values, cotangent=cotangent, w_gate=w_gate, w_up=w_up, w_down=w_down)


def contract(left, right, left_dim, right_dim):
    return lax.dot_general(left, right, (((left_dim,), (right_dim,)), ((), ())), preferred_element_type=jnp.float32)


def expert_pass(expert_in, expert_dy, weight_gate, weight_up, weight_down):
    gate_pre = jnp.dot(expert_in, weight_gate, preferred_element_type=jnp.float32)
    up_pre = jnp.dot(expert_in, weight_up, preferred_element_type=jnp.float32)
    sigmoid_g = jax.nn.sigmoid(gate_pre)
    activated = gate_pre * sigmoid_g
    hidden = (activated * up_pre).astype(jnp.bfloat16)
    outputs = jnp.dot(hidden, weight_down, preferred_element_type=jnp.float32).astype(jnp.bfloat16)
    hidden_grad = contract(expert_dy, weight_down, 1, 1)
    gate_grad = (hidden_grad * up_pre * sigmoid_g * (1.0 + gate_pre * (1.0 - sigmoid_g))).astype(jnp.bfloat16)
    up_grad = (hidden_grad * activated).astype(jnp.bfloat16)
    input_rows = (contract(gate_grad, weight_gate, 1, 1) + contract(up_grad, weight_up, 1, 1)).astype(jnp.bfloat16)
    grad_g = contract(expert_in, gate_grad, 0, 0).astype(jnp.bfloat16)
    grad_u = contract(expert_in, up_grad, 0, 0).astype(jnp.bfloat16)
    grad_d = contract(hidden, expert_dy, 0, 0).astype(jnp.bfloat16)
    return outputs, input_rows, grad_g, grad_u, grad_d


def reference(gen_rows, gen_lengths, gen_adv, destination, expert_ids, gate_values, cotangent, w_gate, w_up, w_down):
    n_gen, n_ex, seq_dev = destination.shape
    model_width = gen_rows.shape[1]
    total_rows = gen_rows.shape[0]
    slot_len = total_rows // (n_gen * n_ex * seq_dev)
    per_token = expert_ids.shape[1]
    experts = w_gate.shape[0]
    hidden_units = w_gate.shape[2]
    tok_rows = seq_dev * slot_len
    capacity = 2 * tok_rows * per_token // experts
    send_table = (destination[..., None] == jnp.arange(n_gen, dtype=jnp.int32)).astype(jnp.int32)
    to_peer = jnp.sum(send_table, axis=2)
    before = jnp.cumsum(to_peer, axis=0) - to_peer
    arrival = jnp.take_along_axis(before, destination, axis=2)
    ex_idx = jnp.arange(n_ex, dtype=jnp.int32)[None, :, None]
    train_seq = ((destination * n_ex + ex_idx) * seq_dev + arrival).reshape(-1).astype(jnp.int32)
    row_index = (train_seq[:, None] * slot_len + jnp.arange(slot_len, dtype=jnp.int32)[None, :]).reshape(-1)
    train_rows = jnp.zeros_like(gen_rows).at[row_index].set(gen_rows)
    total_seq = n_gen * n_ex * seq_dev
    train_len = jnp.zeros((total_seq,), jnp.int32).at[train_seq].set(gen_lengths.reshape(-1))
    train_adv = jnp.zeros((total_seq,), jnp.float32).at[train_seq].set(gen_adv.reshape(-1).astype(jnp.float32))
    position = jnp.arange(total_rows, dtype=jnp.int32) % slot_len
    seq_of = jnp.arange(total_rows, dtype=jnp.int32) // slot_len
    in_length = position < train_len[seq_of]
    seq_scale = jnp.where(in_length, train_adv[seq_of] / train_len[seq_of].astype(jnp.float32), jnp.float32(0.0))
    token_dy = seq_scale[:, None] * cotangent.astype(jnp.float32)
    pair_dy = (gate_values[:, :, None] * token_dy[:, None, :]).astype(jnp.bfloat16)
    rows_d = n_ex * tok_rows
    pair_count = rows_d * per_token
    buffer_rows = n_ex * capacity

    def row_step(totals, inputs):
        x_rows, ids_rows, gates_rows, dy_rows = inputs
        flat_ids = ids_rows.reshape(-1)
        dy_flat = dy_rows.reshape(pair_count, model_width)

        def per_expert(expert):
            is_hit = flat_ids == expert
            running = jnp.cumsum(is_hit.astype(jnp.int32)) - 1
            target = jnp.where(is_hit, running, buffer_rows)
            source = jnp.full((buffer_rows,), pair_count, jnp.int32).at[target].set(jnp.arange(pair_count, dtype=jnp.int32), mode="drop")
            is_valid = source < pair_count
            safe_index = jnp.minimum(source, pair_count - 1)
            expert_in = jnp.where(is_valid[:, None], x_rows[safe_index // per_token], jnp.zeros((), jnp.bfloat16))
            expert_dy = jnp.where(is_valid[:, None], dy_flat[safe_index], jnp.zeros((), jnp.bfloat16))
            outputs, input_rows, grad_g, grad_u, grad_d = expert_pass(expert_in, expert_dy, w_gate[expert], w_up[expert], w_down[expert])
            return outputs, input_rows, source, grad_g, grad_u, grad_d

        outputs, input_rows, source, grad_g, grad_u, grad_d = lax.map(per_expert, jnp.arange(experts, dtype=jnp.int32))
        flat_source = source.reshape(-1)
        pair_out = jnp.zeros((pair_count + 1, model_width), jnp.bfloat16).at[flat_source].set(outputs.reshape(-1, model_width))[:pair_count]
        pair_dx = jnp.zeros((pair_count + 1, model_width), jnp.bfloat16).at[flat_source].set(input_rows.reshape(-1, model_width))[:pair_count]
        out_rows = jnp.sum(gates_rows[:, :, None] * pair_out.reshape(rows_d, per_token, model_width).astype(jnp.float32), axis=1).astype(jnp.bfloat16)
        dx_rows = jnp.sum(pair_dx.reshape(rows_d, per_token, model_width).astype(jnp.float32), axis=1).astype(jnp.bfloat16)
        totals = (totals[0] + grad_g.astype(jnp.float32), totals[1] + grad_u.astype(jnp.float32), totals[2] + grad_d.astype(jnp.float32))
        return totals, (out_rows, dx_rows)

    start = (jnp.zeros((experts, model_width, hidden_units), jnp.float32), jnp.zeros((experts, model_width, hidden_units), jnp.float32), jnp.zeros((experts, hidden_units, model_width), jnp.float32))
    inputs = (train_rows.reshape(n_gen, rows_d, model_width), expert_ids.reshape(n_gen, rows_d, per_token), gate_values.reshape(n_gen, rows_d, per_token), pair_dy.reshape(n_gen, rows_d, per_token, model_width))
    totals, stacked = lax.scan(row_step, start, inputs)
    layer_out = stacked[0].reshape(total_rows, model_width)
    input_grad = stacked[1].reshape(total_rows, model_width)
    return layer_out, input_grad, totals[0].astype(jnp.bfloat16), totals[1].astype(jnp.bfloat16), totals[2].astype(jnp.bfloat16)
```

```python
import functools

import jax
import jax.numpy as jnp
from jax import lax
from jax.sharding import PartitionSpec as P


def contract(left, right, left_dim, right_dim):
    return lax.dot_general(
        left, right, (((left_dim,), (right_dim,)), ((), ())), preferred_element_type=jnp.float32
    )


def on_device(
    gen_rows,
    gen_lengths,
    gen_adv,
    destination,
    expert_ids,
    gate_values,
    cotangent,
    w_gate,
    w_up,
    w_down,
):
    n_dp = lax.axis_size("dp")
    n_ex = lax.axis_size("expert")
    seq_dev = destination.shape[2]
    model_width = gen_rows.shape[1]
    slot_len = gen_rows.shape[0] // seq_dev
    per_token = expert_ids.shape[1]
    tok_rows = seq_dev * slot_len
    capacity = 2 * tok_rows * per_token // n_ex
    weight_gate = w_gate[0]
    weight_up = w_up[0]
    weight_down = w_down[0]
    hidden_units = weight_gate.shape[1]
    targets = destination[0, 0]
    bf = jnp.bfloat16
    peer_ids = jnp.arange(n_dp, dtype=jnp.int32)
    matches = targets[None, :] == peer_ids[:, None]
    same_place = jnp.arange(slot_len)[:, None] == jnp.arange(slot_len)[None, :]
    spread = (
        (matches[:, None, :, None] & same_place[None, :, None, :])
        .astype(bf)
        .reshape(n_dp * slot_len, tok_rows)
    )
    out_rows = jnp.dot(spread, gen_rows, preferred_element_type=jnp.float32).astype(bf)
    lens_adv = jnp.stack(
        [gen_lengths[0, 0].astype(jnp.float32), gen_adv[0, 0].astype(jnp.float32)], axis=0
    )
    out_meta = jnp.sum(jnp.where(matches[:, None, :], lens_adv[None], 0.0), axis=2)
    got_meta = lax.all_to_all(out_meta, "dp", split_axis=0, concat_axis=0, tiled=True)
    got_rows = lax.all_to_all(out_rows, "dp", split_axis=0, concat_axis=0, tiled=True)
    got_lengths, got_adv = got_meta[:, 0], got_meta[:, 1]
    arrived = got_lengths > 0
    earlier = peer_ids[None, :] < peer_ids[:, None]
    arrival = jnp.sum((earlier & arrived[None, :]).astype(jnp.int32), axis=1)
    chosen = arrived[None, :] & (arrival[None, :] == jnp.arange(seq_dev, dtype=jnp.int32)[:, None])
    place = (
        (chosen[:, None, :, None] & same_place[None, :, None, :])
        .astype(bf)
        .reshape(tok_rows, n_dp * slot_len)
    )
    seq_scale8 = jnp.where(arrived, got_adv / jnp.maximum(got_lengths, 1.0), 0.0)
    train_scale = jnp.sum(jnp.where(chosen, seq_scale8[None, :], 0.0), axis=1)
    train_lengths = jnp.sum(jnp.where(chosen, got_lengths[None, :], 0.0), axis=1)
    tok = jnp.arange(tok_rows, dtype=jnp.int32)
    position = (tok % slot_len).astype(jnp.float32)
    tok_len = jnp.repeat(train_lengths, slot_len)
    tok_scale = jnp.where(position < tok_len, jnp.repeat(train_scale, slot_len), 0.0)
    experts = jnp.arange(n_ex, dtype=jnp.int32)
    named = [expert_ids[:, k][None, :] == experts[:, None] for k in range(per_token)]
    routed = functools.reduce(jnp.logical_or, named)
    gate_of = sum(jnp.where(named[k], gate_values[:, k][None, :], 0.0) for k in range(per_token))
    before = (tok[:, None] < tok[None, :]).astype(bf)
    pos = jnp.dot(routed.astype(bf), before, preferred_element_type=jnp.float32)
    code = jnp.where(routed, pos, -1.0)
    buffer_rows = n_ex * capacity
    hit = code[:, None, :] == jnp.arange(capacity, dtype=jnp.float32)[None, :, None]
    pick = hit.astype(bf).reshape(buffer_rows, tok_rows)
    weighted = jnp.where(hit, gate_of[:, None, :], 0.0).reshape(buffer_rows, tok_rows)
    row_scale = jnp.sum(
        jnp.where(hit, (gate_of * tok_scale[None, :])[:, None, :], 0.0), axis=2
    ).reshape(buffer_rows, 1)
    send_dy = (
        (jnp.dot(pick, cotangent, preferred_element_type=jnp.float32) * row_scale)
        .astype(bf)
        .reshape(n_ex, capacity, model_width)
    )
    pick_got = jnp.dot(pick, place, preferred_element_type=jnp.float32).astype(bf)
    send_rows = (
        jnp.dot(pick_got, got_rows, preferred_element_type=jnp.float32)
        .astype(bf)
        .reshape(n_ex, capacity, model_width)
    )
    expert_in = lax.all_to_all(send_rows, "expert", split_axis=0, concat_axis=0, tiled=True)
    flat_in = expert_in.reshape(-1, model_width)
    gate_pre = jnp.dot(flat_in, weight_gate, preferred_element_type=jnp.float32)
    up_pre = jnp.dot(flat_in, weight_up, preferred_element_type=jnp.float32)
    hidden = (gate_pre * jax.nn.sigmoid(gate_pre) * up_pre).astype(jnp.bfloat16)
    outputs = (
        jnp.dot(hidden, weight_down, preferred_element_type=jnp.float32)
        .astype(jnp.bfloat16)
        .reshape(expert_in.shape)
    )
    returned = lax.all_to_all(outputs, "expert", split_axis=0, concat_axis=0, tiled=True)
    item_shape = (expert_in.shape[0], expert_in.shape[1], hidden_units)
    returned, expert_in, gate_all, up_all = (
        returned,
        expert_in,
        gate_pre.reshape(item_shape),
        up_pre.reshape(item_shape),
    )
    hi = weighted.astype(bf)
    lo = (weighted - hi.astype(jnp.float32)).astype(bf)
    flat_back = returned.reshape(buffer_rows, model_width)
    layer_out = (contract(hi, flat_back, 0, 0) + contract(lo, flat_back, 0, 0)).astype(bf)
    expert_dy = lax.all_to_all(send_dy, "expert", split_axis=0, concat_axis=0, tiled=True).reshape(
        -1, model_width
    )
    flat_in = expert_in.reshape(-1, model_width)
    gate_flat = gate_all.reshape(-1, hidden_units)
    up_flat = up_all.reshape(-1, hidden_units)
    sigmoid_g = jax.nn.sigmoid(gate_flat)
    activated = gate_flat * sigmoid_g
    hidden = (activated * up_flat).astype(jnp.bfloat16)
    hidden_grad = contract(expert_dy, weight_down, 1, 1)
    gate_grad = (hidden_grad * up_flat * sigmoid_g * (1.0 + gate_flat * (1.0 - sigmoid_g))).astype(
        jnp.bfloat16
    )
    up_grad = (hidden_grad * activated).astype(jnp.bfloat16)
    input_rows = (
        (contract(gate_grad, weight_gate, 1, 1) + contract(up_grad, weight_up, 1, 1))
        .astype(jnp.bfloat16)
        .reshape(n_ex, capacity, model_width)
    )
    back_rows = lax.all_to_all(input_rows, "expert", split_axis=0, concat_axis=0, tiled=True)
    input_grad = contract(pick, back_rows.reshape(buffer_rows, model_width), 0, 0).astype(bf)
    gate_sum, up_sum, down_sum = (
        lax.psum_scatter(
            contract(flat_in, gate_grad, 0, 0).astype(jnp.bfloat16),
            "dp",
            scatter_dimension=0,
            tiled=True,
        ).astype(jnp.float32),
        lax.psum_scatter(
            contract(flat_in, up_grad, 0, 0).astype(jnp.bfloat16),
            "dp",
            scatter_dimension=0,
            tiled=True,
        ).astype(jnp.float32),
        lax.psum_scatter(
            contract(hidden, expert_dy, 0, 0).astype(jnp.bfloat16),
            "dp",
            scatter_dimension=0,
            tiled=True,
        ).astype(jnp.float32),
    )
    return (
        layer_out,
        input_grad,
        gate_sum.astype(jnp.bfloat16)[None],
        up_sum.astype(jnp.bfloat16)[None],
        down_sum.astype(jnp.bfloat16)[None],
    )


def solution(mesh):
    in_specs = (
        P(("dp", "expert"), None),
        P("dp", "expert", None),
        P("dp", "expert", None),
        P("dp", "expert", None),
        P(("dp", "expert"), None),
        P(("dp", "expert"), None),
        P(("dp", "expert"), None),
        P("expert", None, None),
        P("expert", None, None),
        P("expert", None, None),
    )
    out_specs = (
        P(("dp", "expert"), None),
        P(("dp", "expert"), None),
        P("expert", "dp", None),
        P("expert", "dp", None),
        P("expert", "dp", None),
    )
    return jax.shard_map(
        on_device, mesh=mesh, in_specs=in_specs, out_specs=out_specs, check_vma=False
    )
```

```python
import functools

import jax
import jax.numpy as jnp
from jax import lax
from jax.experimental import pallas as pl
from jax.experimental.pallas import tpu as pltpu
from jax.sharding import PartitionSpec as P

MESH = pl.DeviceIdType.MESH
BF = jnp.bfloat16
F32 = jnp.float32


def contract(left, right, left_dim, right_dim):
    return lax.dot_general(
        left, right, (((left_dim,), (right_dim,)), ((), ())), preferred_element_type=F32
    )


def iota(shape, dim):
    return lax.broadcasted_iota(jnp.int32, shape, dim)


def step_kernel(
    n_dp,
    n_ex,
    slot,
    cap,
    small_ref,
    gen_ref,
    cot_ref,
    wg_hbm,
    wu_hbm,
    wd_hbm,
    out_ref,
    dx_ref,
    gg_out,
    gu_out,
    gd_out,
    wg,
    wu,
    wd,
    meta_send,
    meta_recv,
    seq_send,
    seq_recv,
    x_send,
    x_recv,
    y_send,
    y_recv,
    o_send,
    o_recv,
    b_send,
    b_recv,
    pick,
    hi,
    lo,
    fac_a,
    fac_b,
    hid,
    gg,
    ug,
    grad_g,
    grad_u,
    grad_d,
    twin_g,
    twin_u,
    twin_d,
    ring_g,
    ring_u,
    ring_d,
    w_sem,
    meta_ss,
    meta_rs,
    seq_ss,
    seq_rs,
    x_ss,
    x_rs,
    y_ss,
    y_rs,
    o_ss,
    o_rs,
    b_ss,
    b_rs,
    twin_ss,
    twin_rs,
    ring_ss,
    ring_rs,
):
    g = lax.axis_index("dp")
    e = lax.axis_index("expert")
    core = lax.rem(g, 2)
    z = lax.div(g, 2)
    n_z = n_dp // 2
    half = n_z // 2
    rows = gen_ref.shape[0]
    width = gen_ref.shape[1]
    ff = wg.shape[1]
    slots = n_ex * cap
    dtile = min(256, width)
    ftile = min(256, ff)
    nd, nf = width // dtile, ff // ftile

    weights = [
        pltpu.make_async_copy(src, dst, w_sem.at[i])
        for i, (src, dst) in enumerate(((wg_hbm, wg), (wu_hbm, wu), (wd_hbm, wd)))
    ]
    for copy in weights:
        copy.start()

    barrier = pltpu.get_barrier_semaphore()

    @pl.loop(1, n_dp)
    def _(o):
        pl.semaphore_signal(barrier, 1, device_id={"dp": lax.rem(g + o, n_dp)}, device_id_type=MESH)

    @pl.loop(1, n_ex)
    def _(o):
        pl.semaphore_signal(
            barrier, 1, device_id={"expert": lax.rem(e + o, n_ex)}, device_id_type=MESH
        )

    shift = slot.bit_length() - 1
    dest_row = small_ref[0:1, :]
    len_row = small_ref[1:2, :]
    adv_row = small_ref[2:3, :]
    srow, scol = iota((n_dp * slot, rows), 0), iota((n_dp * slot, rows), 1)
    spread = (dest_row == (srow >> shift).astype(F32)) & ((srow & (slot - 1)) == (scol & (slot - 1)))
    spread = spread.astype(BF)
    mine = dest_row == iota((n_dp, rows), 0).astype(F32)
    first = (iota((n_dp, rows), 1) & (slot - 1)) == 0
    len_to = jnp.max(jnp.where(mine, len_row, 0.0), axis=1, keepdims=True)
    adv_to = jnp.sum(jnp.where(mine & first, adv_row, 0.0), axis=1, keepdims=True)
    line = iota((n_dp, 8, 128), 1)
    meta_send[...] = jnp.where(line == 0, len_to[:, :, None], adv_to[:, :, None])

    @pl.loop(0, nd)
    def _(j):
        cols = pl.ds(pl.multiple_of(j * dtile, dtile), dtile)
        seq_send[:, :, cols] = (
            jnp.dot(spread, gen_ref[:, cols], preferred_element_type=F32)
            .astype(BF)
            .reshape(n_dp, slot, dtile)
        )

    names = iota((n_ex, rows), 0).astype(F32)
    hit0, hit1 = small_ref[3:4, :] == names, small_ref[4:5, :] == names
    routed = hit0 | hit1
    gate_of = jnp.where(hit0, small_ref[5:6, :], 0.0) + jnp.where(hit1, small_ref[6:7, :], 0.0)
    before = (iota((rows, rows), 0) < iota((rows, rows), 1)).astype(BF)
    pos = jnp.dot(routed.astype(BF), before, preferred_element_type=F32)
    code = jnp.where(routed, pos, -1.0)
    hit = code[:, None, :] == iota((n_ex, cap, rows), 1).astype(F32)
    picked = hit.astype(BF).reshape(slots, rows)
    pick[...] = picked
    weighted = jnp.where(hit, gate_of[:, None, :], 0.0).reshape(slots, rows)
    whole = weighted.astype(BF)
    hi[...] = whole
    lo[...] = (weighted - whole.astype(F32)).astype(BF)

    pl.semaphore_wait(barrier, n_dp + n_ex - 2)

    def exchange(axis, me, n, send, recv, ss, rs):
        def copy(o):
            peer = lax.rem(me + o, n)
            return pltpu.make_async_remote_copy(
                src_ref=send.at[peer],
                dst_ref=recv.at[me],
                send_sem=ss.at[o],
                recv_sem=rs.at[o],
                device_id={axis: peer},
                device_id_type=MESH,
            )

        def own():
            return pltpu.make_async_copy(send.at[me], recv.at[me], ss.at[0])

        def start():
            own().start()

            @pl.loop(1, n)
            def _(o):
                copy(o).start()

        def wait_recv():
            own().wait()

            @pl.loop(1, n)
            def _(o):
                copy(o).wait_recv()

        def wait_send():
            @pl.loop(1, n)
            def _(o):
                copy(o).wait_send()

        return start, wait_recv, wait_send

    meta_start, meta_wait, meta_done = exchange("dp", g, n_dp, meta_send, meta_recv, meta_ss, meta_rs)
    seq_start, seq_wait, seq_done = exchange("dp", g, n_dp, seq_send, seq_recv, seq_ss, seq_rs)
    x_start, x_wait, x_done = exchange("expert", e, n_ex, x_send, x_recv, x_ss, x_rs)
    y_start, y_wait, y_done = exchange("expert", e, n_ex, y_send, y_recv, y_ss, y_rs)
    o_start, o_wait, o_done = exchange("expert", e, n_ex, o_send, o_recv, o_ss, o_rs)
    b_start, b_wait, b_done = exchange("expert", e, n_ex, b_send, b_recv, b_ss, b_rs)

    meta_start()
    seq_start()
    meta_wait()

    got_len = meta_recv[:, 0, :]
    got_adv = meta_recv[:, 1, :]
    alive = (got_len > 0.0).astype(BF)
    lower = (iota((n_dp, n_dp), 1) < iota((n_dp, n_dp), 0)).astype(BF)
    arrival = jnp.dot(lower, alive, preferred_element_type=F32)
    arrival = jnp.where(got_len > 0.0, arrival, -1.0)
    per_len = got_adv / jnp.maximum(got_len, 1.0)

    def widen(v):
        return jnp.broadcast_to(v[:, None, :rows], (n_dp, slot, rows)).reshape(n_dp * slot, rows)

    placed = (widen(arrival) == (scol >> shift).astype(F32)) & (
        (srow & (slot - 1)) == (scol & (slot - 1))
    )
    within = (srow & (slot - 1)).astype(F32) < widen(got_len)
    tok_scale = jnp.sum(
        jnp.where(placed & within, widen(per_len), 0.0), axis=0, keepdims=True
    )
    row_scale = jnp.sum(
        jnp.where(hit, (gate_of * tok_scale)[:, None, :], 0.0), axis=2, keepdims=True
    ).reshape(slots, 1)

    @pl.loop(0, nd)
    def _(j):
        cols = pl.ds(pl.multiple_of(j * dtile, dtile), dtile)
        rowsel = jnp.dot(pick[...], cot_ref[:, cols], preferred_element_type=F32)
        y_send[:, :, cols] = (rowsel * row_scale).astype(BF).reshape(n_ex, cap, dtile)

    y_start()
    fetch = contract(picked, placed.astype(BF), 1, 1).astype(BF)
    seq_wait()

    @pl.loop(0, nd)
    def _(j):
        cols = pl.ds(pl.multiple_of(j * dtile, dtile), dtile)
        source = seq_recv[:, :, cols].reshape(n_dp * slot, dtile)
        x_send[:, :, cols] = (
            jnp.dot(fetch, source, preferred_element_type=F32).astype(BF).reshape(n_ex, cap, dtile)
        )

    x_start()
    for copy in weights:
        copy.wait()
    x_wait()

    @pl.loop(0, nf)
    def _(j):
        cols = pl.ds(pl.multiple_of(j * ftile, ftile), ftile)
        x_all = x_recv[...].reshape(slots, width)
        gate_pre = jnp.dot(x_all, wg[:, cols], preferred_element_type=F32)
        up_pre = jnp.dot(x_all, wu[:, cols], preferred_element_type=F32)
        sig = jax.nn.sigmoid(gate_pre)
        act = gate_pre * sig
        hid[:, cols] = (act * up_pre).astype(BF)
        fac_a[:, cols] = up_pre * sig * (1.0 + gate_pre * (1.0 - sig))
        fac_b[:, cols] = act

    @pl.loop(0, nd)
    def _(j):
        cols = pl.ds(pl.multiple_of(j * dtile, dtile), dtile)
        o_send[:, :, cols] = (
            jnp.dot(hid[...], wd[:, cols], preferred_element_type=F32)
            .astype(BF)
            .reshape(n_ex, cap, dtile)
        )

    o_start()
    y_wait()

    @pl.loop(0, nf)
    def _(j):
        cols = pl.ds(pl.multiple_of(j * ftile, ftile), ftile)
        y_all = y_recv[...].reshape(slots, width)
        hidden_grad = contract(y_all, wd[cols, :], 1, 1)
        gg[:, cols] = (hidden_grad * fac_a[:, cols]).astype(BF)
        ug[:, cols] = (hidden_grad * fac_b[:, cols]).astype(BF)

    grads = ((grad_d, twin_d, ring_d, gd_out), (grad_g, twin_g, ring_g, gg_out), (grad_u, twin_u, ring_u, gu_out))

    def block(i, b, c):
        part = grads[i][1].shape[1]
        return pl.ds(pl.multiple_of((b * 2 + c) * part, part), part)

    def twin_copy(i, b):
        return pltpu.make_async_remote_copy(
            src_ref=grads[i][0].at[block(i, b, 1 - core)],
            dst_ref=grads[i][1].at[b],
            send_sem=twin_ss.at[i, b],
            recv_sem=twin_rs.at[i, b],
            device_id={"dp": g + 1 - 2 * core},
            device_id_type=MESH,
        )

    def ring_copy(i, way, s):
        grad, _, ring, _ = grads[i]
        mid = grad.shape[1] // 2
        if s == 0:
            b = lax.rem(z + half, n_z)
            cols = pl.ds(way * mid, mid)
        else:
            b = lax.rem(z + (half - s) * (1 - 2 * way) + n_z, n_z)
            cols = pl.ds(0, 2 * mid)
        return pltpu.make_async_remote_copy(
            src_ref=grad.at[block(i, b, core), cols],
            dst_ref=ring.at[way, s, :, cols],
            send_sem=ring_ss.at[i, way, s],
            recv_sem=ring_rs.at[i, way, s],
            device_id={"dp": lax.rem(g + 2 * (1 - 2 * way) + n_dp, n_dp)},
            device_id_type=MESH,
        )

    def ring_step(i, s):
        grad, twin, ring, _ = grads[i]
        mid = grad.shape[1] // 2
        if s == 0:
            b = lax.rem(z + half, n_z)
            here = block(i, b, core)
            twin_copy(i, b).wait_recv()
            grad[here, :] = (grad[here, :].astype(F32) + twin[b].astype(F32)).astype(BF)
            ring_copy(i, 0, 0).start()
            ring_copy(i, 1, 0).start()
            return
        for way in range(2):
            b = lax.rem(z + (half - s) * (1 - 2 * way) + n_z, n_z)
            here = block(i, b, core)
            twin_copy(i, b).wait_recv()
            ring_copy(i, way, s - 1).wait_recv()
            if s == 1:
                near, far = pl.ds(way * mid, mid), pl.ds((1 - way) * mid, mid)
                grad[here, near] = (
                    grad[here, near].astype(F32)
                    + twin[b, :, near].astype(F32)
                    + ring[way, 0, :, near].astype(F32)
                ).astype(BF)
                grad[here, far] = (
                    grad[here, far].astype(F32) + twin[b, :, far].astype(F32)
                ).astype(BF)
            else:
                grad[here, :] = (
                    grad[here, :].astype(F32)
                    + twin[b].astype(F32)
                    + ring[way, s - 1].astype(F32)
                ).astype(BF)
            ring_copy(i, way, s).start()

    def ring_last(i):
        grad, twin, ring, out = grads[i]
        twin_copy(i, z).wait_recv()
        ring_copy(i, 0, half - 1).wait_recv()
        ring_copy(i, 1, half - 1).wait_recv()
        here = block(i, z, core)
        out[...] = (
            grad[here, :].astype(F32)
            + twin[z].astype(F32)
            + ring[0, half - 1].astype(F32)
            + ring[1, half - 1].astype(F32)
        ).astype(BF)

    @pl.loop(0, nf * nd)
    def _(j):
        units = pl.ds(pl.multiple_of(lax.div(j, nd) * ftile, ftile), ftile)
        cols = pl.ds(pl.multiple_of(lax.rem(j, nd) * dtile, dtile), dtile)
        grad_d[units, cols] = contract(
            hid[:, units], y_recv[:, :, cols].reshape(slots, dtile), 0, 0
        ).astype(BF)

    @pl.loop(0, n_z)
    def _(k):
        twin_copy(0, lax.rem(z + half + k, n_z)).start()

    @pl.loop(0, nd)
    def _(j):
        cols = pl.ds(pl.multiple_of(j * dtile, dtile), dtile)
        b_send[:, :, cols] = (
            (contract(gg[...], wg[cols, :], 1, 1) + contract(ug[...], wu[cols, :], 1, 1))
            .astype(BF)
            .reshape(n_ex, cap, dtile)
        )

    b_start()
    ring_step(0, 0)

    pair = width // n_z

    @pl.loop(0, n_z)
    def _(k):
        b = lax.rem(z + half + k, n_z)
        cols = pl.ds(pl.multiple_of(b * pair, pair), pair)
        x_part = x_recv[:, :, cols].reshape(slots, pair)
        grad_g[cols, :] = contract(x_part, gg[...], 0, 0).astype(BF)
        grad_u[cols, :] = contract(x_part, ug[...], 0, 0).astype(BF)
        twin_copy(1, b).start()
        twin_copy(2, b).start()

    ring_step(1, 0)
    ring_step(2, 0)
    for s in range(1, half):
        for i in range(3):
            ring_step(i, s)

    o_wait()

    @pl.loop(0, nd)
    def _(j):
        cols = pl.ds(pl.multiple_of(j * dtile, dtile), dtile)
        back = o_recv[:, :, cols].reshape(slots, dtile)
        out_ref[:, cols] = (contract(hi[...], back, 0, 0) + contract(lo[...], back, 0, 0)).astype(BF)

    b_wait()

    @pl.loop(0, nd)
    def _(j):
        cols = pl.ds(pl.multiple_of(j * dtile, dtile), dtile)
        back = b_recv[:, :, cols].reshape(slots, dtile)
        dx_ref[:, cols] = contract(pick[...], back, 0, 0).astype(BF)

    for i in range(3):
        ring_last(i)

    for done in (meta_done, seq_done, x_done, y_done, o_done, b_done):
        done()

    for i in range(3):

        @pl.loop(0, n_z)
        def _(b):
            twin_copy(i, b).wait_send()

        for s in range(half):
            for way in range(2):
                ring_copy(i, way, s).wait_send()


def on_device(
    n_dp,
    n_ex,
    gen_rows,
    gen_lengths,
    gen_adv,
    destination,
    expert_ids,
    gate_values,
    cotangent,
    w_gate,
    w_up,
    w_down,
):
    rows, width = gen_rows.shape
    seqs = destination.shape[2]
    slot = rows // seqs
    ff = w_gate.shape[2]
    cap = 2 * rows * expert_ids.shape[1] // n_ex
    slots = n_ex * cap
    n_z = n_dp // 2
    per_seq = jnp.stack(
        [destination[0, 0].astype(F32), gen_lengths[0, 0].astype(F32), gen_adv[0, 0].astype(F32)]
    )
    small = jnp.concatenate(
        [
            jnp.repeat(per_seq, slot, axis=1),
            expert_ids.astype(F32).T,
            gate_values.T,
            jnp.zeros((1, rows), F32),
        ]
    )
    vmem = pl.BlockSpec(memory_space=pltpu.VMEM)
    hbm = pl.BlockSpec(memory_space=pl.ANY)
    dma = pltpu.SemaphoreType.DMA
    part, part_d = width // n_dp, ff // n_dp
    buffers = [pltpu.VMEM((n_ex, cap, width), BF)] * 8
    ring = [
        pltpu.VMEM((2, n_z // 2, p, c), BF) for p, c in ((part, ff), (part, ff), (part_d, width))
    ]
    twin = [pltpu.VMEM((n_z, p, c), BF) for p, c in ((part, ff), (part, ff), (part_d, width))]
    outs = pl.pallas_call(
        functools.partial(step_kernel, n_dp, n_ex, slot, cap),
        out_shape=(
            jax.ShapeDtypeStruct((rows, width), BF),
            jax.ShapeDtypeStruct((rows, width), BF),
            jax.ShapeDtypeStruct((part, ff), BF),
            jax.ShapeDtypeStruct((part, ff), BF),
            jax.ShapeDtypeStruct((part_d, width), BF),
        ),
        in_specs=[vmem, vmem, vmem, hbm, hbm, hbm],
        out_specs=[vmem] * 5,
        scratch_shapes=[
            pltpu.VMEM((width, ff), BF),
            pltpu.VMEM((width, ff), BF),
            pltpu.VMEM((ff, width), BF),
            pltpu.VMEM((n_dp, 8, 128), F32),
            pltpu.VMEM((n_dp, 8, 128), F32),
            pltpu.VMEM((n_dp, slot, width), BF),
            pltpu.VMEM((n_dp, slot, width), BF),
            *buffers,
            pltpu.VMEM((slots, rows), BF),
            pltpu.VMEM((slots, rows), BF),
            pltpu.VMEM((slots, rows), BF),
            pltpu.VMEM((slots, ff), F32),
            pltpu.VMEM((slots, ff), F32),
            pltpu.VMEM((slots, ff), BF),
            pltpu.VMEM((slots, ff), BF),
            pltpu.VMEM((slots, ff), BF),
            pltpu.VMEM((width, ff), BF),
            pltpu.VMEM((width, ff), BF),
            pltpu.VMEM((ff, width), BF),
            *twin,
            *ring,
            dma((3,)),
            dma((n_dp,)),
            dma((n_dp,)),
            dma((n_dp,)),
            dma((n_dp,)),
            *([dma((n_ex,))] * 8),
            dma((3, n_z)),
            dma((3, n_z)),
            dma((3, 2, n_z // 2)),
            dma((3, 2, n_z // 2)),
        ],
        compiler_params=pltpu.CompilerParams(
            collective_id=0, has_side_effects=True, vmem_limit_bytes=67043328
        ),
    )(small, gen_rows, cotangent, w_gate[0], w_up[0], w_down[0])
    return outs[0], outs[1], outs[2][None], outs[3][None], outs[4][None]


def solution(mesh):
    n_dp, n_ex = mesh.shape["dp"], mesh.shape["expert"]
    in_specs = (
        P(("dp", "expert"), None),
        P("dp", "expert", None),
        P("dp", "expert", None),
        P("dp", "expert", None),
        P(("dp", "expert"), None),
        P(("dp", "expert"), None),
        P(("dp", "expert"), None),
        P("expert", None, None),
        P("expert", None, None),
        P("expert", None, None),
    )
    out_specs = (
        P(("dp", "expert"), None),
        P(("dp", "expert"), None),
        P("expert", "dp", None),
        P("expert", "dp", None),
        P("expert", "dp", None),
    )
    return jax.shard_map(
        functools.partial(on_device, n_dp, n_ex),
        mesh=mesh,
        in_specs=in_specs,
        out_specs=out_specs,
        check_vma=False,
    )
```

```python
import functools

import jax
import jax.numpy as jnp
from jax import lax
from jax.experimental import pallas as pl
from jax.experimental.pallas import tpu as pltpu
from jax.sharding import PartitionSpec as P

MESH = pl.DeviceIdType.MESH
BF = jnp.bfloat16
F32 = jnp.float32


def contract(left, right, left_dim, right_dim):
    return lax.dot_general(
        left, right, (((left_dim,), (right_dim,)), ((), ())), preferred_element_type=F32
    )


def iota(shape, dim):
    return lax.broadcasted_iota(jnp.int32, shape, dim)


def step_kernel(
    n_dp,
    n_ex,
    slot,
    cap,
    dest_ref,
    len_ref,
    adv_ref,
    ids_ref,
    gate_ref,
    gen_hbm,
    cot_hbm,
    wg_hbm,
    wu_hbm,
    wd_hbm,
    out_ref,
    dx_ref,
    gg_out,
    gu_out,
    gd_out,
    gen_ref,
    cot_ref,
    wg,
    wu,
    wd,
    meta_send,
    meta_recv,
    scale_send,
    scale_recv,
    seq_send,
    seq_recv,
    x_send,
    x_recv,
    y_send,
    y_recv,
    o_send,
    o_recv,
    b_send,
    b_recv,
    pick,
    hi,
    low,
    fac_a,
    fac_b,
    hid,
    gg,
    ug,
    grad_g,
    grad_u,
    grad_d,
    twin_g,
    twin_u,
    twin_d,
    ring_g,
    ring_u,
    ring_d,
    w_sem,
    meta_ss,
    meta_rs,
    scale_ss,
    scale_rs,
    seq_ss,
    seq_rs,
    x_ss,
    x_rs,
    y_ss,
    y_rs,
    o_ss,
    o_rs,
    b_ss,
    b_rs,
    twin_ss,
    twin_rs,
    ring_ss,
    ring_rs,
):
    g = lax.axis_index("dp")
    e = lax.axis_index("expert")
    core = lax.rem(g, 2)
    z = lax.div(g, 2)
    n_z = n_dp // 2
    half = n_z // 2
    rows = gen_ref.shape[0]
    width = gen_ref.shape[1]
    ff = wg.shape[1]
    slots = n_ex * cap
    lanes = max(cap, 128)
    dtile = min(256, width)
    ftile = min(256, ff)
    nd, nf = width // dtile, ff // ftile

    nx = 1
    while (nx * 2) * (nx * 2) <= n_ex:
        nx *= 2
    ny = n_ex // nx
    ex, ey = lax.rem(e, nx), lax.div(e, nx)

    def far(d, n):
        return min(d, n - d)

    tokens = sorted(
        ((dy, dx) for dy in range(ny) for dx in range(nx)),
        key=lambda d: -(far(d[0], ny) + far(d[1], nx)),
    )
    trainers = sorted(
        ((dz, dc) for dz in range(n_z) for dc in range(2)), key=lambda d: -(far(d[0], n_z) + d[1])
    )

    def expert_to(i, sign=1):
        dy, dx = tokens[i]
        return lax.rem(ey + sign * dy + ny, ny) * nx + lax.rem(ex + sign * dx + nx, nx)

    def trainer_to(i):
        dz, dc = trainers[i]
        return lax.rem(z + dz, n_z) * 2 + lax.rem(core + dc, 2)

    barrier = pltpu.get_barrier_semaphore()

    @pl.loop(1, n_dp)
    def _(o):
        pl.semaphore_signal(barrier, 1, device_id={"dp": lax.rem(g + o, n_dp)}, device_id_type=MESH)

    @pl.loop(1, n_ex)
    def _(o):
        pl.semaphore_signal(
            barrier, 1, device_id={"expert": lax.rem(e + o, n_ex)}, device_id_type=MESH
        )

    loads = [
        pltpu.make_async_copy(src, dst, w_sem.at[i])
        for i, (src, dst) in enumerate(
            ((gen_hbm, gen_ref), (cot_hbm, cot_ref), (wg_hbm, wg), (wu_hbm, wu), (wd_hbm, wd))
        )
    ]
    for copy in loads:
        copy.start()

    shift = slot.bit_length() - 1
    seqs = dest_ref.shape[1]
    srow, scol = iota((n_dp * slot, rows), 0), iota((n_dp * slot, rows), 1)
    same_place = (srow & (slot - 1)) == (scol & (slot - 1))
    mine = dest_ref[...] == iota((n_dp, seqs), 0)
    len_to = jnp.sum(jnp.where(mine, len_ref[...].astype(F32), 0.0), axis=1, keepdims=True)
    adv_to = jnp.sum(jnp.where(mine, adv_ref[...].astype(F32), 0.0), axis=1, keepdims=True)
    line = iota((n_dp, 8, 128), 1)
    meta_send[...] = jnp.where(line == 0, len_to[:, :, None], adv_to[:, :, None])
    seq_lanes = ((iota((seqs, rows), 1) >> shift) == iota((seqs, rows), 0)).astype(F32)
    mine_lanes = jnp.dot(mine.astype(F32), seq_lanes, preferred_element_type=F32)
    spread = jnp.broadcast_to(mine_lanes[:, None, :], (n_dp, slot, rows)).reshape(n_dp * slot, rows)
    spread = jnp.where(same_place, spread, 0.0).astype(BF)
    loads[0].wait()

    @pl.loop(0, nd)
    def _(j):
        cols = pl.ds(pl.multiple_of(j * dtile, dtile), dtile)
        seq_send[:, :, cols] = (
            jnp.dot(spread, gen_ref[:, cols], preferred_element_type=F32)
            .astype(BF)
            .reshape(n_dp, slot, dtile)
        )

    names = jnp.zeros((n_ex, rows), jnp.int32)
    for i in range(n_ex):
        names = jnp.where(iota((n_ex, rows), 0) == i, expert_to(i), names)
    hit0, hit1 = ids_ref[0:1, :] == names, ids_ref[1:2, :] == names
    routed = hit0 | hit1
    gate_of = jnp.where(hit0, gate_ref[0:1, :], 0.0) + jnp.where(hit1, gate_ref[1:2, :], 0.0)
    before = (iota((rows, rows), 0) < iota((rows, rows), 1)).astype(BF)
    pos = jnp.dot(routed.astype(BF), before, preferred_element_type=F32)
    code = jnp.where(routed, pos, -1.0)
    hit = code[:, None, :] == iota((n_ex, cap, rows), 1).astype(F32)
    picked = hit.astype(BF).reshape(slots, rows)
    pick[...] = picked
    weighted = jnp.where(hit, gate_of[:, None, :], 0.0).reshape(slots, rows)
    whole = weighted.astype(BF)
    hi[...] = whole
    low[...] = (weighted - whole.astype(F32)).astype(BF)

    loads[1].wait()

    @pl.loop(0, nd)
    def _(j):
        cols = pl.ds(pl.multiple_of(j * dtile, dtile), dtile)
        y_send[:, :, cols] = (
            jnp.dot(pick[...], cot_ref[:, cols], preferred_element_type=F32)
            .astype(BF)
            .reshape(n_ex, cap, dtile)
        )

    pl.semaphore_wait(barrier, n_dp + n_ex - 2)

    def dp_exchange(send, recv, ss, rs):
        def copy(i):
            peer = trainer_to(i)
            return pltpu.make_async_remote_copy(
                src_ref=send.at[peer],
                dst_ref=recv.at[g],
                send_sem=ss.at[i],
                recv_sem=rs.at[i],
                device_id={"dp": peer},
                device_id_type=MESH,
            )

        own = pltpu.make_async_copy(send.at[g], recv.at[g], ss.at[n_dp - 1])

        def start():
            for i in range(n_dp - 1):
                copy(i).start()
            own.start()

        def wait_recv():
            own.wait()
            for i in range(n_dp - 1):
                copy(i).wait_recv()

        def wait_send():
            for i in range(n_dp - 1):
                copy(i).wait_send()

        return start, wait_recv, wait_send

    def token_exchange(sign, send, recv, ss, rs):
        def copy(i):
            return pltpu.make_async_remote_copy(
                src_ref=send.at[i],
                dst_ref=recv.at[i],
                send_sem=ss.at[i],
                recv_sem=rs.at[i],
                device_id={"expert": expert_to(i, sign)},
                device_id_type=MESH,
            )

        own = pltpu.make_async_copy(send.at[n_ex - 1], recv.at[n_ex - 1], ss.at[n_ex - 1])

        def start(lo=0, hi=n_ex):
            for i in range(lo, min(hi, n_ex - 1)):
                copy(i).start()
            if hi == n_ex:
                own.start()

        def wait_recv(lo=0, hi=n_ex):
            if hi == n_ex:
                own.wait()
            for i in range(lo, min(hi, n_ex - 1)):
                copy(i).wait_recv()

        def wait_send():
            for i in range(n_ex - 1):
                copy(i).wait_send()

        return start, wait_recv, wait_send

    meta_start, meta_wait, meta_done = dp_exchange(meta_send, meta_recv, meta_ss, meta_rs)
    seq_start, seq_wait, seq_done = dp_exchange(seq_send, seq_recv, seq_ss, seq_rs)
    x_start, x_wait, x_done = token_exchange(1, x_send, x_recv, x_ss, x_rs)
    y_start, y_wait, y_done = token_exchange(1, y_send, y_recv, y_ss, y_rs)
    v_start, v_wait, v_done = token_exchange(1, scale_send, scale_recv, scale_ss, scale_rs)
    o_start, o_wait, o_done = token_exchange(-1, o_send, o_recv, o_ss, o_rs)
    b_start, b_wait, b_done = token_exchange(-1, b_send, b_recv, b_ss, b_rs)

    meta_start()
    seq_start()
    y_start()
    meta_wait()

    got_len = meta_recv[:, 0, :]
    got_adv = meta_recv[:, 1, :]
    alive = (got_len > 0.0).astype(BF)
    lower = (iota((n_dp, n_dp), 1) < iota((n_dp, n_dp), 0)).astype(BF)
    arrival = jnp.dot(lower, alive, preferred_element_type=F32)
    arrival = jnp.where(got_len > 0.0, arrival, -1.0)
    per_len = got_adv / jnp.maximum(got_len, 1.0)

    def widen(v):
        return jnp.broadcast_to(v[:, None, :rows], (n_dp, slot, rows)).reshape(n_dp * slot, rows)

    placed = (widen(arrival) == (scol >> shift).astype(F32)) & same_place
    within = (srow & (slot - 1)).astype(F32) < widen(got_len)
    tok_scale = jnp.sum(
        jnp.where(placed & within, widen(per_len), 0.0), axis=0, keepdims=True
    )
    row_scale = jnp.sum(
        jnp.where(hit, (gate_of * tok_scale)[:, None, :], 0.0), axis=2, keepdims=True
    )
    on_lane = iota((n_ex, cap, lanes), 1) == iota((n_ex, cap, lanes), 2)
    scale_send[...] = jnp.broadcast_to(
        jnp.sum(jnp.where(on_lane, row_scale, 0.0), axis=1, keepdims=True), (n_ex, 8, lanes)
    )
    v_start()
    fetch = contract(picked, placed.astype(BF), 1, 1).astype(BF)
    seq_wait()

    @pl.loop(0, nd)
    def _(j):
        cols = pl.ds(pl.multiple_of(j * dtile, dtile), dtile)
        source = seq_recv[:, :, cols].reshape(n_dp * slot, dtile)
        x_send[:, :, cols] = (
            jnp.dot(fetch, source, preferred_element_type=F32).astype(BF).reshape(n_ex, cap, dtile)
        )

    x_start()
    y_wait()
    v_wait()
    scale = jnp.sum(
        jnp.where(on_lane, scale_recv[:, 0:1, :], 0.0), axis=2, keepdims=True
    ).reshape(slots, 1)

    @pl.loop(0, nd)
    def _(j):
        cols = pl.ds(pl.multiple_of(j * dtile, dtile), dtile)
        y_recv[:, :, cols] = (
            (y_recv[:, :, cols].reshape(slots, dtile).astype(F32) * scale)
            .astype(BF)
            .reshape(n_ex, cap, dtile)
        )

    for copy in loads[2:]:
        copy.wait()

    group = n_ex // 2
    for part in range(2):
        lo, n_rows = part * group, group * cap
        here = pl.ds(lo * cap, n_rows)
        x_wait(lo, lo + group)

        @pl.loop(0, nf)
        def _(j):
            cols = pl.ds(pl.multiple_of(j * ftile, ftile), ftile)
            x_some = x_recv[lo : lo + group].reshape(n_rows, width)
            gate_pre = jnp.dot(x_some, wg[:, cols], preferred_element_type=F32)
            up_pre = jnp.dot(x_some, wu[:, cols], preferred_element_type=F32)
            sig = jax.nn.sigmoid(gate_pre)
            act = gate_pre * sig
            hid[here, cols] = (act * up_pre).astype(BF)
            fac_a[here, cols] = up_pre * sig * (1.0 + gate_pre * (1.0 - sig))
            fac_b[here, cols] = act

        @pl.loop(0, nd)
        def _(j):
            cols = pl.ds(pl.multiple_of(j * dtile, dtile), dtile)
            o_send[lo : lo + group, :, cols] = (
                jnp.dot(hid[here, :], wd[:, cols], preferred_element_type=F32)
                .astype(BF)
                .reshape(group, cap, dtile)
            )

        o_start(lo, lo + group)

    @pl.loop(0, nf)
    def _(j):
        cols = pl.ds(pl.multiple_of(j * ftile, ftile), ftile)
        y_all = y_recv[...].reshape(slots, width)
        hidden_grad = contract(y_all, wd[cols, :], 1, 1)
        gg[:, cols] = (hidden_grad * fac_a[:, cols]).astype(BF)
        ug[:, cols] = (hidden_grad * fac_b[:, cols]).astype(BF)

    grads = ((grad_d, twin_d, ring_d, gd_out), (grad_g, twin_g, ring_g, gg_out), (grad_u, twin_u, ring_u, gu_out))

    def block(i, b, c):
        part = grads[i][1].shape[1]
        return pl.ds(pl.multiple_of((b * 2 + c) * part, part), part)

    def twin_copy(i, b):
        return pltpu.make_async_remote_copy(
            src_ref=grads[i][0].at[block(i, b, 1 - core)],
            dst_ref=grads[i][1].at[b],
            send_sem=twin_ss.at[i, b],
            recv_sem=twin_rs.at[i, b],
            device_id={"dp": g + 1 - 2 * core},
            device_id_type=MESH,
        )

    def ring_copy(i, way, s):
        grad, _, ring, _ = grads[i]
        mid = grad.shape[1] // 2
        if s == 0:
            b = lax.rem(z + half, n_z)
            cols = pl.ds(way * mid, mid)
        else:
            b = lax.rem(z + (half - s) * (1 - 2 * way) + n_z, n_z)
            cols = pl.ds(0, 2 * mid)
        return pltpu.make_async_remote_copy(
            src_ref=grad.at[block(i, b, core), cols],
            dst_ref=ring.at[way, s, :, cols],
            send_sem=ring_ss.at[i, way, s],
            recv_sem=ring_rs.at[i, way, s],
            device_id={"dp": lax.rem(g + 2 * (1 - 2 * way) + n_dp, n_dp)},
            device_id_type=MESH,
        )

    def ring_step(i, s):
        grad, twin, ring, _ = grads[i]
        mid = grad.shape[1] // 2
        if s == 0:
            b = lax.rem(z + half, n_z)
            here = block(i, b, core)
            twin_copy(i, b).wait_recv()
            grad[here, :] = (grad[here, :].astype(F32) + twin[b].astype(F32)).astype(BF)
            ring_copy(i, 0, 0).start()
            ring_copy(i, 1, 0).start()
            return
        for way in range(2):
            b = lax.rem(z + (half - s) * (1 - 2 * way) + n_z, n_z)
            here = block(i, b, core)
            twin_copy(i, b).wait_recv()
            ring_copy(i, way, s - 1).wait_recv()
            if s == 1:
                near, far = pl.ds(way * mid, mid), pl.ds((1 - way) * mid, mid)
                grad[here, near] = (
                    grad[here, near].astype(F32)
                    + twin[b, :, near].astype(F32)
                    + ring[way, 0, :, near].astype(F32)
                ).astype(BF)
                grad[here, far] = (
                    grad[here, far].astype(F32) + twin[b, :, far].astype(F32)
                ).astype(BF)
            else:
                grad[here, :] = (
                    grad[here, :].astype(F32)
                    + twin[b].astype(F32)
                    + ring[way, s - 1].astype(F32)
                ).astype(BF)
            ring_copy(i, way, s).start()

    def ring_last(i):
        grad, twin, ring, out = grads[i]
        twin_copy(i, z).wait_recv()
        ring_copy(i, 0, half - 1).wait_recv()
        ring_copy(i, 1, half - 1).wait_recv()
        here = block(i, z, core)
        out[...] = (
            grad[here, :].astype(F32)
            + twin[z].astype(F32)
            + ring[0, half - 1].astype(F32)
            + ring[1, half - 1].astype(F32)
        ).astype(BF)

    pair = width // n_z

    def ring_order(k):
        d = half - lax.div(k + 1, 2)
        way = 2 * lax.rem(k, 2) - 1
        return lax.rem(z + way * d + n_z, n_z)

    def gate_up(lo, hi):
        @pl.loop(lo, hi)
        def _(k):
            b = ring_order(k)
            cols = pl.ds(pl.multiple_of(b * pair, pair), pair)
            x_part = x_recv[:, :, cols].reshape(slots, pair)
            grad_g[cols, :] = contract(x_part, gg[...], 0, 0).astype(BF)
            twin_copy(1, b).start()
            grad_u[cols, :] = contract(x_part, ug[...], 0, 0).astype(BF)
            twin_copy(2, b).start()

    def input_rows(lo, hi):
        @pl.loop(lo, hi)
        def _(j):
            cols = pl.ds(pl.multiple_of(j * dtile, dtile), dtile)
            b_send[:, :, cols] = (
                (contract(gg[...], wg[cols, :], 1, 1) + contract(ug[...], wu[cols, :], 1, 1))
                .astype(BF)
                .reshape(n_ex, cap, dtile)
            )

    gate_up(0, 1)

    @pl.loop(0, nf * nd)
    def _(j):
        units = pl.ds(pl.multiple_of(lax.div(j, nd) * ftile, ftile), ftile)
        cols = pl.ds(pl.multiple_of(lax.rem(j, nd) * dtile, dtile), dtile)
        grad_d[units, cols] = contract(
            hid[:, units], y_recv[:, :, cols].reshape(slots, dtile), 0, 0
        ).astype(BF)

    @pl.loop(0, n_z)
    def _(k):
        twin_copy(0, ring_order(k)).start()

    ring_step(1, 0)
    ring_step(2, 0)
    gate_up(1, 3)
    ring_step(0, 0)
    gate_up(3, n_z)
    ring_step(1, 1)
    ring_step(2, 1)
    first = nd * 3 // 8
    input_rows(0, first)
    ring_step(0, 1)
    input_rows(first, nd)
    b_start()

    def tokens_out():
        o_wait()

        @pl.loop(0, nd)
        def _(j):
            cols = pl.ds(pl.multiple_of(j * dtile, dtile), dtile)
            back = o_recv[:, :, cols].reshape(slots, dtile)
            out_ref[:, cols] = (
                contract(hi[...], back, 0, 0) + contract(low[...], back, 0, 0)
            ).astype(BF)

    for s in range(2, half):
        ring_step(1, s)
        ring_step(2, s)
        if s == 2:
            tokens_out()
        ring_step(0, s)
    if half < 3:
        tokens_out()

    b_wait()

    @pl.loop(0, nd)
    def _(j):
        cols = pl.ds(pl.multiple_of(j * dtile, dtile), dtile)
        back = b_recv[:, :, cols].reshape(slots, dtile)
        dx_ref[:, cols] = contract(pick[...], back, 0, 0).astype(BF)

    for i in (1, 2, 0):
        ring_last(i)

    for done in (meta_done, v_done, seq_done, x_done, y_done, o_done, b_done):
        done()

    for i in range(3):

        @pl.loop(0, n_z)
        def _(b):
            twin_copy(i, b).wait_send()

        for s in range(half):
            for way in range(2):
                ring_copy(i, way, s).wait_send()


def settle_kernel(*refs):
    n = (len(refs) - 2) // 3
    src, dst, held, sems = refs[:n], refs[n : 2 * n], refs[2 * n : 3 * n], refs[3 * n :]
    ins = [pltpu.make_async_copy(src[i], held[i], sems[0].at[i]) for i in range(n)]
    outs = [pltpu.make_async_copy(held[i], dst[i], sems[1].at[i]) for i in range(n)]
    for copy in ins:
        copy.start()
    for i in range(n):
        ins[i].wait()
        outs[i].start()
    for copy in outs:
        copy.wait()


def settle(arrays):
    n = len(arrays)
    hbm = pl.BlockSpec(memory_space=pl.ANY)
    return pl.pallas_call(
        settle_kernel,
        out_shape=[jax.ShapeDtypeStruct(a.shape, a.dtype) for a in arrays],
        in_specs=[hbm] * n,
        out_specs=[hbm] * n,
        scratch_shapes=[pltpu.VMEM(a.shape, a.dtype) for a in arrays]
        + [pltpu.SemaphoreType.DMA((n,)), pltpu.SemaphoreType.DMA((n,))],
    )(*arrays)


def on_device(
    n_dp,
    n_ex,
    gen_rows,
    gen_lengths,
    gen_adv,
    destination,
    expert_ids,
    gate_values,
    cotangent,
    w_gate,
    w_up,
    w_down,
):
    rows, width = gen_rows.shape
    seqs = destination.shape[2]
    slot = rows // seqs
    ff = w_gate.shape[2]
    cap = 2 * rows * expert_ids.shape[1] // n_ex
    slots = n_ex * cap
    n_z = n_dp // 2
    lanes = max(cap, 128)
    vmem = pl.BlockSpec(memory_space=pltpu.VMEM)
    hbm = pl.BlockSpec(memory_space=pl.ANY)
    dma = pltpu.SemaphoreType.DMA
    part, part_d = width // n_dp, ff // n_dp
    buffers = [pltpu.VMEM((n_ex, cap, width), BF)] * 8
    ring = [
        pltpu.VMEM((2, n_z // 2, p, c), BF) for p, c in ((part, ff), (part, ff), (part_d, width))
    ]
    twin = [pltpu.VMEM((n_z, p, c), BF) for p, c in ((part, ff), (part, ff), (part_d, width))]
    outs = pl.pallas_call(
        functools.partial(step_kernel, n_dp, n_ex, slot, cap),
        out_shape=(
            jax.ShapeDtypeStruct((rows, width), BF),
            jax.ShapeDtypeStruct((rows, width), BF),
            jax.ShapeDtypeStruct((part, ff), BF),
            jax.ShapeDtypeStruct((part, ff), BF),
            jax.ShapeDtypeStruct((part_d, width), BF),
        ),
        in_specs=[vmem] * 5 + [hbm] * 5,
        out_specs=[vmem] * 5,
        scratch_shapes=[
            pltpu.VMEM((rows, width), BF),
            pltpu.VMEM((rows, width), BF),
            pltpu.VMEM((width, ff), BF),
            pltpu.VMEM((width, ff), BF),
            pltpu.VMEM((ff, width), BF),
            pltpu.VMEM((n_dp, 8, 128), F32),
            pltpu.VMEM((n_dp, 8, 128), F32),
            pltpu.VMEM((n_ex, 8, lanes), F32),
            pltpu.VMEM((n_ex, 8, lanes), F32),
            pltpu.VMEM((n_dp, slot, width), BF),
            pltpu.VMEM((n_dp, slot, width), BF),
            *buffers,
            pltpu.VMEM((slots, rows), BF),
            pltpu.VMEM((slots, rows), BF),
            pltpu.VMEM((slots, rows), BF),
            pltpu.VMEM((slots, ff), F32),
            pltpu.VMEM((slots, ff), F32),
            pltpu.VMEM((slots, ff), BF),
            pltpu.VMEM((slots, ff), BF),
            pltpu.VMEM((slots, ff), BF),
            pltpu.VMEM((width, ff), BF),
            pltpu.VMEM((width, ff), BF),
            pltpu.VMEM((ff, width), BF),
            *twin,
            *ring,
            dma((5,)),
            dma((n_dp,)),
            dma((n_dp,)),
            dma((n_ex,)),
            dma((n_ex,)),
            dma((n_dp,)),
            dma((n_dp,)),
            *([dma((n_ex,))] * 8),
            dma((3, n_z)),
            dma((3, n_z)),
            dma((3, 2, n_z // 2)),
            dma((3, 2, n_z // 2)),
        ],
        compiler_params=pltpu.CompilerParams(
            collective_id=0, has_side_effects=True, vmem_limit_bytes=67043328
        ),
    )(
        destination[0],
        gen_lengths[0],
        gen_adv[0],
        expert_ids.T,
        gate_values.T,
        gen_rows,
        cotangent,
        w_gate[0],
        w_up[0],
        w_down[0],
    )
    outs = settle(outs)
    return outs[0], outs[1], outs[2][None], outs[3][None], outs[4][None]


def solution(mesh):
    n_dp, n_ex = mesh.shape["dp"], mesh.shape["expert"]
    in_specs = (
        P(("dp", "expert"), None),
        P("dp", "expert", None),
        P("dp", "expert", None),
        P("dp", "expert", None),
        P(("dp", "expert"), None),
        P(("dp", "expert"), None),
        P(("dp", "expert"), None),
        P("expert", None, None),
        P("expert", None, None),
        P("expert", None, None),
    )
    out_specs = (
        P(("dp", "expert"), None),
        P(("dp", "expert"), None),
        P("expert", "dp", None),
        P("expert", "dp", None),
        P("expert", "dp", None),
    )
    return jax.shard_map(
        functools.partial(on_device, n_dp, n_ex),
        mesh=mesh,
        in_specs=in_specs,
        out_specs=out_specs,
        check_vma=False,
    )
```

```python
import functools

import jax
import jax.numpy as jnp
from jax import lax
from jax.experimental import pallas as pl
from jax.experimental.pallas import tpu as pltpu
from jax.sharding import PartitionSpec as P

MESH = pl.DeviceIdType.MESH
BF = jnp.bfloat16
F32 = jnp.float32


def contract(left, right, left_dim, right_dim):
    return lax.dot_general(
        left, right, (((left_dim,), (right_dim,)), ((), ())), preferred_element_type=F32
    )


def iota(shape, dim):
    return lax.broadcasted_iota(jnp.int32, shape, dim)


def step_kernel(
    n_dp,
    n_ex,
    slot,
    cap,
    dest_ref,
    len_ref,
    adv_ref,
    ids_ref,
    gate_ref,
    gen_hbm,
    cot_hbm,
    wg_hbm,
    wu_hbm,
    wd_hbm,
    out_hbm,
    dx_hbm,
    gg_hbm,
    gu_hbm,
    gd_hbm,
    out_ref,
    dx_ref,
    gg_out,
    gu_out,
    gd_out,
    gen_ref,
    cot_ref,
    wg,
    wu,
    wd,
    meta_send,
    meta_recv,
    scale_send,
    scale_recv,
    seq_send,
    seq_recv,
    x_send,
    x_recv,
    y_send,
    y_recv,
    o_send,
    o_recv,
    b_send,
    b_recv,
    pick,
    hi,
    low,
    hidden_grad,
    hid,
    gg,
    ug,
    grad_g,
    grad_u,
    grad_d,
    twin_g,
    twin_u,
    twin_d,
    ring_g,
    ring_u,
    ring_d,
    w_sem,
    store_sem,
    meta_sem,
    scale_sem,
    seq_sem,
    x_sem,
    y_sem,
    o_sem,
    b_sem,
    twin_ss,
    twin_rs,
    ring_ss,
    ring_rs,
):
    g = lax.axis_index("dp")
    e = lax.axis_index("expert")
    core = lax.rem(g, 2)
    z = lax.div(g, 2)
    n_z = n_dp // 2
    half = n_z // 2
    rows = gen_ref.shape[0]
    width = gen_ref.shape[1]
    ff = wg.shape[1]
    slots = n_ex * cap
    hc = cap // 2
    lanes = max(cap, 128)
    dtile = min(256, width)
    ftile = min(256, ff)
    nd, nf = width // dtile, ff // ftile

    nx = 1
    while (nx * 2) * (nx * 2) <= n_ex:
        nx *= 2
    ny = n_ex // nx
    ex, ey = lax.rem(e, nx), lax.div(e, nx)

    def far(d, n):
        return min(d, n - d)

    tokens = sorted(
        ((dy, dx) for dy in range(ny) for dx in range(nx)),
        key=lambda d: -(far(d[0], ny) + far(d[1], nx)),
    )
    trainers = sorted(
        ((dz, dc) for dz in range(n_z) for dc in range(2)), key=lambda d: -(far(d[0], n_z) + d[1])
    )

    def expert_to(i, sign=1):
        dy, dx = tokens[i]
        return lax.rem(ey + sign * dy + ny, ny) * nx + lax.rem(ex + sign * dx + nx, nx)

    def trainer_to(i):
        dz, dc = trainers[i]
        return lax.rem(z + dz, n_z) * 2 + lax.rem(core + dc, 2)

    barrier = pltpu.get_barrier_semaphore()

    @pl.loop(1, n_dp)
    def _(o):
        pl.semaphore_signal(barrier, 1, device_id={"dp": lax.rem(g + o, n_dp)}, device_id_type=MESH)

    @pl.loop(1, n_ex)
    def _(o):
        pl.semaphore_signal(
            barrier, 1, device_id={"expert": lax.rem(e + o, n_ex)}, device_id_type=MESH
        )

    loads = [
        pltpu.make_async_copy(src, dst, w_sem.at[i])
        for i, (src, dst) in enumerate(
            ((gen_hbm, gen_ref), (cot_hbm, cot_ref), (wg_hbm, wg), (wu_hbm, wu), (wd_hbm, wd))
        )
    ]
    for copy in loads:
        copy.start()

    shift = slot.bit_length() - 1
    seqs = dest_ref.shape[1]
    srow, scol = iota((n_dp * slot, rows), 0), iota((n_dp * slot, rows), 1)
    same_place = (srow & (slot - 1)) == (scol & (slot - 1))
    mine = dest_ref[...] == iota((n_dp, seqs), 0)
    len_to = jnp.sum(jnp.where(mine, len_ref[...].astype(F32), 0.0), axis=1, keepdims=True)
    adv_to = jnp.sum(jnp.where(mine, adv_ref[...].astype(F32), 0.0), axis=1, keepdims=True)
    line = iota((n_dp, 8, 128), 1)
    meta_send[...] = jnp.where(line == 0, len_to[:, :, None], adv_to[:, :, None])
    seq_lanes = ((iota((seqs, rows), 1) >> shift) == iota((seqs, rows), 0)).astype(F32)
    mine_lanes = jnp.dot(mine.astype(F32), seq_lanes, preferred_element_type=F32)
    spread = jnp.broadcast_to(mine_lanes[:, None, :], (n_dp, slot, rows)).reshape(n_dp * slot, rows)
    spread = jnp.where(same_place, spread, 0.0).astype(BF)
    loads[0].wait()

    @pl.loop(0, nd)
    def _(j):
        cols = pl.ds(pl.multiple_of(j * dtile, dtile), dtile)
        seq_send[:, :, cols] = (
            jnp.dot(spread, gen_ref[:, cols], preferred_element_type=F32)
            .astype(BF)
            .reshape(n_dp, slot, dtile)
        )

    def dp_exchange(send, recv, sems):
        def copy(src, dst, peer):
            return pltpu.make_async_remote_copy(
                src_ref=src,
                dst_ref=dst,
                send_sem=sems.at[0],
                recv_sem=sems.at[1],
                device_id={"dp": peer},
                device_id_type=MESH,
            )

        own = pltpu.make_async_copy(send.at[g], recv.at[g], sems.at[2])
        others = pl.ds(0, n_dp - 1)
        every = copy(send.at[others], recv.at[others], trainer_to(0))

        def start():
            for i in range(n_dp - 1):
                peer = trainer_to(i)
                copy(send.at[peer], recv.at[g], peer).start()
            own.start()

        def wait_recv():
            own.wait()
            every.wait_recv()

        return start, wait_recv, every.wait_send

    def token_exchange(sign, send, recv, sems):
        def copy(p, i):
            return pltpu.make_async_remote_copy(
                src_ref=send.at[p, i],
                dst_ref=recv.at[p, i],
                send_sem=sems.at[p, 0],
                recv_sem=sems.at[p, 1],
                device_id={"expert": expert_to(0 if isinstance(i, pl.Slice) else i, sign)},
                device_id_type=MESH,
            )

        last = n_ex - 1

        def own(p):
            return pltpu.make_async_copy(send.at[p, last], recv.at[p, last], sems.at[p, 2])

        def start(p):
            for i in range(last):
                copy(p, i).start()
            own(p).start()

        def wait_recv(p):
            own(p).wait()
            copy(p, pl.ds(0, last)).wait_recv()

        def wait_send():
            for p in range(send.shape[0]):
                copy(p, pl.ds(0, last)).wait_send()

        return start, wait_recv, wait_send

    meta_start, meta_wait, meta_done = dp_exchange(meta_send, meta_recv, meta_sem)
    seq_start, seq_wait, seq_done = dp_exchange(seq_send, seq_recv, seq_sem)
    x_start, x_wait, x_done = token_exchange(1, x_send, x_recv, x_sem)
    y_start, y_wait, y_done = token_exchange(1, y_send, y_recv, y_sem)
    v_start, v_wait, v_done = token_exchange(1, scale_send, scale_recv, scale_sem)
    o_start, o_wait, o_done = token_exchange(-1, o_send, o_recv, o_sem)
    b_start, b_wait, b_done = token_exchange(-1, b_send, b_recv, b_sem)

    pl.semaphore_wait(barrier, n_dp + n_ex - 2)
    meta_start()
    seq_start()

    names = jnp.zeros((n_ex, rows), jnp.int32)
    for i in range(n_ex):
        names = jnp.where(iota((n_ex, rows), 0) == i, expert_to(i), names)
    hit0, hit1 = ids_ref[0:1, :] == names, ids_ref[1:2, :] == names
    routed = hit0 | hit1
    gate_of = jnp.where(hit0, gate_ref[0:1, :], 0.0) + jnp.where(hit1, gate_ref[1:2, :], 0.0)
    before = (iota((rows, rows), 0) < iota((rows, rows), 1)).astype(BF)
    pos = jnp.dot(routed.astype(BF), before, preferred_element_type=F32)
    code = jnp.where(routed, pos, -1.0)
    place = iota((2, n_ex, hc, rows), 0) * hc + iota((2, n_ex, hc, rows), 2)
    hit = code[None, :, None, :] == place.astype(F32)
    picked = hit.astype(BF).reshape(slots, rows)
    pick[...] = picked
    weighted = jnp.where(hit, gate_of[None, :, None, :], 0.0).reshape(slots, rows)
    whole = weighted.astype(BF)
    hi[...] = whole
    low[...] = (weighted - whole.astype(F32)).astype(BF)

    loads[1].wait()

    @pl.loop(0, nd)
    def _(j):
        cols = pl.ds(pl.multiple_of(j * dtile, dtile), dtile)
        y_send[:, :, :, cols] = (
            jnp.dot(pick[...], cot_ref[:, cols], preferred_element_type=F32)
            .astype(BF)
            .reshape(2, n_ex, hc, dtile)
        )

    y_start(0)
    y_start(1)
    meta_wait()

    got_len = meta_recv[:, 0, :]
    got_adv = meta_recv[:, 1, :]
    alive = (got_len > 0.0).astype(BF)
    lower = (iota((n_dp, n_dp), 1) < iota((n_dp, n_dp), 0)).astype(BF)
    arrival = jnp.dot(lower, alive, preferred_element_type=F32)
    arrival = jnp.where(got_len > 0.0, arrival, -1.0)
    per_len = got_adv / jnp.maximum(got_len, 1.0)

    def widen(v):
        return jnp.broadcast_to(v[:, None, :rows], (n_dp, slot, rows)).reshape(n_dp * slot, rows)

    placed = (widen(arrival) == (scol >> shift).astype(F32)) & same_place
    within = (srow & (slot - 1)).astype(F32) < widen(got_len)
    tok_scale = jnp.sum(
        jnp.where(placed & within, widen(per_len), 0.0), axis=0, keepdims=True
    )
    row_scale = jnp.sum(
        jnp.where(hit, (gate_of * tok_scale)[None, :, None, :], 0.0), axis=3, keepdims=True
    )
    lane_of = iota((2, n_ex, hc, lanes), 0) * hc + iota((2, n_ex, hc, lanes), 2)
    on_lane = lane_of == iota((2, n_ex, hc, lanes), 3)
    spread_scale = jnp.where(on_lane, row_scale, 0.0)
    spread_scale = jnp.sum(spread_scale[0] + spread_scale[1], axis=1, keepdims=True)
    scale_send[0] = jnp.broadcast_to(spread_scale, (n_ex, 8, lanes))
    v_start(0)
    fetch = contract(picked, placed.astype(BF), 1, 1).astype(BF)
    seq_wait()

    @pl.loop(0, nd)
    def _(j):
        cols = pl.ds(pl.multiple_of(j * dtile, dtile), dtile)
        source = seq_recv[:, :, cols].reshape(n_dp * slot, dtile)
        x_send[:, :, :, cols] = (
            jnp.dot(fetch, source, preferred_element_type=F32)
            .astype(BF)
            .reshape(2, n_ex, hc, dtile)
        )

    x_start(0)
    x_start(1)
    y_wait(0)
    y_wait(1)
    v_wait(0)
    scale = jnp.sum(
        jnp.where(on_lane, scale_recv[:, :, 0:1, :], 0.0), axis=3, keepdims=True
    ).reshape(slots, 1)

    @pl.loop(0, nd)
    def _(j):
        cols = pl.ds(pl.multiple_of(j * dtile, dtile), dtile)
        y_recv[:, :, :, cols] = (
            (y_recv[:, :, :, cols].reshape(slots, dtile).astype(F32) * scale)
            .astype(BF)
            .reshape(2, n_ex, hc, dtile)
        )

    for copy in loads[2:]:
        copy.wait()

    @pl.loop(0, nf)
    def _(j):
        cols = pl.ds(pl.multiple_of(j * ftile, ftile), ftile)
        hidden_grad[:, cols] = contract(y_recv[...].reshape(slots, width), wd[cols, :], 1, 1)

    n_rows = n_ex * hc

    def hidden_units(p):
        here = pl.ds(p * n_rows, n_rows)

        @pl.loop(0, nf)
        def _(j):
            cols = pl.ds(pl.multiple_of(j * ftile, ftile), ftile)
            x_some = x_recv[p].reshape(n_rows, width)
            gate_pre = jnp.dot(x_some, wg[:, cols], preferred_element_type=F32)
            up_pre = jnp.dot(x_some, wu[:, cols], preferred_element_type=F32)
            sig = jax.nn.sigmoid(gate_pre)
            act = gate_pre * sig
            hid[here, cols] = (act * up_pre).astype(BF)
            down = hidden_grad[here, cols]
            gg[here, cols] = (down * up_pre * sig * (1.0 + gate_pre * (1.0 - sig))).astype(BF)
            ug[here, cols] = (down * act).astype(BF)

    def output_rows(p):
        here = pl.ds(p * n_rows, n_rows)

        @pl.loop(0, nd)
        def _(j):
            cols = pl.ds(pl.multiple_of(j * dtile, dtile), dtile)
            o_send[p, :, :, cols] = (
                jnp.dot(hid[here, :], wd[:, cols], preferred_element_type=F32)
                .astype(BF)
                .reshape(n_ex, hc, dtile)
            )

    def input_rows():
        @pl.loop(0, nd)
        def _(j):
            cols = pl.ds(pl.multiple_of(j * dtile, dtile), dtile)
            b_send[:, :, :, cols] = (
                (contract(gg[...], wg[cols, :], 1, 1) + contract(ug[...], wu[cols, :], 1, 1))
                .astype(BF)
                .reshape(2, n_ex, hc, dtile)
            )

    grads = ((grad_d, twin_d, ring_d, gd_out), (grad_g, twin_g, ring_g, gg_out), (grad_u, twin_u, ring_u, gu_out))

    def block(i, b, c):
        part = grads[i][1].shape[1]
        return pl.ds(pl.multiple_of((b * 2 + c) * part, part), part)

    def twin_copy(i, b):
        return pltpu.make_async_remote_copy(
            src_ref=grads[i][0].at[block(i, b, 1 - core)],
            dst_ref=grads[i][1].at[b],
            send_sem=twin_ss.at[i],
            recv_sem=twin_rs.at[i, b],
            device_id={"dp": g + 1 - 2 * core},
            device_id_type=MESH,
        )

    def ring_copy(i, way, s):
        grad, _, ring, _ = grads[i]
        mid = grad.shape[1] // 2
        if s == 0:
            b = lax.rem(z + half, n_z)
            cols = pl.ds(way * mid, mid)
        else:
            b = lax.rem(z + (half - s) * (1 - 2 * way) + n_z, n_z)
            cols = pl.ds(0, 2 * mid)
        return pltpu.make_async_remote_copy(
            src_ref=grad.at[block(i, b, core), cols],
            dst_ref=ring.at[way, s, :, cols],
            send_sem=ring_ss.at[i],
            recv_sem=ring_rs.at[i, way, s],
            device_id={"dp": lax.rem(g + 2 * (1 - 2 * way) + n_dp, n_dp)},
            device_id_type=MESH,
        )

    def ring_step(i, s):
        grad, twin, ring, _ = grads[i]
        mid = grad.shape[1] // 2
        if s == 0:
            b = lax.rem(z + half, n_z)
            here = block(i, b, core)
            twin_copy(i, b).wait_recv()
            grad[here, :] = (grad[here, :].astype(F32) + twin[b].astype(F32)).astype(BF)
            ring_copy(i, 0, 0).start()
            ring_copy(i, 1, 0).start()
            return
        for way in range(2):
            b = lax.rem(z + (half - s) * (1 - 2 * way) + n_z, n_z)
            here = block(i, b, core)
            twin_copy(i, b).wait_recv()
            ring_copy(i, way, s - 1).wait_recv()
            if s == 1:
                near, far = pl.ds(way * mid, mid), pl.ds((1 - way) * mid, mid)
                grad[here, near] = (
                    grad[here, near].astype(F32)
                    + twin[b, :, near].astype(F32)
                    + ring[way, 0, :, near].astype(F32)
                ).astype(BF)
                grad[here, far] = (
                    grad[here, far].astype(F32) + twin[b, :, far].astype(F32)
                ).astype(BF)
            else:
                grad[here, :] = (
                    grad[here, :].astype(F32)
                    + twin[b].astype(F32)
                    + ring[way, s - 1].astype(F32)
                ).astype(BF)
            ring_copy(i, way, s).start()

    def ring_last(i):
        grad, twin, ring, out = grads[i]
        twin_copy(i, z).wait_recv()
        ring_copy(i, 0, half - 1).wait_recv()
        ring_copy(i, 1, half - 1).wait_recv()
        here = block(i, z, core)
        out[...] = (
            grad[here, :].astype(F32)
            + twin[z].astype(F32)
            + ring[0, half - 1].astype(F32)
            + ring[1, half - 1].astype(F32)
        ).astype(BF)

    pair = width // n_z

    def ring_order(k):
        d = half - lax.div(k + 1, 2)
        way = 2 * lax.rem(k, 2) - 1
        return lax.rem(z + way * d + n_z, n_z)

    def gate_up(lo, hi):
        @pl.loop(lo, hi)
        def _(k):
            b = ring_order(k)
            cols = pl.ds(pl.multiple_of(b * pair, pair), pair)
            x_part = x_recv[:, :, :, cols].reshape(slots, pair)
            grad_g[cols, :] = contract(x_part, gg[...], 0, 0).astype(BF)
            twin_copy(1, b).start()
            grad_u[cols, :] = contract(x_part, ug[...], 0, 0).astype(BF)
            twin_copy(2, b).start()

    def down_units(lo, hi):
        @pl.loop(lo * nd, hi * nd)
        def _(j):
            units = pl.ds(pl.multiple_of(lax.div(j, nd) * ftile, ftile), ftile)
            cols = pl.ds(pl.multiple_of(lax.rem(j, nd) * dtile, dtile), dtile)
            grad_d[units, cols] = contract(
                hid[:, units], y_recv[:, :, :, cols].reshape(slots, dtile), 0, 0
            ).astype(BF)

    def tokens_out():
        o_wait(0)
        o_wait(1)

        @pl.loop(0, nd)
        def _(j):
            cols = pl.ds(pl.multiple_of(j * dtile, dtile), dtile)
            back = o_recv[:, :, :, cols].reshape(slots, dtile)
            out_ref[:, cols] = (
                contract(hi[...], back, 0, 0) + contract(low[...], back, 0, 0)
            ).astype(BF)

        stores[0].start()

    def tokens_dx():
        b_wait(0)
        b_wait(1)

        @pl.loop(0, nd)
        def _(j):
            cols = pl.ds(pl.multiple_of(j * dtile, dtile), dtile)
            back = b_recv[:, :, :, cols].reshape(slots, dtile)
            dx_ref[:, cols] = contract(pick[...], back, 0, 0).astype(BF)

        stores[1].start()

    stores = [
        pltpu.make_async_copy(src, dst, store_sem.at[i])
        for i, (src, dst) in enumerate(
            (
                (out_ref, out_hbm),
                (dx_ref, dx_hbm),
                (gg_out, gg_hbm),
                (gu_out, gu_hbm),
                (gd_out, gd_hbm),
            )
        )
    ]
    cut1, cut2 = nf // 3, nf * 2 // 3

    x_wait(0)
    hidden_units(0)
    output_rows(0)
    x_wait(1)
    o_start(0)
    hidden_units(1)
    gate_up(0, 1)
    gate_up(1, 3)
    ring_step(1, 0)
    ring_step(2, 0)
    output_rows(1)
    o_start(1)
    down_units(0, cut1)
    ring_step(1, 1)
    down_units(cut1, cut2)
    ring_step(2, 1)
    down_units(cut2, nf)

    @pl.loop(0, n_z)
    def _(k):
        twin_copy(0, ring_order(k)).start()

    gate_up(3, min(5, n_z))
    ring_step(0, 0)
    if half > 2:
        ring_step(1, 2)
    input_rows()
    b_start(0)
    b_start(1)
    if n_z > 5:
        gate_up(5, n_z)
    if half > 2:
        ring_step(2, 2)
    ring_step(0, 1)
    if half > 3:
        ring_step(1, 3)
    tokens_out()
    if half > 2:
        ring_step(0, 2)
    if half > 3:
        ring_step(2, 3)
        ring_step(0, 3)
    for s in range(4, half):
        for i in (1, 2, 0):
            ring_step(i, s)
    tokens_dx()
    for i in (1, 2, 0):
        ring_last(i)
        stores[(4, 2, 3)[i]].start()

    for copy in stores:
        copy.wait()

    for done in (meta_done, v_done, seq_done, x_done, y_done, o_done, b_done):
        done()

    for i in range(3):
        grad, twin, _, _ = grads[i]
        part = twin.shape[1]
        for sem, count in ((twin_ss, n_z), (ring_ss, n_z - 1)):
            rows_sent = pl.ds(0, count * part)
            pltpu.make_async_remote_copy(
                src_ref=grad.at[rows_sent],
                dst_ref=grad.at[rows_sent],
                send_sem=sem.at[i],
                recv_sem=sem.at[i],
                device_id={"dp": g + 1 - 2 * core},
                device_id_type=MESH,
            ).wait_send()


def settle_kernel(*refs):
    n = (len(refs) - 2) // 3
    src, dst, held, sems = refs[:n], refs[n : 2 * n], refs[2 * n : 3 * n], refs[3 * n :]
    ins = [pltpu.make_async_copy(src[i], held[i], sems[0].at[i]) for i in range(n)]
    outs = [pltpu.make_async_copy(held[i], dst[i], sems[1].at[i]) for i in range(n)]
    for copy in ins:
        copy.start()
    for i in range(n):
        ins[i].wait()
        outs[i].start()
    for copy in outs:
        copy.wait()


def settle(arrays):
    n = len(arrays)
    hbm = pl.BlockSpec(memory_space=pl.ANY)
    return pl.pallas_call(
        settle_kernel,
        out_shape=[jax.ShapeDtypeStruct(a.shape, a.dtype) for a in arrays],
        in_specs=[hbm] * n,
        out_specs=[hbm] * n,
        scratch_shapes=[pltpu.VMEM(a.shape, a.dtype) for a in arrays]
        + [pltpu.SemaphoreType.DMA((n,)), pltpu.SemaphoreType.DMA((n,))],
    )(*arrays)


def on_device(
    n_dp,
    n_ex,
    gen_rows,
    gen_lengths,
    gen_adv,
    destination,
    expert_ids,
    gate_values,
    cotangent,
    w_gate,
    w_up,
    w_down,
):
    rows, width = gen_rows.shape
    seqs = destination.shape[2]
    slot = rows // seqs
    ff = w_gate.shape[2]
    cap = 2 * rows * expert_ids.shape[1] // n_ex
    slots = n_ex * cap
    n_z = n_dp // 2
    lanes = max(cap, 128)
    vmem = pl.BlockSpec(memory_space=pltpu.VMEM)
    hbm = pl.BlockSpec(memory_space=pl.ANY)
    dma = pltpu.SemaphoreType.DMA
    part, part_d = width // n_dp, ff // n_dp
    buffers = [pltpu.VMEM((2, n_ex, cap // 2, width), BF)] * 8
    ring = [
        pltpu.VMEM((2, n_z // 2, p, c), BF) for p, c in ((part, ff), (part, ff), (part_d, width))
    ]
    twin = [pltpu.VMEM((n_z, p, c), BF) for p, c in ((part, ff), (part, ff), (part_d, width))]
    outs = pl.pallas_call(
        functools.partial(step_kernel, n_dp, n_ex, slot, cap),
        out_shape=(
            jax.ShapeDtypeStruct((rows, width), BF),
            jax.ShapeDtypeStruct((rows, width), BF),
            jax.ShapeDtypeStruct((part, ff), BF),
            jax.ShapeDtypeStruct((part, ff), BF),
            jax.ShapeDtypeStruct((part_d, width), BF),
        ),
        in_specs=[vmem] * 5 + [hbm] * 5,
        out_specs=[hbm] * 5,
        scratch_shapes=[
            pltpu.VMEM((rows, width), BF),
            pltpu.VMEM((rows, width), BF),
            pltpu.VMEM((part, ff), BF),
            pltpu.VMEM((part, ff), BF),
            pltpu.VMEM((part_d, width), BF),
            pltpu.VMEM((rows, width), BF),
            pltpu.VMEM((rows, width), BF),
            pltpu.VMEM((width, ff), BF),
            pltpu.VMEM((width, ff), BF),
            pltpu.VMEM((ff, width), BF),
            pltpu.VMEM((n_dp, 8, 128), F32),
            pltpu.VMEM((n_dp, 8, 128), F32),
            pltpu.VMEM((1, n_ex, 8, lanes), F32),
            pltpu.VMEM((1, n_ex, 8, lanes), F32),
            pltpu.VMEM((n_dp, slot, width), BF),
            pltpu.VMEM((n_dp, slot, width), BF),
            *buffers,
            pltpu.VMEM((slots, rows), BF),
            pltpu.VMEM((slots, rows), BF),
            pltpu.VMEM((slots, rows), BF),
            pltpu.VMEM((slots, ff), F32),
            pltpu.VMEM((slots, ff), BF),
            pltpu.VMEM((slots, ff), BF),
            pltpu.VMEM((slots, ff), BF),
            pltpu.VMEM((width, ff), BF),
            pltpu.VMEM((width, ff), BF),
            pltpu.VMEM((ff, width), BF),
            *twin,
            *ring,
            dma((5,)),
            dma((5,)),
            dma((3,)),
            dma((1, 3)),
            dma((3,)),
            *([dma((2, 3))] * 4),
            dma((3,)),
            dma((3, n_z)),
            dma((3,)),
            dma((3, 2, n_z // 2)),
        ],
        compiler_params=pltpu.CompilerParams(
            collective_id=0, has_side_effects=True, vmem_limit_bytes=67043328
        ),
    )(
        destination[0],
        gen_lengths[0],
        gen_adv[0],
        expert_ids.T,
        gate_values.T,
        gen_rows,
        cotangent,
        w_gate[0],
        w_up[0],
        w_down[0],
    )
    outs = settle(outs)
    return outs[0], outs[1], outs[2][None], outs[3][None], outs[4][None]


def solution(mesh):
    n_dp, n_ex = mesh.shape["dp"], mesh.shape["expert"]
    in_specs = (
        P(("dp", "expert"), None),
        P("dp", "expert", None),
        P("dp", "expert", None),
        P("dp", "expert", None),
        P(("dp", "expert"), None),
        P(("dp", "expert"), None),
        P(("dp", "expert"), None),
        P("expert", None, None),
        P("expert", None, None),
        P("expert", None, None),
    )
    out_specs = (
        P(("dp", "expert"), None),
        P(("dp", "expert"), None),
        P("expert", "dp", None),
        P("expert", "dp", None),
        P("expert", "dp", None),
    )
    return jax.shard_map(
        functools.partial(on_device, n_dp, n_ex),
        mesh=mesh,
        in_specs=in_specs,
        out_specs=out_specs,
        check_vma=False,
    )
```

```python
import functools

import jax
import jax.numpy as jnp
from jax import lax
from jax.experimental import pallas as pl
from jax.experimental.pallas import tpu as pltpu
from jax.sharding import PartitionSpec as P

MESH = pl.DeviceIdType.MESH
BF = jnp.bfloat16
F32 = jnp.float32
WIDE = 1024


def contract(left, right, left_dim, right_dim):
    return lax.dot_general(
        left, right, (((left_dim,), (right_dim,)), ((), ())), preferred_element_type=F32
    )


def iota(shape, dim):
    return lax.broadcasted_iota(jnp.int32, shape, dim)


def step_kernel(
    n_dp,
    n_ex,
    slot,
    cap,
    dest_ref,
    len_ref,
    adv_ref,
    ids_ref,
    gate_ref,
    gen_hbm,
    cot_hbm,
    wg_hbm,
    wu_hbm,
    wd_hbm,
    out_ref,
    dx_ref,
    gg_out,
    gu_out,
    gd_out,
    gen_ref,
    cot_ref,
    wg,
    wu,
    wd,
    meta_send,
    meta_recv,
    scale_send,
    scale_recv,
    seq_send,
    seq_recv,
    x_send,
    x_recv,
    y_send,
    y_recv,
    o_send,
    o_recv,
    b_send,
    b_recv,
    pick,
    hi,
    low,
    dx_half,
    hidden_grad,
    hid,
    both,
    grad_g,
    grad_u,
    grad_d,
    twin_g,
    twin_u,
    twin_d,
    ring_g,
    ring_u,
    ring_d,
    w_sem,
    meta_sem,
    scale_sem,
    seq_sem,
    x_sem,
    y_sem,
    o_sem,
    b_sem,
    twin_ss,
    twin_rs,
    ring_ss,
    ring_rs,
):
    g = lax.axis_index("dp")
    e = lax.axis_index("expert")
    core = lax.rem(g, 2)
    z = lax.div(g, 2)
    n_z = n_dp // 2
    half = n_z // 2
    rows = gen_ref.shape[0]
    width = gen_ref.shape[1]
    ff = wg.shape[1]
    slots = n_ex * cap
    hc = cap // 2
    lanes = max(cap, 128)
    dtile = min(256, width)
    ftile = min(256, ff)
    nd, nf = width // dtile, ff // ftile

    nx = 1
    while (nx * 2) * (nx * 2) <= n_ex:
        nx *= 2
    ny = n_ex // nx
    ex, ey = lax.rem(e, nx), lax.div(e, nx)

    def far(d, n):
        return min(d, n - d)

    tokens = sorted(
        ((dy, dx) for dy in range(ny) for dx in range(nx)),
        key=lambda d: -(far(d[0], ny) + far(d[1], nx)),
    )
    trainers = sorted(
        ((dz, dc) for dz in range(n_z) for dc in range(2)), key=lambda d: -(far(d[0], n_z) + d[1])
    )

    def expert_to(i, sign=1):
        dy, dx = tokens[i]
        return lax.rem(ey + sign * dy + ny, ny) * nx + lax.rem(ex + sign * dx + nx, nx)

    def trainer_to(i):
        dz, dc = trainers[i]
        return lax.rem(z + dz, n_z) * 2 + lax.rem(core + dc, 2)

    barrier = pltpu.get_barrier_semaphore()

    @pl.loop(1, n_dp)
    def _(o):
        pl.semaphore_signal(barrier, 1, device_id={"dp": lax.rem(g + o, n_dp)}, device_id_type=MESH)

    @pl.loop(1, n_ex)
    def _(o):
        pl.semaphore_signal(
            barrier, 1, device_id={"expert": lax.rem(e + o, n_ex)}, device_id_type=MESH
        )

    loads = [
        pltpu.make_async_copy(src, dst, w_sem.at[i])
        for i, (src, dst) in enumerate(
            ((gen_hbm, gen_ref), (cot_hbm, cot_ref), (wg_hbm, wg), (wu_hbm, wu), (wd_hbm, wd))
        )
    ]
    for copy in loads:
        copy.start()

    shift = slot.bit_length() - 1
    seqs = dest_ref.shape[1]
    srow, scol = iota((n_dp * slot, rows), 0), iota((n_dp * slot, rows), 1)
    same_place = (srow & (slot - 1)) == (scol & (slot - 1))
    mine = dest_ref[...] == iota((n_dp, seqs), 0)
    len_to = jnp.sum(jnp.where(mine, len_ref[...].astype(F32), 0.0), axis=1, keepdims=True)
    adv_to = jnp.sum(jnp.where(mine, adv_ref[...].astype(F32), 0.0), axis=1, keepdims=True)
    line = iota((n_dp, 8, 128), 1)
    meta_send[...] = jnp.where(line == 0, len_to[:, :, None], adv_to[:, :, None])
    seq_lanes = ((iota((seqs, rows), 1) >> shift) == iota((seqs, rows), 0)).astype(F32)
    mine_lanes = jnp.dot(mine.astype(F32), seq_lanes, preferred_element_type=F32)
    spread = jnp.broadcast_to(mine_lanes[:, None, :], (n_dp, slot, rows)).reshape(n_dp * slot, rows)
    spread = jnp.where(same_place, spread, 0.0).astype(BF)
    loads[0].wait()

    @pl.loop(0, nd)
    def _(j):
        cols = pl.ds(pl.multiple_of(j * dtile, dtile), dtile)
        seq_send[:, :, cols] = (
            jnp.dot(spread, gen_ref[:, cols], preferred_element_type=F32)
            .astype(BF)
            .reshape(n_dp, slot, dtile)
        )

    def dp_exchange(send, recv, sems):
        def copy(src, dst, peer):
            return pltpu.make_async_remote_copy(
                src_ref=src,
                dst_ref=dst,
                send_sem=sems.at[0],
                recv_sem=sems.at[1],
                device_id={"dp": peer},
                device_id_type=MESH,
            )

        own = pltpu.make_async_copy(send.at[g], recv.at[g], sems.at[2])
        others = pl.ds(0, n_dp - 1)
        every = copy(send.at[others], recv.at[others], trainer_to(0))

        def start():
            for i in range(n_dp - 1):
                peer = trainer_to(i)
                copy(send.at[peer], recv.at[g], peer).start()
            own.start()

        def wait_recv():
            own.wait()
            every.wait_recv()

        return start, wait_recv, every.wait_send

    def token_exchange(sign, send, recv, sems):
        def copy(p, i):
            return pltpu.make_async_remote_copy(
                src_ref=send.at[p, i],
                dst_ref=recv.at[p, i],
                send_sem=sems.at[p, 0],
                recv_sem=sems.at[p, 1],
                device_id={"expert": expert_to(0 if isinstance(i, pl.Slice) else i, sign)},
                device_id_type=MESH,
            )

        last = n_ex - 1

        def own(p):
            return pltpu.make_async_copy(send.at[p, last], recv.at[p, last], sems.at[p, 2])

        def start(p):
            for i in range(last):
                copy(p, i).start()
            own(p).start()

        def wait_recv(p):
            own(p).wait()
            copy(p, pl.ds(0, last)).wait_recv()

        def wait_send():
            for p in range(send.shape[0]):
                copy(p, pl.ds(0, last)).wait_send()

        return start, wait_recv, wait_send

    meta_start, meta_wait, meta_done = dp_exchange(meta_send, meta_recv, meta_sem)
    seq_start, seq_wait, seq_done = dp_exchange(seq_send, seq_recv, seq_sem)
    x_start, x_wait, x_done = token_exchange(1, x_send, x_recv, x_sem)
    y_start, y_wait, y_done = token_exchange(1, y_send, y_recv, y_sem)
    v_start, v_wait, v_done = token_exchange(1, scale_send, scale_recv, scale_sem)
    o_start, o_wait, o_done = token_exchange(-1, o_send, o_recv, o_sem)
    b_start, b_wait, b_done = token_exchange(-1, b_send, b_recv, b_sem)

    pl.semaphore_wait(barrier, n_dp + n_ex - 2)
    meta_start()
    seq_start()

    names = jnp.zeros((n_ex, rows), jnp.int32)
    for i in range(n_ex):
        names = jnp.where(iota((n_ex, rows), 0) == i, expert_to(i), names)
    hit0, hit1 = ids_ref[0:1, :] == names, ids_ref[1:2, :] == names
    routed = hit0 | hit1
    gate_of = jnp.where(hit0, gate_ref[0:1, :], 0.0) + jnp.where(hit1, gate_ref[1:2, :], 0.0)
    before = (iota((rows, rows), 0) < iota((rows, rows), 1)).astype(BF)
    pos = jnp.dot(routed.astype(BF), before, preferred_element_type=F32)
    code = jnp.where(routed, pos, -1.0)
    place = iota((2, n_ex, hc, rows), 0) * hc + iota((2, n_ex, hc, rows), 2)
    hit = code[None, :, None, :] == place.astype(F32)
    picked = hit.astype(BF).reshape(slots, rows)
    pick[...] = picked
    weighted = jnp.where(hit, gate_of[None, :, None, :], 0.0).reshape(slots, rows)
    whole = weighted.astype(BF)
    hi[...] = whole
    low[...] = (weighted - whole.astype(F32)).astype(BF)

    loads[1].wait()

    n_rows = n_ex * hc

    for p in range(2):

        @pl.loop(0, nd)
        def _(j):
            cols = pl.ds(pl.multiple_of(j * dtile, dtile), dtile)
            y_send[p, :, :, cols] = (
                jnp.dot(pick[p * n_rows : (p + 1) * n_rows, :], cot_ref[:, cols], preferred_element_type=F32)
                .astype(BF)
                .reshape(n_ex, hc, dtile)
            )

        y_start(p)

    meta_wait()

    got_len = meta_recv[:, 0, :]
    got_adv = meta_recv[:, 1, :]
    alive = (got_len > 0.0).astype(BF)
    lower = (iota((n_dp, n_dp), 1) < iota((n_dp, n_dp), 0)).astype(BF)
    arrival = jnp.dot(lower, alive, preferred_element_type=F32)
    arrival = jnp.where(got_len > 0.0, arrival, -1.0)
    per_len = got_adv / jnp.maximum(got_len, 1.0)

    def widen(v):
        return jnp.broadcast_to(v[:, None, :rows], (n_dp, slot, rows)).reshape(n_dp * slot, rows)

    placed = (widen(arrival) == (scol >> shift).astype(F32)) & same_place
    within = (srow & (slot - 1)).astype(F32) < widen(got_len)
    tok_scale = jnp.sum(
        jnp.where(placed & within, widen(per_len), 0.0), axis=0, keepdims=True
    )
    row_scale = jnp.sum(
        jnp.where(hit, (gate_of * tok_scale)[None, :, None, :], 0.0), axis=3, keepdims=True
    )
    lane_of = iota((2, n_ex, hc, lanes), 0) * hc + iota((2, n_ex, hc, lanes), 2)
    on_lane = lane_of == iota((2, n_ex, hc, lanes), 3)
    spread_scale = jnp.where(on_lane, row_scale, 0.0)
    spread_scale = jnp.sum(spread_scale[0] + spread_scale[1], axis=1, keepdims=True)
    scale_send[0] = jnp.broadcast_to(spread_scale, (n_ex, 8, lanes))
    v_start(0)
    fetch = contract(picked, placed.astype(BF), 1, 1).astype(BF)
    seq_wait()

    for p in range(2):

        @pl.loop(0, nd)
        def _(j):
            cols = pl.ds(pl.multiple_of(j * dtile, dtile), dtile)
            source = seq_recv[:, :, cols].reshape(n_dp * slot, dtile)
            x_send[p, :, :, cols] = (
                jnp.dot(fetch[p * n_rows : (p + 1) * n_rows, :], source, preferred_element_type=F32)
                .astype(BF)
                .reshape(n_ex, hc, dtile)
            )

        x_start(p)

    y_wait(0)
    y_wait(1)
    v_wait(0)
    scale = jnp.sum(
        jnp.where(on_lane, scale_recv[:, :, 0:1, :], 0.0), axis=3, keepdims=True
    ).reshape(slots, 1)

    @pl.loop(0, nd)
    def _(j):
        cols = pl.ds(pl.multiple_of(j * dtile, dtile), dtile)
        y_recv[:, :, :, cols] = (
            (y_recv[:, :, :, cols].reshape(slots, dtile).astype(F32) * scale)
            .astype(BF)
            .reshape(2, n_ex, hc, dtile)
        )

    for copy in loads[2:]:
        copy.wait()

    @pl.loop(0, nf)
    def _(j):
        cols = pl.ds(pl.multiple_of(j * ftile, ftile), ftile)
        hidden_grad[:, cols] = contract(y_recv[...].reshape(slots, width), wd[cols, :], 1, 1)

    def hidden_units(p):
        here = pl.ds(p * n_rows, n_rows)

        @pl.loop(0, nf)
        def _(j):
            cols = pl.ds(pl.multiple_of(j * ftile, ftile), ftile)
            x_some = x_recv[p].reshape(n_rows, width)
            gate_pre = jnp.dot(x_some, wg[:, cols], preferred_element_type=F32)
            up_pre = jnp.dot(x_some, wu[:, cols], preferred_element_type=F32)
            sig = jax.nn.sigmoid(gate_pre)
            act = gate_pre * sig
            hid[here, cols] = (act * up_pre).astype(BF)
            down = hidden_grad[here, cols]
            both[here, cols] = (
                down * up_pre * sig * (1.0 + gate_pre * (1.0 - sig))
            ).astype(BF)
            ups = pl.ds(pl.multiple_of(ff + j * ftile, ftile), ftile)
            both[here, ups] = (down * act).astype(BF)

    def output_rows(p):
        here = pl.ds(p * n_rows, n_rows)

        @pl.loop(0, nd)
        def _(j):
            cols = pl.ds(pl.multiple_of(j * dtile, dtile), dtile)
            o_send[p, :, :, cols] = (
                jnp.dot(hid[here, :], wd[:, cols], preferred_element_type=F32)
                .astype(BF)
                .reshape(n_ex, hc, dtile)
            )

    def input_rows(lo, hi):
        @pl.loop(lo, hi)
        def _(j):
            cols = pl.ds(pl.multiple_of(j * dtile, dtile), dtile)
            b_send[:, :, :, cols] = (
                (
                    contract(both[:, :ff], wg[cols, :], 1, 1)
                    + contract(both[:, ff:], wu[cols, :], 1, 1)
                )
                .astype(BF)
                .reshape(2, n_ex, hc, dtile)
            )

    grads = ((grad_d, twin_d, ring_d, gd_out), (grad_g, twin_g, ring_g, gg_out), (grad_u, twin_u, ring_u, gu_out))

    def block(i, b, c):
        part = grads[i][1].shape[1]
        return pl.ds(pl.multiple_of((b * 2 + c) * part, part), part)

    def twin_copy(i, b):
        return pltpu.make_async_remote_copy(
            src_ref=grads[i][0].at[block(i, b, 1 - core)],
            dst_ref=grads[i][1].at[b],
            send_sem=twin_ss.at[i],
            recv_sem=twin_rs.at[i, b],
            device_id={"dp": g + 1 - 2 * core},
            device_id_type=MESH,
        )

    def ring_copy(i, way, s):
        grad, _, ring, _ = grads[i]
        mid = grad.shape[1] // 2
        if s == 0:
            b = lax.rem(z + half, n_z)
            cols = pl.ds(way * mid, mid)
        else:
            b = lax.rem(z + (half - s) * (1 - 2 * way) + n_z, n_z)
            cols = pl.ds(0, 2 * mid)
        return pltpu.make_async_remote_copy(
            src_ref=grad.at[block(i, b, core), cols],
            dst_ref=ring.at[way, s, :, cols],
            send_sem=ring_ss.at[i],
            recv_sem=ring_rs.at[i, way, s],
            device_id={"dp": lax.rem(g + 2 * (1 - 2 * way) + n_dp, n_dp)},
            device_id_type=MESH,
        )

    def ring_step(i, s):
        grad, twin, ring, _ = grads[i]
        mid = grad.shape[1] // 2
        if s == 0:
            b = lax.rem(z + half, n_z)
            here = block(i, b, core)
            twin_copy(i, b).wait_recv()
            grad[here, :] = (grad[here, :].astype(F32) + twin[b].astype(F32)).astype(BF)
            ring_copy(i, 0, 0).start()
            ring_copy(i, 1, 0).start()
            return
        for way in range(2):
            b = lax.rem(z + (half - s) * (1 - 2 * way) + n_z, n_z)
            here = block(i, b, core)
            twin_copy(i, b).wait_recv()
            ring_copy(i, way, s - 1).wait_recv()
            if s == 1:
                near, far = pl.ds(way * mid, mid), pl.ds((1 - way) * mid, mid)
                grad[here, near] = (
                    grad[here, near].astype(F32)
                    + twin[b, :, near].astype(F32)
                    + ring[way, 0, :, near].astype(F32)
                ).astype(BF)
                grad[here, far] = (
                    grad[here, far].astype(F32) + twin[b, :, far].astype(F32)
                ).astype(BF)
            else:
                grad[here, :] = (
                    grad[here, :].astype(F32)
                    + twin[b].astype(F32)
                    + ring[way, s - 1].astype(F32)
                ).astype(BF)
            ring_copy(i, way, s).start()

    def ring_last(i):
        grad, twin, ring, out = grads[i]
        twin_copy(i, z).wait_recv()
        ring_copy(i, 0, half - 1).wait_recv()
        ring_copy(i, 1, half - 1).wait_recv()
        here = block(i, z, core)
        out[...] = (
            grad[here, :].astype(F32)
            + twin[z].astype(F32)
            + ring[0, half - 1].astype(F32)
            + ring[1, half - 1].astype(F32)
        ).astype(BF)

    pair = width // n_z

    def ring_order(k):
        d = half - lax.div(k + 1, 2)
        way = 2 * lax.rem(k, 2) - 1
        return lax.rem(z + way * d + n_z, n_z)

    def gate_up(lo, hi):
        @pl.loop(lo, hi)
        def _(k):
            b = ring_order(k)
            cols = pl.ds(pl.multiple_of(b * pair, pair), pair)
            x_part = x_recv[:, :, :, cols].reshape(slots, pair)
            sums = contract(x_part, both[...], 0, 0).astype(BF)
            grad_g[cols, :] = sums[:, :ff]
            grad_u[cols, :] = sums[:, ff:]
            twin_copy(1, b).start()
            twin_copy(2, b).start()

    wide = min(WIDE, width)

    def down_units(lo, hi):
        per = width // wide

        @pl.loop(lo * per, hi * per)
        def _(j):
            units = pl.ds(pl.multiple_of(lax.div(j, per) * ftile, ftile), ftile)
            cols = pl.ds(pl.multiple_of(lax.rem(j, per) * wide, wide), wide)
            grad_d[units, cols] = contract(
                hid[:, units], y_recv[:, :, :, cols].reshape(slots, wide), 0, 0
            ).astype(BF)

    def tokens_out():
        o_wait(0)
        o_wait(1)

        @pl.loop(0, nd)
        def _(j):
            cols = pl.ds(pl.multiple_of(j * dtile, dtile), dtile)
            back = o_recv[:, :, :, cols].reshape(slots, dtile)
            out_ref[:, cols] = (
                contract(hi[...], back, 0, 0) + contract(low[...], back, 0, 0)
            ).astype(BF)

    def tokens_dx(p):
        b_wait(p)

        @pl.loop(0, nd)
        def _(j):
            cols = pl.ds(pl.multiple_of(j * dtile, dtile), dtile)
            back = contract(
                pick[p * n_rows : (p + 1) * n_rows, :],
                b_recv[p, :, :, cols].reshape(n_rows, dtile),
                0,
                0,
            )
            if p == 0:
                dx_half[:, cols] = back
            else:
                dx_ref[:, cols] = (dx_half[:, cols] + back).astype(BF)

    cut1 = nf // 3

    x_wait(0)
    hidden_units(0)
    output_rows(0)
    x_wait(1)
    o_start(0)
    hidden_units(1)
    gate_up(0, 1)
    down_units(0, cut1)
    ring_step(1, 0)
    ring_step(2, 0)
    down_units(cut1, nf)

    @pl.loop(0, n_z)
    def _(k):
        twin_copy(0, ring_order(k)).start()

    gate_up(1, 3)
    ring_step(0, 0)
    output_rows(1)
    o_start(1)
    ring_step(1, 1)
    ring_step(2, 1)
    gate_up(3, min(5, n_z))
    ring_step(0, 1)
    input_rows(0, nd)
    b_start(0)
    b_start(1)
    if half > 2:
        ring_step(1, 2)
    if n_z > 5:
        gate_up(5, n_z)
    if half > 2:
        ring_step(2, 2)
        ring_step(0, 2)
    tokens_out()
    for s in range(3, half):
        for i in (1, 2, 0):
            ring_step(i, s)
    tokens_dx(0)
    tokens_dx(1)
    for i in (1, 2, 0):
        ring_last(i)

    for done in (meta_done, v_done, seq_done, x_done, y_done, o_done, b_done):
        done()

    for i in range(3):
        grad, twin, _, _ = grads[i]
        part = twin.shape[1]
        for sem, count in ((twin_ss, n_z), (ring_ss, n_z - 1)):
            rows_sent = pl.ds(0, count * part)
            pltpu.make_async_remote_copy(
                src_ref=grad.at[rows_sent],
                dst_ref=grad.at[rows_sent],
                send_sem=sem.at[i],
                recv_sem=sem.at[i],
                device_id={"dp": g + 1 - 2 * core},
                device_id_type=MESH,
            ).wait_send()


def settle_kernel(*refs):
    n = (len(refs) - 1) // 2
    copies = [pltpu.make_async_copy(refs[i], refs[n + i], refs[2 * n].at[i]) for i in range(n)]
    for copy in copies:
        copy.start()
    for copy in copies:
        copy.wait()


def settle(arrays):
    n = len(arrays)
    return pl.pallas_call(
        settle_kernel,
        out_shape=[jax.ShapeDtypeStruct(a.shape, a.dtype) for a in arrays],
        in_specs=[pl.BlockSpec(memory_space=pltpu.VMEM)] * n,
        out_specs=[pl.BlockSpec(memory_space=pl.ANY)] * n,
        scratch_shapes=[pltpu.SemaphoreType.DMA((n,))],
        compiler_params=pltpu.CompilerParams(vmem_limit_bytes=4 * 1024 * 1024),
    )(*[pltpu.with_memory_space_constraint(a, pltpu.VMEM) for a in arrays])


def on_device(
    n_dp,
    n_ex,
    gen_rows,
    gen_lengths,
    gen_adv,
    destination,
    expert_ids,
    gate_values,
    cotangent,
    w_gate,
    w_up,
    w_down,
):
    rows, width = gen_rows.shape
    seqs = destination.shape[2]
    slot = rows // seqs
    ff = w_gate.shape[2]
    cap = 2 * rows * expert_ids.shape[1] // n_ex
    slots = n_ex * cap
    n_z = n_dp // 2
    lanes = max(cap, 128)
    vmem = pl.BlockSpec(memory_space=pltpu.VMEM)
    hbm = pl.BlockSpec(memory_space=pl.ANY)
    dma = pltpu.SemaphoreType.DMA
    part, part_d = width // n_dp, ff // n_dp
    buffers = [pltpu.VMEM((2, n_ex, cap // 2, width), BF)] * 8
    ring = [
        pltpu.VMEM((2, n_z // 2, p, c), BF) for p, c in ((part, ff), (part, ff), (part_d, width))
    ]
    twin = [pltpu.VMEM((n_z, p, c), BF) for p, c in ((part, ff), (part, ff), (part_d, width))]
    outs = pl.pallas_call(
        functools.partial(step_kernel, n_dp, n_ex, slot, cap),
        out_shape=(
            pltpu.VMEM((rows, width), BF),
            pltpu.VMEM((rows, width), BF),
            pltpu.VMEM((part, ff), BF),
            pltpu.VMEM((part, ff), BF),
            pltpu.VMEM((part_d, width), BF),
        ),
        in_specs=[vmem] * 5 + [hbm] * 5,
        out_specs=[vmem] * 5,
        scratch_shapes=[
            pltpu.VMEM((rows, width), BF),
            pltpu.VMEM((rows, width), BF),
            pltpu.VMEM((width, ff), BF),
            pltpu.VMEM((width, ff), BF),
            pltpu.VMEM((ff, width), BF),
            pltpu.VMEM((n_dp, 8, 128), F32),
            pltpu.VMEM((n_dp, 8, 128), F32),
            pltpu.VMEM((1, n_ex, 8, lanes), F32),
            pltpu.VMEM((1, n_ex, 8, lanes), F32),
            pltpu.VMEM((n_dp, slot, width), BF),
            pltpu.VMEM((n_dp, slot, width), BF),
            *buffers,
            pltpu.VMEM((slots, rows), BF),
            pltpu.VMEM((slots, rows), BF),
            pltpu.VMEM((slots, rows), BF),
            pltpu.VMEM((rows, width), F32),
            pltpu.VMEM((slots, ff), F32),
            pltpu.VMEM((slots, ff), BF),
            pltpu.VMEM((slots, 2 * ff), BF),
            pltpu.VMEM((width, ff), BF),
            pltpu.VMEM((width, ff), BF),
            pltpu.VMEM((ff, width), BF),
            *twin,
            *ring,
            dma((5,)),
            dma((3,)),
            dma((1, 3)),
            dma((3,)),
            *([dma((2, 3))] * 4),
            dma((3,)),
            dma((3, n_z)),
            dma((3,)),
            dma((3, 2, n_z // 2)),
        ],
        compiler_params=pltpu.CompilerParams(
            collective_id=0, has_side_effects=True, vmem_limit_bytes=62 * 1024 * 1024
        ),
    )(
        destination[0],
        gen_lengths[0],
        gen_adv[0],
        expert_ids.T,
        gate_values.T,
        gen_rows,
        cotangent,
        w_gate[0],
        w_up[0],
        w_down[0],
    )
    outs = settle(outs)
    return outs[0], outs[1], outs[2][None], outs[3][None], outs[4][None]


def solution(mesh):
    n_dp, n_ex = mesh.shape["dp"], mesh.shape["expert"]
    in_specs = (
        P(("dp", "expert"), None),
        P("dp", "expert", None),
        P("dp", "expert", None),
        P("dp", "expert", None),
        P(("dp", "expert"), None),
        P(("dp", "expert"), None),
        P(("dp", "expert"), None),
        P("expert", None, None),
        P("expert", None, None),
        P("expert", None, None),
    )
    out_specs = (
        P(("dp", "expert"), None),
        P(("dp", "expert"), None),
        P("expert", "dp", None),
        P("expert", "dp", None),
        P("expert", "dp", None),
    )
    return jax.shard_map(
        functools.partial(on_device, n_dp, n_ex),
        mesh=mesh,
        in_specs=in_specs,
        out_specs=out_specs,
        check_vma=False,
    )
```

```python
import functools

import jax
import jax.numpy as jnp
from jax import lax
from jax.experimental import pallas as pl
from jax.experimental.pallas import tpu as pltpu
from jax.sharding import PartitionSpec as P

MESH = pl.DeviceIdType.MESH
BF = jnp.bfloat16
F32 = jnp.float32
WIDE = 1024


def contract(left, right, left_dim, right_dim):
    return lax.dot_general(
        left, right, (((left_dim,), (right_dim,)), ((), ())), preferred_element_type=F32
    )


def iota(shape, dim):
    return lax.broadcasted_iota(jnp.int32, shape, dim)


def step_kernel(
    n_dp,
    n_ex,
    slot,
    cap,
    dest_ref,
    len_ref,
    adv_ref,
    ids_ref,
    gate_ref,
    gen_hbm,
    cot_hbm,
    wg_hbm,
    wu_hbm,
    wd_hbm,
    out_ref,
    dx_ref,
    gg_out,
    gu_out,
    gd_out,
    gen_ref,
    cot_ref,
    wg,
    wu,
    wd,
    meta_send,
    meta_recv,
    scale_send,
    scale_recv,
    seq_send,
    seq_recv,
    x_send,
    x_recv,
    y_send,
    y_recv,
    o_send,
    o_recv,
    b_send,
    b_recv,
    pick,
    hi,
    low,
    dx_half,
    gate_part,
    up_part,
    hidden_grad,
    hid,
    both,
    grad_g,
    grad_u,
    grad_d,
    twin_g,
    twin_u,
    twin_d,
    ring_g,
    ring_u,
    ring_d,
    w_sem,
    meta_sem,
    scale_sem,
    seq_sem,
    x_sem,
    y_sem,
    o_sem,
    b_sem,
    twin_ss,
    twin_rs,
    ring_ss,
    ring_rs,
):
    g = lax.axis_index("dp")
    e = lax.axis_index("expert")
    core = lax.rem(g, 2)
    z = lax.div(g, 2)
    n_z = n_dp // 2
    half = n_z // 2
    rows = gen_ref.shape[0]
    width = gen_ref.shape[1]
    ff = wg.shape[1]
    slots = n_ex * cap
    hc = cap // 2
    lanes = max(cap, 128)
    dtile = min(256, width)
    ftile = min(256, ff)
    nd, nf = width // dtile, ff // ftile

    nx = 1
    while (nx * 2) * (nx * 2) <= n_ex:
        nx *= 2
    ny = n_ex // nx
    ex, ey = lax.rem(e, nx), lax.div(e, nx)

    def far(d, n):
        return min(d, n - d)

    tokens = sorted(
        ((dy, dx) for dy in range(ny) for dx in range(nx)),
        key=lambda d: -(far(d[0], ny) + far(d[1], nx)),
    )
    trainers = sorted(
        ((dz, dc) for dz in range(n_z) for dc in range(2)), key=lambda d: -(far(d[0], n_z) + d[1])
    )

    def expert_to(i, sign=1):
        dy, dx = tokens[i]
        return lax.rem(ey + sign * dy + ny, ny) * nx + lax.rem(ex + sign * dx + nx, nx)

    def trainer_to(i):
        dz, dc = trainers[i]
        return lax.rem(z + dz, n_z) * 2 + lax.rem(core + dc, 2)

    barrier = pltpu.get_barrier_semaphore()

    @pl.loop(1, n_dp)
    def _(o):
        pl.semaphore_signal(barrier, 1, device_id={"dp": lax.rem(g + o, n_dp)}, device_id_type=MESH)

    @pl.loop(1, n_ex)
    def _(o):
        pl.semaphore_signal(
            barrier, 1, device_id={"expert": lax.rem(e + o, n_ex)}, device_id_type=MESH
        )

    loads = [
        pltpu.make_async_copy(src, dst, w_sem.at[i])
        for i, (src, dst) in enumerate(
            ((gen_hbm, gen_ref), (cot_hbm, cot_ref), (wg_hbm, wg), (wu_hbm, wu), (wd_hbm, wd))
        )
    ]
    for copy in loads:
        copy.start()

    shift = slot.bit_length() - 1
    seqs = dest_ref.shape[1]
    srow, scol = iota((n_dp * slot, rows), 0), iota((n_dp * slot, rows), 1)
    same_place = (srow & (slot - 1)) == (scol & (slot - 1))
    mine = dest_ref[...] == iota((n_dp, seqs), 0)
    len_to = jnp.sum(jnp.where(mine, len_ref[...].astype(F32), 0.0), axis=1, keepdims=True)
    adv_to = jnp.sum(jnp.where(mine, adv_ref[...].astype(F32), 0.0), axis=1, keepdims=True)
    line = iota((n_dp, 8, 128), 1)
    meta_send[...] = jnp.where(line == 0, len_to[:, :, None], adv_to[:, :, None])
    seq_lanes = ((iota((seqs, rows), 1) >> shift) == iota((seqs, rows), 0)).astype(F32)
    mine_lanes = jnp.dot(mine.astype(F32), seq_lanes, preferred_element_type=F32)
    spread = jnp.broadcast_to(mine_lanes[:, None, :], (n_dp, slot, rows)).reshape(n_dp * slot, rows)
    spread = jnp.where(same_place, spread, 0.0).astype(BF)
    loads[0].wait()

    mid = width // 2
    for h in range(2):

        @pl.loop(0, nd // 2)
        def _(j):
            cols = pl.ds(pl.multiple_of(j * dtile, dtile), dtile)
            from_cols = pl.ds(pl.multiple_of(h * mid + j * dtile, dtile), dtile)
            seq_send[h, :, :, cols] = (
                jnp.dot(spread, gen_ref[:, from_cols], preferred_element_type=F32)
                .astype(BF)
                .reshape(n_dp, slot, dtile)
            )

    def dp_exchange(send, recv, sems):
        def copy(src, dst, peer):
            return pltpu.make_async_remote_copy(
                src_ref=src,
                dst_ref=dst,
                send_sem=sems.at[0],
                recv_sem=sems.at[1],
                device_id={"dp": peer},
                device_id_type=MESH,
            )

        own = pltpu.make_async_copy(send.at[g], recv.at[g], sems.at[2])
        others = pl.ds(0, n_dp - 1)
        every = copy(send.at[others], recv.at[others], trainer_to(0))

        def start():
            for i in range(n_dp - 1):
                peer = trainer_to(i)
                copy(send.at[peer], recv.at[g], peer).start()
            own.start()

        def wait_recv():
            own.wait()
            every.wait_recv()

        return start, wait_recv, every.wait_send

    def token_exchange(sign, send, recv, sems):
        def copy(p, i):
            return pltpu.make_async_remote_copy(
                src_ref=send.at[p, i],
                dst_ref=recv.at[p, i],
                send_sem=sems.at[p, 0],
                recv_sem=sems.at[p, 1],
                device_id={"expert": expert_to(0 if isinstance(i, pl.Slice) else i, sign)},
                device_id_type=MESH,
            )

        last = n_ex - 1

        def own(p):
            return pltpu.make_async_copy(send.at[p, last], recv.at[p, last], sems.at[p, 2])

        def start(p):
            for i in range(last):
                copy(p, i).start()
            own(p).start()

        def wait_recv(p):
            own(p).wait()
            copy(p, pl.ds(0, last)).wait_recv()

        def wait_send():
            for p in range(sems.shape[0]):
                copy(p, pl.ds(0, last)).wait_send()

        return start, wait_recv, wait_send

    meta_start, meta_wait, meta_done = dp_exchange(meta_send, meta_recv, meta_sem)
    seqs_of = [dp_exchange(seq_send.at[h], seq_recv.at[h], seq_sem.at[h]) for h in range(2)]
    halves = [pl.ds(h * mid, mid) for h in range(2)]
    x_of = [
        token_exchange(
            1,
            x_send.at[:, :, :, halves[h]],
            x_recv.at[:, :, :, halves[h]],
            x_sem.at[h],
        )
        for h in range(2)
    ]
    y_start, y_wait, y_done = token_exchange(1, y_send, y_recv, y_sem)
    v_start, v_wait, v_done = token_exchange(1, scale_send, scale_recv, scale_sem)
    o_start, o_wait, o_done = token_exchange(-1, o_send, o_recv, o_sem)
    b_start, b_wait, b_done = token_exchange(-1, b_send, b_recv, b_sem)

    pl.semaphore_wait(barrier, n_dp + n_ex - 2)
    meta_start()
    for seq_start, _, _ in seqs_of:
        seq_start()

    names = jnp.zeros((n_ex, rows), jnp.int32)
    for i in range(n_ex):
        names = jnp.where(iota((n_ex, rows), 0) == i, expert_to(i), names)
    hit0, hit1 = ids_ref[0:1, :] == names, ids_ref[1:2, :] == names
    routed = hit0 | hit1
    gate_of = jnp.where(hit0, gate_ref[0:1, :], 0.0) + jnp.where(hit1, gate_ref[1:2, :], 0.0)
    before = (iota((rows, rows), 0) < iota((rows, rows), 1)).astype(BF)
    pos = jnp.dot(routed.astype(BF), before, preferred_element_type=F32)
    code = jnp.where(routed, pos, -1.0)
    place = iota((2, n_ex, hc, rows), 0) * hc + iota((2, n_ex, hc, rows), 2)
    hit = code[None, :, None, :] == place.astype(F32)
    picked = hit.astype(BF).reshape(slots, rows)
    pick[...] = picked
    weighted = jnp.where(hit, gate_of[None, :, None, :], 0.0).reshape(slots, rows)
    whole = weighted.astype(BF)
    hi[...] = whole
    low[...] = (weighted - whole.astype(F32)).astype(BF)

    loads[1].wait()

    n_rows = n_ex * hc

    for p in range(2):

        @pl.loop(0, nd)
        def _(j):
            cols = pl.ds(pl.multiple_of(j * dtile, dtile), dtile)
            y_send[p, :, :, cols] = (
                jnp.dot(pick[p * n_rows : (p + 1) * n_rows, :], cot_ref[:, cols], preferred_element_type=F32)
                .astype(BF)
                .reshape(n_ex, hc, dtile)
            )

        y_start(p)

    meta_wait()

    got_len = meta_recv[:, 0, :]
    got_adv = meta_recv[:, 1, :]
    alive = (got_len > 0.0).astype(BF)
    lower = (iota((n_dp, n_dp), 1) < iota((n_dp, n_dp), 0)).astype(BF)
    arrival = jnp.dot(lower, alive, preferred_element_type=F32)
    arrival = jnp.where(got_len > 0.0, arrival, -1.0)
    per_len = got_adv / jnp.maximum(got_len, 1.0)

    def widen(v):
        return jnp.broadcast_to(v[:, None, :rows], (n_dp, slot, rows)).reshape(n_dp * slot, rows)

    placed = (widen(arrival) == (scol >> shift).astype(F32)) & same_place
    within = (srow & (slot - 1)).astype(F32) < widen(got_len)
    tok_scale = jnp.sum(
        jnp.where(placed & within, widen(per_len), 0.0), axis=0, keepdims=True
    )
    row_scale = jnp.sum(
        jnp.where(hit, (gate_of * tok_scale)[None, :, None, :], 0.0), axis=3, keepdims=True
    )
    lane_of = iota((2, n_ex, hc, lanes), 0) * hc + iota((2, n_ex, hc, lanes), 2)
    on_lane = lane_of == iota((2, n_ex, hc, lanes), 3)
    spread_scale = jnp.where(on_lane, row_scale, 0.0)
    spread_scale = jnp.sum(spread_scale[0] + spread_scale[1], axis=1, keepdims=True)
    scale_send[0] = jnp.broadcast_to(spread_scale, (n_ex, 8, lanes))
    v_start(0)
    fetch = contract(picked, placed.astype(BF), 1, 1).astype(BF)
    def fill_x(h, p):
        here = slice(p * n_rows, (p + 1) * n_rows)

        @pl.loop(0, nd // 2)
        def _(j):
            cols = pl.ds(pl.multiple_of(j * dtile, dtile), dtile)
            to_cols = pl.ds(pl.multiple_of(h * mid + j * dtile, dtile), dtile)
            source = seq_recv[h, :, :, cols].reshape(n_dp * slot, dtile)
            x_send[p, :, :, to_cols] = (
                jnp.dot(fetch[here, :], source, preferred_element_type=F32)
                .astype(BF)
                .reshape(n_ex, hc, dtile)
            )

        x_of[h][0](p)

    for h in range(2):
        seqs_of[h][1]()
        fill_x(h, 0)
        fill_x(h, 1)

    y_wait(0)
    y_wait(1)
    v_wait(0)
    scale = jnp.sum(
        jnp.where(on_lane, scale_recv[:, :, 0:1, :], 0.0), axis=3, keepdims=True
    ).reshape(slots, 1)

    @pl.loop(0, nd)
    def _(j):
        cols = pl.ds(pl.multiple_of(j * dtile, dtile), dtile)
        y_recv[:, :, :, cols] = (
            (y_recv[:, :, :, cols].reshape(slots, dtile).astype(F32) * scale)
            .astype(BF)
            .reshape(2, n_ex, hc, dtile)
        )

    for copy in loads[2:]:
        copy.wait()

    @pl.loop(0, nf)
    def _(j):
        cols = pl.ds(pl.multiple_of(j * ftile, ftile), ftile)
        hidden_grad[:, cols] = contract(y_recv[...].reshape(slots, width), wd[cols, :], 1, 1)

    def first_products():
        x_of[0][1](0)
        x_of[0][1](1)

        @pl.loop(0, nf)
        def _(j):
            cols = pl.ds(pl.multiple_of(j * ftile, ftile), ftile)
            x_some = x_recv[:, :, :, :mid].reshape(slots, mid)
            gate_part[:, cols] = jnp.dot(x_some, wg[:mid, cols], preferred_element_type=F32)
            up_part[:, cols] = jnp.dot(x_some, wu[:mid, cols], preferred_element_type=F32)

    def hidden_units(p):
        here = pl.ds(p * n_rows, n_rows)

        @pl.loop(0, nf)
        def _(j):
            cols = pl.ds(pl.multiple_of(j * ftile, ftile), ftile)
            x_some = x_recv[p, :, :, mid:].reshape(n_rows, mid)
            gate_pre = gate_part[here, cols] + jnp.dot(
                x_some, wg[mid:, cols], preferred_element_type=F32
            )
            up_pre = up_part[here, cols] + jnp.dot(
                x_some, wu[mid:, cols], preferred_element_type=F32
            )
            sig = jax.nn.sigmoid(gate_pre)
            act = gate_pre * sig
            hid[here, cols] = (act * up_pre).astype(BF)
            down = hidden_grad[here, cols]
            both[here, cols] = (
                down * up_pre * sig * (1.0 + gate_pre * (1.0 - sig))
            ).astype(BF)
            ups = pl.ds(pl.multiple_of(ff + j * ftile, ftile), ftile)
            both[here, ups] = (down * act).astype(BF)

    def output_rows(p):
        here = pl.ds(p * n_rows, n_rows)

        @pl.loop(0, nd)
        def _(j):
            cols = pl.ds(pl.multiple_of(j * dtile, dtile), dtile)
            o_send[p, :, :, cols] = (
                jnp.dot(hid[here, :], wd[:, cols], preferred_element_type=F32)
                .astype(BF)
                .reshape(n_ex, hc, dtile)
            )

    def input_rows(lo, hi):
        @pl.loop(lo, hi)
        def _(j):
            cols = pl.ds(pl.multiple_of(j * dtile, dtile), dtile)
            b_send[:, :, :, cols] = (
                (
                    contract(both[:, :ff], wg[cols, :], 1, 1)
                    + contract(both[:, ff:], wu[cols, :], 1, 1)
                )
                .astype(BF)
                .reshape(2, n_ex, hc, dtile)
            )

    grads = ((grad_d, twin_d, ring_d, gd_out), (grad_g, twin_g, ring_g, gg_out), (grad_u, twin_u, ring_u, gu_out))

    def block(i, b, c):
        part = grads[i][1].shape[1]
        return pl.ds(pl.multiple_of((b * 2 + c) * part, part), part)

    def twin_copy(i, b):
        return pltpu.make_async_remote_copy(
            src_ref=grads[i][0].at[block(i, b, 1 - core)],
            dst_ref=grads[i][1].at[b],
            send_sem=twin_ss.at[i],
            recv_sem=twin_rs.at[i, b],
            device_id={"dp": g + 1 - 2 * core},
            device_id_type=MESH,
        )

    def ring_copy(i, way, s):
        grad, _, ring, _ = grads[i]
        mid = grad.shape[1] // 2
        if s == 0:
            b = lax.rem(z + half, n_z)
            cols = pl.ds(way * mid, mid)
        else:
            b = lax.rem(z + (half - s) * (1 - 2 * way) + n_z, n_z)
            cols = pl.ds(0, 2 * mid)
        return pltpu.make_async_remote_copy(
            src_ref=grad.at[block(i, b, core), cols],
            dst_ref=ring.at[way, s, :, cols],
            send_sem=ring_ss.at[i],
            recv_sem=ring_rs.at[i, way, s],
            device_id={"dp": lax.rem(g + 2 * (1 - 2 * way) + n_dp, n_dp)},
            device_id_type=MESH,
        )

    def ring_step(i, s):
        grad, twin, ring, _ = grads[i]
        mid = grad.shape[1] // 2
        if s == 0:
            b = lax.rem(z + half, n_z)
            here = block(i, b, core)
            twin_copy(i, b).wait_recv()
            grad[here, :] = (grad[here, :].astype(F32) + twin[b].astype(F32)).astype(BF)
            ring_copy(i, 0, 0).start()
            ring_copy(i, 1, 0).start()
            return
        for way in range(2):
            b = lax.rem(z + (half - s) * (1 - 2 * way) + n_z, n_z)
            here = block(i, b, core)
            twin_copy(i, b).wait_recv()
            ring_copy(i, way, s - 1).wait_recv()
            if s == 1:
                near, far = pl.ds(way * mid, mid), pl.ds((1 - way) * mid, mid)
                grad[here, near] = (
                    grad[here, near].astype(F32)
                    + twin[b, :, near].astype(F32)
                    + ring[way, 0, :, near].astype(F32)
                ).astype(BF)
                grad[here, far] = (
                    grad[here, far].astype(F32) + twin[b, :, far].astype(F32)
                ).astype(BF)
            else:
                grad[here, :] = (
                    grad[here, :].astype(F32)
                    + twin[b].astype(F32)
                    + ring[way, s - 1].astype(F32)
                ).astype(BF)
            ring_copy(i, way, s).start()

    def ring_last(i):
        grad, twin, ring, out = grads[i]
        twin_copy(i, z).wait_recv()
        ring_copy(i, 0, half - 1).wait_recv()
        ring_copy(i, 1, half - 1).wait_recv()
        here = block(i, z, core)
        out[...] = (
            grad[here, :].astype(F32)
            + twin[z].astype(F32)
            + ring[0, half - 1].astype(F32)
            + ring[1, half - 1].astype(F32)
        ).astype(BF)

    pair = width // n_z

    def ring_order(k):
        d = half - lax.div(k + 1, 2)
        way = 2 * lax.rem(k, 2) - 1
        return lax.rem(z + way * d + n_z, n_z)

    def gate_up(lo, hi):
        @pl.loop(lo, hi)
        def _(k):
            b = ring_order(k)
            cols = pl.ds(pl.multiple_of(b * pair, pair), pair)
            x_part = x_recv[:, :, :, cols].reshape(slots, pair)
            sums = contract(x_part, both[...], 0, 0).astype(BF)
            grad_g[cols, :] = sums[:, :ff]
            grad_u[cols, :] = sums[:, ff:]
            twin_copy(1, b).start()
            twin_copy(2, b).start()

    wide = min(WIDE, width)

    def down_units(lo, hi):
        per = width // wide

        @pl.loop(lo * per, hi * per)
        def _(j):
            units = pl.ds(pl.multiple_of(lax.div(j, per) * ftile, ftile), ftile)
            cols = pl.ds(pl.multiple_of(lax.rem(j, per) * wide, wide), wide)
            grad_d[units, cols] = contract(
                hid[:, units], y_recv[:, :, :, cols].reshape(slots, wide), 0, 0
            ).astype(BF)

    def tokens_out():
        o_wait(0)
        o_wait(1)

        @pl.loop(0, nd)
        def _(j):
            cols = pl.ds(pl.multiple_of(j * dtile, dtile), dtile)
            back = o_recv[:, :, :, cols].reshape(slots, dtile)
            out_ref[:, cols] = (
                contract(hi[...], back, 0, 0) + contract(low[...], back, 0, 0)
            ).astype(BF)

    def tokens_dx(p):
        b_wait(p)

        @pl.loop(0, nd)
        def _(j):
            cols = pl.ds(pl.multiple_of(j * dtile, dtile), dtile)
            back = contract(
                pick[p * n_rows : (p + 1) * n_rows, :],
                b_recv[p, :, :, cols].reshape(n_rows, dtile),
                0,
                0,
            )
            if p == 0:
                dx_half[:, cols] = back
            else:
                dx_ref[:, cols] = (dx_half[:, cols] + back).astype(BF)

    cut1 = nf // 3

    first_products()
    x_of[1][1](0)
    hidden_units(0)
    output_rows(0)
    x_of[1][1](1)
    o_start(0)
    hidden_units(1)
    gate_up(0, 1)
    down_units(0, cut1)
    ring_step(1, 0)
    ring_step(2, 0)
    down_units(cut1, nf)

    @pl.loop(0, n_z)
    def _(k):
        twin_copy(0, ring_order(k)).start()

    gate_up(1, 3)
    ring_step(0, 0)
    output_rows(1)
    o_start(1)
    ring_step(1, 1)
    ring_step(2, 1)
    gate_up(3, min(5, n_z))
    ring_step(0, 1)
    input_rows(0, nd)
    b_start(0)
    b_start(1)
    if half > 2:
        ring_step(1, 2)
    if n_z > 5:
        gate_up(5, n_z)
    if half > 2:
        ring_step(2, 2)
        ring_step(0, 2)
    tokens_out()
    for s in range(3, half):
        for i in (1, 2, 0):
            ring_step(i, s)
    tokens_dx(0)
    tokens_dx(1)
    for i in (1, 2, 0):
        ring_last(i)

    for done in (
        meta_done,
        v_done,
        seqs_of[0][2],
        seqs_of[1][2],
        x_of[0][2],
        x_of[1][2],
        y_done,
        o_done,
        b_done,
    ):
        done()

    for i in range(3):
        grad, twin, _, _ = grads[i]
        part = twin.shape[1]
        for sem, count in ((twin_ss, n_z), (ring_ss, n_z - 1)):
            rows_sent = pl.ds(0, count * part)
            pltpu.make_async_remote_copy(
                src_ref=grad.at[rows_sent],
                dst_ref=grad.at[rows_sent],
                send_sem=sem.at[i],
                recv_sem=sem.at[i],
                device_id={"dp": g + 1 - 2 * core},
                device_id_type=MESH,
            ).wait_send()


def settle_kernel(*refs):
    n = (len(refs) - 1) // 2
    copies = [pltpu.make_async_copy(refs[i], refs[n + i], refs[2 * n].at[i]) for i in range(n)]
    for copy in copies:
        copy.start()
    for copy in copies:
        copy.wait()


def settle(arrays):
    n = len(arrays)
    return pl.pallas_call(
        settle_kernel,
        out_shape=[jax.ShapeDtypeStruct(a.shape, a.dtype) for a in arrays],
        in_specs=[pl.BlockSpec(memory_space=pltpu.VMEM)] * n,
        out_specs=[pl.BlockSpec(memory_space=pl.ANY)] * n,
        scratch_shapes=[pltpu.SemaphoreType.DMA((n,))],
        compiler_params=pltpu.CompilerParams(vmem_limit_bytes=4 * 1024 * 1024),
    )(*[pltpu.with_memory_space_constraint(a, pltpu.VMEM) for a in arrays])


def on_device(
    n_dp,
    n_ex,
    gen_rows,
    gen_lengths,
    gen_adv,
    destination,
    expert_ids,
    gate_values,
    cotangent,
    w_gate,
    w_up,
    w_down,
):
    rows, width = gen_rows.shape
    seqs = destination.shape[2]
    slot = rows // seqs
    ff = w_gate.shape[2]
    cap = 2 * rows * expert_ids.shape[1] // n_ex
    slots = n_ex * cap
    n_z = n_dp // 2
    lanes = max(cap, 128)
    vmem = pl.BlockSpec(memory_space=pltpu.VMEM)
    hbm = pl.BlockSpec(memory_space=pl.ANY)
    dma = pltpu.SemaphoreType.DMA
    part, part_d = width // n_dp, ff // n_dp
    buffers = [pltpu.VMEM((2, n_ex, cap // 2, width), BF)] * 8
    ring = [
        pltpu.VMEM((2, n_z // 2, p, c), BF) for p, c in ((part, ff), (part, ff), (part_d, width))
    ]
    twin = [pltpu.VMEM((n_z, p, c), BF) for p, c in ((part, ff), (part, ff), (part_d, width))]
    outs = pl.pallas_call(
        functools.partial(step_kernel, n_dp, n_ex, slot, cap),
        out_shape=(
            pltpu.VMEM((rows, width), BF),
            pltpu.VMEM((rows, width), BF),
            pltpu.VMEM((part, ff), BF),
            pltpu.VMEM((part, ff), BF),
            pltpu.VMEM((part_d, width), BF),
        ),
        in_specs=[vmem] * 5 + [hbm] * 5,
        out_specs=[vmem] * 5,
        scratch_shapes=[
            pltpu.VMEM((rows, width), BF),
            pltpu.VMEM((rows, width), BF),
            pltpu.VMEM((width, ff), BF),
            pltpu.VMEM((width, ff), BF),
            pltpu.VMEM((ff, width), BF),
            pltpu.VMEM((n_dp, 8, 128), F32),
            pltpu.VMEM((n_dp, 8, 128), F32),
            pltpu.VMEM((1, n_ex, 8, lanes), F32),
            pltpu.VMEM((1, n_ex, 8, lanes), F32),
            pltpu.VMEM((2, n_dp, slot, width // 2), BF),
            pltpu.VMEM((2, n_dp, slot, width // 2), BF),
            *buffers,
            pltpu.VMEM((slots, rows), BF),
            pltpu.VMEM((slots, rows), BF),
            pltpu.VMEM((slots, rows), BF),
            pltpu.VMEM((rows, width), F32),
            pltpu.VMEM((slots, ff), F32),
            pltpu.VMEM((slots, ff), F32),
            pltpu.VMEM((slots, ff), F32),
            pltpu.VMEM((slots, ff), BF),
            pltpu.VMEM((slots, 2 * ff), BF),
            pltpu.VMEM((width, ff), BF),
            pltpu.VMEM((width, ff), BF),
            pltpu.VMEM((ff, width), BF),
            *twin,
            *ring,
            dma((5,)),
            dma((3,)),
            dma((1, 3)),
            dma((2, 3)),
            dma((2, 2, 3)),
            *([dma((2, 3))] * 3),
            dma((3,)),
            dma((3, n_z)),
            dma((3,)),
            dma((3, 2, n_z // 2)),
        ],
        compiler_params=pltpu.CompilerParams(
            collective_id=0, has_side_effects=True, vmem_limit_bytes=62 * 1024 * 1024
        ),
    )(
        destination[0],
        gen_lengths[0],
        gen_adv[0],
        expert_ids.T,
        gate_values.T,
        gen_rows,
        cotangent,
        w_gate[0],
        w_up[0],
        w_down[0],
    )
    outs = settle(outs)
    return outs[0], outs[1], outs[2][None], outs[3][None], outs[4][None]


def solution(mesh):
    n_dp, n_ex = mesh.shape["dp"], mesh.shape["expert"]
    in_specs = (
        P(("dp", "expert"), None),
        P("dp", "expert", None),
        P("dp", "expert", None),
        P("dp", "expert", None),
        P(("dp", "expert"), None),
        P(("dp", "expert"), None),
        P(("dp", "expert"), None),
        P("expert", None, None),
        P("expert", None, None),
        P("expert", None, None),
    )
    out_specs = (
        P(("dp", "expert"), None),
        P(("dp", "expert"), None),
        P("expert", "dp", None),
        P("expert", "dp", None),
        P("expert", "dp", None),
    )
    return jax.shard_map(
        functools.partial(on_device, n_dp, n_ex),
        mesh=mesh,
        in_specs=in_specs,
        out_specs=out_specs,
        check_vma=False,
    )
```

```python
import functools

import jax
import jax.numpy as jnp
from jax import lax
from jax.experimental import pallas as pl
from jax.experimental.pallas import tpu as pltpu
from jax.sharding import PartitionSpec as P

MESH = pl.DeviceIdType.MESH
BF = jnp.bfloat16
F32 = jnp.float32
WIDE = 1024


def contract(left, right, left_dim, right_dim):
    return lax.dot_general(
        left, right, (((left_dim,), (right_dim,)), ((), ())), preferred_element_type=F32
    )


def iota(shape, dim):
    return lax.broadcasted_iota(jnp.int32, shape, dim)


def step_kernel(
    n_dp,
    n_ex,
    slot,
    cap,
    dest_ref,
    len_ref,
    adv_ref,
    ids_ref,
    gate_ref,
    gen_hbm,
    cot_hbm,
    wg_hbm,
    wu_hbm,
    wd_hbm,
    out_ref,
    dx_ref,
    gg_out,
    gu_out,
    gd_out,
    gen_ref,
    cot_ref,
    wg,
    wu,
    wd,
    meta_send,
    meta_recv,
    scale_send,
    scale_recv,
    seq_send,
    seq_recv,
    x_send,
    x_recv,
    y_send,
    y_recv,
    o_send,
    o_recv,
    b_send,
    b_recv,
    pick,
    hi,
    low,
    dx_half,
    gate_part,
    up_part,
    hidden_grad,
    hid,
    both,
    grad_g,
    grad_u,
    grad_d,
    twin_g,
    twin_u,
    twin_d,
    ring_g,
    ring_u,
    ring_d,
    w_sem,
    meta_sem,
    scale_sem,
    seq_sem,
    x_sem,
    y_sem,
    o_sem,
    b_sem,
    twin_ss,
    twin_rs,
    ring_ss,
    ring_rs,
):
    g = lax.axis_index("dp")
    e = lax.axis_index("expert")
    core = lax.rem(g, 2)
    z = lax.div(g, 2)
    n_z = n_dp // 2
    half = n_z // 2
    rows = gen_ref.shape[0]
    width = gen_ref.shape[1]
    ff = wg.shape[1]
    mid = width // 2
    slots = n_ex * cap
    hc = cap // 2
    lanes = max(cap, 128)
    dtile = min(256, width)
    ftile = min(256, ff)
    nd, nf = width // dtile, ff // ftile

    nx = 1
    while (nx * 2) * (nx * 2) <= n_ex:
        nx *= 2
    ny = n_ex // nx
    ex, ey = lax.rem(e, nx), lax.div(e, nx)

    def far(d, n):
        return min(d, n - d)

    tokens = sorted(
        ((dy, dx) for dy in range(ny) for dx in range(nx)),
        key=lambda d: -(far(d[0], ny) + far(d[1], nx)),
    )
    trainers = sorted(
        ((dz, dc) for dz in range(n_z) for dc in range(2)), key=lambda d: -(far(d[0], n_z) + d[1])
    )

    def expert_to(i, sign=1):
        dy, dx = tokens[i]
        return lax.rem(ey + sign * dy + ny, ny) * nx + lax.rem(ex + sign * dx + nx, nx)

    def trainer_to(i):
        dz, dc = trainers[i]
        return lax.rem(z + dz, n_z) * 2 + lax.rem(core + dc, 2)

    loads = [
        pltpu.make_async_copy(src, dst, w_sem.at[i])
        for i, (src, dst) in enumerate(
            ((cot_hbm, cot_ref), (gen_hbm, gen_ref), (wg_hbm, wg), (wu_hbm, wu), (wd_hbm, wd))
        )
    ]
    for copy in loads:
        copy.start()

    barrier = pltpu.get_barrier_semaphore()

    @pl.loop(1, n_dp)
    def _(o):
        pl.semaphore_signal(barrier, 1, device_id={"dp": lax.rem(g + o, n_dp)}, device_id_type=MESH)

    @pl.loop(1, n_ex)
    def _(o):
        pl.semaphore_signal(
            barrier, 1, device_id={"expert": lax.rem(e + o, n_ex)}, device_id_type=MESH
        )

    def dp_exchange(send, recv, sems):
        def copy(src, dst, peer):
            return pltpu.make_async_remote_copy(
                src_ref=src,
                dst_ref=dst,
                send_sem=sems.at[0],
                recv_sem=sems.at[1],
                device_id={"dp": peer},
                device_id_type=MESH,
            )

        own = pltpu.make_async_copy(send.at[g], recv.at[g], sems.at[2])
        others = pl.ds(0, n_dp - 1)
        every = copy(send.at[others], recv.at[others], trainer_to(0))

        def start():
            for i in range(n_dp - 1):
                peer = trainer_to(i)
                copy(send.at[peer], recv.at[g], peer).start()
            own.start()

        def wait_recv():
            own.wait()
            every.wait_recv()

        return start, wait_recv, every.wait_send

    def token_exchange(sign, send, recv, sems):
        def copy(p, i):
            return pltpu.make_async_remote_copy(
                src_ref=send.at[p, i],
                dst_ref=recv.at[p, i],
                send_sem=sems.at[p, 0],
                recv_sem=sems.at[p, 1],
                device_id={"expert": expert_to(0 if isinstance(i, pl.Slice) else i, sign)},
                device_id_type=MESH,
            )

        last = n_ex - 1

        def own(p):
            return pltpu.make_async_copy(send.at[p, last], recv.at[p, last], sems.at[p, 2])

        def start(p):
            for i in range(last):
                copy(p, i).start()
            own(p).start()

        def wait_recv(p):
            own(p).wait()
            copy(p, pl.ds(0, last)).wait_recv()

        def wait_send():
            for p in range(sems.shape[0]):
                copy(p, pl.ds(0, last)).wait_send()

        return start, wait_recv, wait_send

    meta_start, meta_wait, meta_done = dp_exchange(meta_send, meta_recv, meta_sem)
    seqs_of = [dp_exchange(seq_send.at[h], seq_recv.at[h], seq_sem.at[h]) for h in range(2)]
    halves = [pl.ds(h * mid, mid) for h in range(2)]
    x_of = [
        token_exchange(
            1,
            x_send.at[:, :, :, halves[h]],
            x_recv.at[:, :, :, halves[h]],
            x_sem.at[h],
        )
        for h in range(2)
    ]
    y_start, y_wait, y_done = token_exchange(1, y_send, y_recv, y_sem)
    v_start, v_wait, v_done = token_exchange(1, scale_send, scale_recv, scale_sem)
    o_start, o_wait, o_done = token_exchange(-1, o_send, o_recv, o_sem)
    b_start, b_wait, b_done = token_exchange(-1, b_send, b_recv, b_sem)

    names = jnp.zeros((n_ex, rows), jnp.int32)
    for i in range(n_ex):
        names = jnp.where(iota((n_ex, rows), 0) == i, expert_to(i), names)
    hit0, hit1 = ids_ref[0:1, :] == names, ids_ref[1:2, :] == names
    routed = hit0 | hit1
    gate_of = jnp.where(hit0, gate_ref[0:1, :], 0.0) + jnp.where(hit1, gate_ref[1:2, :], 0.0)
    before = (iota((rows, rows), 0) < iota((rows, rows), 1)).astype(BF)
    pos = jnp.dot(routed.astype(BF), before, preferred_element_type=F32)
    code = jnp.where(routed, pos, -1.0)
    place = iota((2, n_ex, hc, rows), 0) * hc + iota((2, n_ex, hc, rows), 2)
    hit = code[None, :, None, :] == place.astype(F32)
    picked = hit.astype(BF).reshape(slots, rows)
    pick[...] = picked
    weighted = jnp.where(hit, gate_of[None, :, None, :], 0.0).reshape(slots, rows)
    whole = weighted.astype(BF)
    hi[...] = whole
    low[...] = (weighted - whole.astype(F32)).astype(BF)

    n_rows = n_ex * hc

    def fill_y(p):
        @pl.loop(0, nd)
        def _(j):
            cols = pl.ds(pl.multiple_of(j * dtile, dtile), dtile)
            y_send[p, :, :, cols] = (
                jnp.dot(
                    pick[p * n_rows : (p + 1) * n_rows, :],
                    cot_ref[:, cols],
                    preferred_element_type=F32,
                )
                .astype(BF)
                .reshape(n_ex, hc, dtile)
            )

    loads[0].wait()
    fill_y(0)
    pl.semaphore_wait(barrier, n_dp + n_ex - 2)
    y_start(0)

    shift = slot.bit_length() - 1
    seqs = dest_ref.shape[1]
    srow, scol = iota((n_dp * slot, rows), 0), iota((n_dp * slot, rows), 1)
    same_place = (srow & (slot - 1)) == (scol & (slot - 1))
    mine = dest_ref[...] == iota((n_dp, seqs), 0)
    len_to = jnp.sum(jnp.where(mine, len_ref[...].astype(F32), 0.0), axis=1, keepdims=True)
    adv_to = jnp.sum(jnp.where(mine, adv_ref[...].astype(F32), 0.0), axis=1, keepdims=True)
    line = iota((n_dp, 8, 128), 1)
    meta_send[...] = jnp.where(line == 0, len_to[:, :, None], adv_to[:, :, None])
    seq_lanes = ((iota((seqs, rows), 1) >> shift) == iota((seqs, rows), 0)).astype(F32)
    mine_lanes = jnp.dot(mine.astype(F32), seq_lanes, preferred_element_type=F32)
    spread = jnp.broadcast_to(mine_lanes[:, None, :], (n_dp, slot, rows)).reshape(n_dp * slot, rows)
    spread = jnp.where(same_place, spread, 0.0).astype(BF)
    meta_start()
    loads[1].wait()

    for h in range(2):

        @pl.loop(0, nd // 2)
        def _(j):
            cols = pl.ds(pl.multiple_of(j * dtile, dtile), dtile)
            from_cols = pl.ds(pl.multiple_of(h * mid + j * dtile, dtile), dtile)
            seq_send[h, :, :, cols] = (
                jnp.dot(spread, gen_ref[:, from_cols], preferred_element_type=F32)
                .astype(BF)
                .reshape(n_dp, slot, dtile)
            )

        seqs_of[h][0]()

    fill_y(1)
    y_start(1)
    meta_wait()

    got_len = meta_recv[:, 0, :]
    got_adv = meta_recv[:, 1, :]
    alive = (got_len > 0.0).astype(BF)
    lower = (iota((n_dp, n_dp), 1) < iota((n_dp, n_dp), 0)).astype(BF)
    arrival = jnp.dot(lower, alive, preferred_element_type=F32)
    arrival = jnp.where(got_len > 0.0, arrival, -1.0)
    per_len = got_adv / jnp.maximum(got_len, 1.0)

    def widen(v):
        return jnp.broadcast_to(v[:, None, :rows], (n_dp, slot, rows)).reshape(n_dp * slot, rows)

    placed = (widen(arrival) == (scol >> shift).astype(F32)) & same_place
    within = (srow & (slot - 1)).astype(F32) < widen(got_len)
    tok_scale = jnp.sum(
        jnp.where(placed & within, widen(per_len), 0.0), axis=0, keepdims=True
    )
    row_scale = jnp.sum(
        jnp.where(hit, (gate_of * tok_scale)[None, :, None, :], 0.0), axis=3, keepdims=True
    )
    lane_of = iota((2, n_ex, hc, lanes), 0) * hc + iota((2, n_ex, hc, lanes), 2)
    on_lane = lane_of == iota((2, n_ex, hc, lanes), 3)
    spread_scale = jnp.where(on_lane, row_scale, 0.0)
    spread_scale = jnp.sum(spread_scale[0] + spread_scale[1], axis=1, keepdims=True)
    scale_send[0] = jnp.broadcast_to(spread_scale, (n_ex, 8, lanes))
    v_start(0)
    fetch = contract(picked, placed.astype(BF), 1, 1).astype(BF)
    def fill_x(h, p):
        here = slice(p * n_rows, (p + 1) * n_rows)

        @pl.loop(0, nd // 2)
        def _(j):
            cols = pl.ds(pl.multiple_of(j * dtile, dtile), dtile)
            to_cols = pl.ds(pl.multiple_of(h * mid + j * dtile, dtile), dtile)
            source = seq_recv[h, :, :, cols].reshape(n_dp * slot, dtile)
            x_send[p, :, :, to_cols] = (
                jnp.dot(fetch[here, :], source, preferred_element_type=F32)
                .astype(BF)
                .reshape(n_ex, hc, dtile)
            )

        x_of[h][0](p)

    for h in range(2):
        seqs_of[h][1]()
        fill_x(h, 0)
        fill_x(h, 1)

    y_wait(0)
    y_wait(1)
    v_wait(0)
    scale = jnp.sum(
        jnp.where(on_lane, scale_recv[:, :, 0:1, :], 0.0), axis=3, keepdims=True
    ).reshape(slots, 1)

    @pl.loop(0, nd)
    def _(j):
        cols = pl.ds(pl.multiple_of(j * dtile, dtile), dtile)
        y_recv[:, :, :, cols] = (
            (y_recv[:, :, :, cols].reshape(slots, dtile).astype(F32) * scale)
            .astype(BF)
            .reshape(2, n_ex, hc, dtile)
        )

    for copy in loads[2:]:
        copy.wait()

    @pl.loop(0, nf)
    def _(j):
        cols = pl.ds(pl.multiple_of(j * ftile, ftile), ftile)
        hidden_grad[:, cols] = contract(y_recv[...].reshape(slots, width), wd[cols, :], 1, 1)

    def first_products():
        x_of[0][1](0)
        x_of[0][1](1)

        @pl.loop(0, nf)
        def _(j):
            cols = pl.ds(pl.multiple_of(j * ftile, ftile), ftile)
            x_some = x_recv[:, :, :, :mid].reshape(slots, mid)
            gate_part[:, cols] = jnp.dot(x_some, wg[:mid, cols], preferred_element_type=F32)
            up_part[:, cols] = jnp.dot(x_some, wu[:mid, cols], preferred_element_type=F32)

    def hidden_units(p):
        here = pl.ds(p * n_rows, n_rows)

        @pl.loop(0, nf)
        def _(j):
            cols = pl.ds(pl.multiple_of(j * ftile, ftile), ftile)
            x_some = x_recv[p, :, :, mid:].reshape(n_rows, mid)
            gate_pre = gate_part[here, cols] + jnp.dot(
                x_some, wg[mid:, cols], preferred_element_type=F32
            )
            up_pre = up_part[here, cols] + jnp.dot(
                x_some, wu[mid:, cols], preferred_element_type=F32
            )
            sig = jax.nn.sigmoid(gate_pre)
            act = gate_pre * sig
            hid[here, cols] = (act * up_pre).astype(BF)
            down = hidden_grad[here, cols]
            both[here, cols] = (
                down * up_pre * sig * (1.0 + gate_pre * (1.0 - sig))
            ).astype(BF)
            ups = pl.ds(pl.multiple_of(ff + j * ftile, ftile), ftile)
            both[here, ups] = (down * act).astype(BF)

    def output_rows(p):
        here = pl.ds(p * n_rows, n_rows)

        @pl.loop(0, nd)
        def _(j):
            cols = pl.ds(pl.multiple_of(j * dtile, dtile), dtile)
            o_send[p, :, :, cols] = (
                jnp.dot(hid[here, :], wd[:, cols], preferred_element_type=F32)
                .astype(BF)
                .reshape(n_ex, hc, dtile)
            )

    def input_rows(lo, hi):
        @pl.loop(lo, hi)
        def _(j):
            cols = pl.ds(pl.multiple_of(j * dtile, dtile), dtile)
            b_send[:, :, :, cols] = (
                (
                    contract(both[:, :ff], wg[cols, :], 1, 1)
                    + contract(both[:, ff:], wu[cols, :], 1, 1)
                )
                .astype(BF)
                .reshape(2, n_ex, hc, dtile)
            )

    grads = ((grad_d, twin_d, ring_d, gd_out), (grad_g, twin_g, ring_g, gg_out), (grad_u, twin_u, ring_u, gu_out))

    def block(i, b, c):
        part = grads[i][1].shape[1]
        return pl.ds(pl.multiple_of((b * 2 + c) * part, part), part)

    def twin_copy(i, b):
        return pltpu.make_async_remote_copy(
            src_ref=grads[i][0].at[block(i, b, 1 - core)],
            dst_ref=grads[i][1].at[b],
            send_sem=twin_ss.at[i],
            recv_sem=twin_rs.at[i, b],
            device_id={"dp": g + 1 - 2 * core},
            device_id_type=MESH,
        )

    def ring_copy(i, way, s):
        grad, _, ring, _ = grads[i]
        mid = grad.shape[1] // 2
        if s == 0:
            b = lax.rem(z + half, n_z)
            cols = pl.ds(way * mid, mid)
        else:
            b = lax.rem(z + (half - s) * (1 - 2 * way) + n_z, n_z)
            cols = pl.ds(0, 2 * mid)
        return pltpu.make_async_remote_copy(
            src_ref=grad.at[block(i, b, core), cols],
            dst_ref=ring.at[way, s, :, cols],
            send_sem=ring_ss.at[i],
            recv_sem=ring_rs.at[i, way, s],
            device_id={"dp": lax.rem(g + 2 * (1 - 2 * way) + n_dp, n_dp)},
            device_id_type=MESH,
        )

    def ring_step(i, s):
        grad, twin, ring, _ = grads[i]
        mid = grad.shape[1] // 2
        if s == 0:
            b = lax.rem(z + half, n_z)
            here = block(i, b, core)
            twin_copy(i, b).wait_recv()
            grad[here, :] = (grad[here, :].astype(F32) + twin[b].astype(F32)).astype(BF)
            ring_copy(i, 0, 0).start()
            ring_copy(i, 1, 0).start()
            return
        for way in range(2):
            b = lax.rem(z + (half - s) * (1 - 2 * way) + n_z, n_z)
            here = block(i, b, core)
            twin_copy(i, b).wait_recv()
            ring_copy(i, way, s - 1).wait_recv()
            if s == 1:
                near, far = pl.ds(way * mid, mid), pl.ds((1 - way) * mid, mid)
                grad[here, near] = (
                    grad[here, near].astype(F32)
                    + twin[b, :, near].astype(F32)
                    + ring[way, 0, :, near].astype(F32)
                ).astype(BF)
                grad[here, far] = (
                    grad[here, far].astype(F32) + twin[b, :, far].astype(F32)
                ).astype(BF)
            else:
                grad[here, :] = (
                    grad[here, :].astype(F32)
                    + twin[b].astype(F32)
                    + ring[way, s - 1].astype(F32)
                ).astype(BF)
            ring_copy(i, way, s).start()

    def ring_last(i):
        grad, twin, ring, out = grads[i]
        twin_copy(i, z).wait_recv()
        ring_copy(i, 0, half - 1).wait_recv()
        ring_copy(i, 1, half - 1).wait_recv()
        here = block(i, z, core)
        out[...] = (
            grad[here, :].astype(F32)
            + twin[z].astype(F32)
            + ring[0, half - 1].astype(F32)
            + ring[1, half - 1].astype(F32)
        ).astype(BF)

    pair = width // n_z

    def ring_order(k):
        d = half - lax.div(k + 1, 2)
        way = 2 * lax.rem(k, 2) - 1
        return lax.rem(z + way * d + n_z, n_z)

    def gate_up(lo, hi):
        @pl.loop(lo, hi)
        def _(k):
            b = ring_order(k)
            cols = pl.ds(pl.multiple_of(b * pair, pair), pair)
            x_part = x_recv[:, :, :, cols].reshape(slots, pair)
            sums = contract(x_part, both[...], 0, 0).astype(BF)
            grad_g[cols, :] = sums[:, :ff]
            grad_u[cols, :] = sums[:, ff:]
            twin_copy(1, b).start()
            twin_copy(2, b).start()

    wide = min(WIDE, width)

    def down_units(lo, hi):
        per = width // wide

        @pl.loop(lo * per, hi * per)
        def _(j):
            units = pl.ds(pl.multiple_of(lax.div(j, per) * ftile, ftile), ftile)
            cols = pl.ds(pl.multiple_of(lax.rem(j, per) * wide, wide), wide)
            grad_d[units, cols] = contract(
                hid[:, units], y_recv[:, :, :, cols].reshape(slots, wide), 0, 0
            ).astype(BF)

    def tokens_out():
        o_wait(0)
        o_wait(1)

        @pl.loop(0, nd)
        def _(j):
            cols = pl.ds(pl.multiple_of(j * dtile, dtile), dtile)
            back = o_recv[:, :, :, cols].reshape(slots, dtile)
            out_ref[:, cols] = (
                contract(hi[...], back, 0, 0) + contract(low[...], back, 0, 0)
            ).astype(BF)

    def tokens_dx(p):
        b_wait(p)

        @pl.loop(0, nd)
        def _(j):
            cols = pl.ds(pl.multiple_of(j * dtile, dtile), dtile)
            back = contract(
                pick[p * n_rows : (p + 1) * n_rows, :],
                b_recv[p, :, :, cols].reshape(n_rows, dtile),
                0,
                0,
            )
            if p == 0:
                dx_half[:, cols] = back
            else:
                dx_ref[:, cols] = (dx_half[:, cols] + back).astype(BF)

    cut1 = nf // 3

    first_products()
    x_of[1][1](0)
    hidden_units(0)
    output_rows(0)
    x_of[1][1](1)
    o_start(0)
    hidden_units(1)
    gate_up(0, 1)
    down_units(0, cut1)
    ring_step(1, 0)
    ring_step(2, 0)
    down_units(cut1, nf)

    @pl.loop(0, n_z)
    def _(k):
        twin_copy(0, ring_order(k)).start()

    gate_up(1, 3)
    ring_step(0, 0)
    output_rows(1)
    o_start(1)
    ring_step(1, 1)
    ring_step(2, 1)
    gate_up(3, min(5, n_z))
    ring_step(0, 1)
    input_rows(0, nd)
    b_start(0)
    b_start(1)
    if half > 2:
        ring_step(1, 2)
    if n_z > 5:
        gate_up(5, n_z)
    if half > 2:
        ring_step(2, 2)
        ring_step(0, 2)
    for s in range(3, half):
        for i in (1, 2, 0):
            ring_step(i, s)
    tokens_out()
    tokens_dx(0)
    tokens_dx(1)
    for i in (1, 2, 0):
        ring_last(i)

    for done in (
        meta_done,
        v_done,
        seqs_of[0][2],
        seqs_of[1][2],
        x_of[0][2],
        x_of[1][2],
        y_done,
        o_done,
        b_done,
    ):
        done()

    for i in range(3):
        grad, twin, _, _ = grads[i]
        part = twin.shape[1]
        for sem, count in ((twin_ss, n_z), (ring_ss, n_z - 1)):
            rows_sent = pl.ds(0, count * part)
            pltpu.make_async_remote_copy(
                src_ref=grad.at[rows_sent],
                dst_ref=grad.at[rows_sent],
                send_sem=sem.at[i],
                recv_sem=sem.at[i],
                device_id={"dp": g + 1 - 2 * core},
                device_id_type=MESH,
            ).wait_send()


def settle_kernel(*refs):
    n = (len(refs) - 1) // 2
    copies = [pltpu.make_async_copy(refs[i], refs[n + i], refs[2 * n].at[i]) for i in range(n)]
    for copy in copies:
        copy.start()
    for copy in copies:
        copy.wait()


def settle(arrays):
    n = len(arrays)
    return pl.pallas_call(
        settle_kernel,
        out_shape=[jax.ShapeDtypeStruct(a.shape, a.dtype) for a in arrays],
        in_specs=[pl.BlockSpec(memory_space=pltpu.VMEM)] * n,
        out_specs=[pl.BlockSpec(memory_space=pl.ANY)] * n,
        scratch_shapes=[pltpu.SemaphoreType.DMA((n,))],
        compiler_params=pltpu.CompilerParams(vmem_limit_bytes=4 * 1024 * 1024),
    )(*[pltpu.with_memory_space_constraint(a, pltpu.VMEM) for a in arrays])


def on_device(
    n_dp,
    n_ex,
    gen_rows,
    gen_lengths,
    gen_adv,
    destination,
    expert_ids,
    gate_values,
    cotangent,
    w_gate,
    w_up,
    w_down,
):
    rows, width = gen_rows.shape
    seqs = destination.shape[2]
    slot = rows // seqs
    ff = w_gate.shape[2]
    cap = 2 * rows * expert_ids.shape[1] // n_ex
    slots = n_ex * cap
    n_z = n_dp // 2
    lanes = max(cap, 128)
    vmem = pl.BlockSpec(memory_space=pltpu.VMEM)
    hbm = pl.BlockSpec(memory_space=pl.ANY)
    dma = pltpu.SemaphoreType.DMA
    part, part_d = width // n_dp, ff // n_dp
    buffers = [pltpu.VMEM((2, n_ex, cap // 2, width), BF)] * 8
    ring = [
        pltpu.VMEM((2, n_z // 2, p, c), BF) for p, c in ((part, ff), (part, ff), (part_d, width))
    ]
    twin = [pltpu.VMEM((n_z, p, c), BF) for p, c in ((part, ff), (part, ff), (part_d, width))]
    outs = pl.pallas_call(
        functools.partial(step_kernel, n_dp, n_ex, slot, cap),
        out_shape=(
            pltpu.VMEM((rows, width), BF),
            pltpu.VMEM((rows, width), BF),
            pltpu.VMEM((part, ff), BF),
            pltpu.VMEM((part, ff), BF),
            pltpu.VMEM((part_d, width), BF),
        ),
        in_specs=[vmem] * 5 + [hbm] * 5,
        out_specs=[vmem] * 5,
        scratch_shapes=[
            pltpu.VMEM((rows, width), BF),
            pltpu.VMEM((rows, width), BF),
            pltpu.VMEM((width, ff), BF),
            pltpu.VMEM((width, ff), BF),
            pltpu.VMEM((ff, width), BF),
            pltpu.VMEM((n_dp, 8, 128), F32),
            pltpu.VMEM((n_dp, 8, 128), F32),
            pltpu.VMEM((1, n_ex, 8, lanes), F32),
            pltpu.VMEM((1, n_ex, 8, lanes), F32),
            pltpu.VMEM((2, n_dp, slot, width // 2), BF),
            pltpu.VMEM((2, n_dp, slot, width // 2), BF),
            *buffers,
            pltpu.VMEM((slots, rows), BF),
            pltpu.VMEM((slots, rows), BF),
            pltpu.VMEM((slots, rows), BF),
            pltpu.VMEM((rows, width), F32),
            pltpu.VMEM((slots, ff), F32),
            pltpu.VMEM((slots, ff), F32),
            pltpu.VMEM((slots, ff), F32),
            pltpu.VMEM((slots, ff), BF),
            pltpu.VMEM((slots, 2 * ff), BF),
            pltpu.VMEM((width, ff), BF),
            pltpu.VMEM((width, ff), BF),
            pltpu.VMEM((ff, width), BF),
            *twin,
            *ring,
            dma((5,)),
            dma((3,)),
            dma((1, 3)),
            dma((2, 3)),
            dma((2, 2, 3)),
            *([dma((2, 3))] * 3),
            dma((3,)),
            dma((3, n_z)),
            dma((3,)),
            dma((3, 2, n_z // 2)),
        ],
        compiler_params=pltpu.CompilerParams(
            collective_id=0, has_side_effects=True, vmem_limit_bytes=62 * 1024 * 1024
        ),
    )(
        destination[0],
        gen_lengths[0],
        gen_adv[0],
        expert_ids.T,
        gate_values.T,
        gen_rows,
        cotangent,
        w_gate[0],
        w_up[0],
        w_down[0],
    )
    outs = settle(outs)
    return outs[0], outs[1], outs[2][None], outs[3][None], outs[4][None]


def solution(mesh):
    n_dp, n_ex = mesh.shape["dp"], mesh.shape["expert"]
    in_specs = (
        P(("dp", "expert"), None),
        P("dp", "expert", None),
        P("dp", "expert", None),
        P("dp", "expert", None),
        P(("dp", "expert"), None),
        P(("dp", "expert"), None),
        P(("dp", "expert"), None),
        P("expert", None, None),
        P("expert", None, None),
        P("expert", None, None),
    )
    out_specs = (
        P(("dp", "expert"), None),
        P(("dp", "expert"), None),
        P("expert", "dp", None),
        P("expert", "dp", None),
        P("expert", "dp", None),
    )
    return jax.shard_map(
        functools.partial(on_device, n_dp, n_ex),
        mesh=mesh,
        in_specs=in_specs,
        out_specs=out_specs,
        check_vma=False,
    )
```

```python
import functools

import jax
import jax.numpy as jnp
from jax import lax
from jax.experimental import pallas as pl
from jax.experimental.pallas import tpu as pltpu
from jax.sharding import PartitionSpec as P

MESH = pl.DeviceIdType.MESH
BF = jnp.bfloat16
F32 = jnp.float32
WIDE = 1024


def contract(left, right, left_dim, right_dim):
    return lax.dot_general(
        left, right, (((left_dim,), (right_dim,)), ((), ())), preferred_element_type=F32
    )


def iota(shape, dim):
    return lax.broadcasted_iota(jnp.int32, shape, dim)


def step_kernel(
    n_dp,
    n_ex,
    slot,
    cap,
    dest_ref,
    len_ref,
    adv_ref,
    ids_ref,
    gate_ref,
    gen_hbm,
    cot_hbm,
    wg_hbm,
    wu_hbm,
    wd_hbm,
    out_ref,
    dx_ref,
    gg_out,
    gu_out,
    gd_out,
    gen_ref,
    cot_ref,
    wg,
    wu,
    wd,
    meta_send,
    meta_recv,
    scale_send,
    scale_recv,
    seq_send,
    seq_recv,
    x_send,
    x_recv,
    y_send,
    y_recv,
    o_send,
    o_recv,
    b_send,
    b_recv,
    pick,
    hi,
    low,
    dx_half,
    gate_part,
    up_part,
    hidden_grad,
    hid,
    both,
    grad_g,
    grad_u,
    grad_d,
    twin_g,
    twin_u,
    twin_d,
    ring_g,
    ring_u,
    ring_d,
    w_sem,
    meta_sem,
    scale_sem,
    seq_sem,
    x_sem,
    y_sem,
    o_sem,
    b_sem,
    twin_ss,
    twin_rs,
    ring_ss,
    ring_rs,
):
    g = lax.axis_index("dp")
    e = lax.axis_index("expert")
    core = lax.rem(g, 2)
    z = lax.div(g, 2)
    n_z = n_dp // 2
    half = n_z // 2
    rows = gen_ref.shape[0]
    width = gen_ref.shape[1]
    ff = wg.shape[1]
    mid = width // 2
    slots = n_ex * cap
    hc = cap // 2
    lanes = max(cap, 128)
    dtile = min(256, width)
    ftile = min(256, ff)
    nd, nf = width // dtile, ff // ftile

    nx = 1
    while (nx * 2) * (nx * 2) <= n_ex:
        nx *= 2
    ny = n_ex // nx
    ex, ey = lax.rem(e, nx), lax.div(e, nx)

    def far(d, n):
        return min(d, n - d)

    tokens = sorted(
        ((dy, dx) for dy in range(ny) for dx in range(nx)),
        key=lambda d: -(far(d[0], ny) + far(d[1], nx)),
    )
    trainers = sorted(
        ((dz, dc) for dz in range(n_z) for dc in range(2)), key=lambda d: -(far(d[0], n_z) + d[1])
    )

    def expert_to(i, sign=1):
        dy, dx = tokens[i]
        return lax.rem(ey + sign * dy + ny, ny) * nx + lax.rem(ex + sign * dx + nx, nx)

    def trainer_to(i):
        dz, dc = trainers[i]
        return lax.rem(z + dz, n_z) * 2 + lax.rem(core + dc, 2)

    loads = [
        pltpu.make_async_copy(src, dst, w_sem.at[i])
        for i, (src, dst) in enumerate(
            ((cot_hbm, cot_ref), (gen_hbm, gen_ref), (wg_hbm, wg), (wu_hbm, wu), (wd_hbm, wd))
        )
    ]
    for copy in loads:
        copy.start()

    barrier = pltpu.get_barrier_semaphore()

    for i in range(max(n_dp, n_ex) - 1):
        if i < n_dp - 1:
            pl.semaphore_signal(
                barrier, 1, device_id={"dp": trainer_to(i)}, device_id_type=MESH
            )
        if i < n_ex - 1:
            pl.semaphore_signal(
                barrier, 1, device_id={"expert": expert_to(i)}, device_id_type=MESH
            )

    def dp_exchange(send, recv, sems):
        def copy(src, dst, peer):
            return pltpu.make_async_remote_copy(
                src_ref=src,
                dst_ref=dst,
                send_sem=sems.at[0],
                recv_sem=sems.at[1],
                device_id={"dp": peer},
                device_id_type=MESH,
            )

        own = pltpu.make_async_copy(send.at[g], recv.at[g], sems.at[2])
        others = pl.ds(0, n_dp - 1)
        every = copy(send.at[others], recv.at[others], trainer_to(0))

        def start():
            for i in range(n_dp - 1):
                peer = trainer_to(i)
                copy(send.at[peer], recv.at[g], peer).start()
            own.start()

        def wait_recv():
            own.wait()
            every.wait_recv()

        return start, wait_recv, every.wait_send

    def token_exchange(sign, send, recv, sems):
        def copy(p, i):
            return pltpu.make_async_remote_copy(
                src_ref=send.at[p, i],
                dst_ref=recv.at[p, i],
                send_sem=sems.at[p, 0],
                recv_sem=sems.at[p, 1],
                device_id={"expert": expert_to(0 if isinstance(i, pl.Slice) else i, sign)},
                device_id_type=MESH,
            )

        last = n_ex - 1

        def own(p):
            return pltpu.make_async_copy(send.at[p, last], recv.at[p, last], sems.at[p, 2])

        def start(p):
            for i in range(last):
                copy(p, i).start()
            own(p).start()

        def wait_recv(p):
            own(p).wait()
            copy(p, pl.ds(0, last)).wait_recv()

        def wait_send():
            for p in range(sems.shape[0]):
                copy(p, pl.ds(0, last)).wait_send()

        return start, wait_recv, wait_send

    meta_start, meta_wait, meta_done = dp_exchange(meta_send, meta_recv, meta_sem)
    seqs_of = [dp_exchange(seq_send.at[h], seq_recv.at[h], seq_sem.at[h]) for h in range(2)]
    halves = [pl.ds(h * mid, mid) for h in range(2)]
    x_of = [
        token_exchange(
            1,
            x_send.at[:, :, :, halves[h]],
            x_recv.at[:, :, :, halves[h]],
            x_sem.at[h],
        )
        for h in range(2)
    ]
    y_start, y_wait, y_done = token_exchange(1, y_send, y_recv, y_sem)
    v_start, v_wait, v_done = token_exchange(1, scale_send, scale_recv, scale_sem)
    o_start, o_wait, o_done = token_exchange(-1, o_send, o_recv, o_sem)
    b_start, b_wait, b_done = token_exchange(-1, b_send, b_recv, b_sem)

    names = jnp.zeros((n_ex, rows), jnp.int32)
    for i in range(n_ex):
        names = jnp.where(iota((n_ex, rows), 0) == i, expert_to(i), names)
    hit0, hit1 = ids_ref[0:1, :] == names, ids_ref[1:2, :] == names
    routed = hit0 | hit1
    gate_of = jnp.where(hit0, gate_ref[0:1, :], 0.0) + jnp.where(hit1, gate_ref[1:2, :], 0.0)
    before = (iota((rows, rows), 0) < iota((rows, rows), 1)).astype(BF)
    pos = jnp.dot(routed.astype(BF), before, preferred_element_type=F32)
    code = jnp.where(routed, pos, -1.0)
    place = iota((2, n_ex, hc, rows), 0) * hc + iota((2, n_ex, hc, rows), 2)
    hit = code[None, :, None, :] == place.astype(F32)
    picked = hit.astype(BF).reshape(slots, rows)
    pick[...] = picked
    weighted = jnp.where(hit, gate_of[None, :, None, :], 0.0).reshape(slots, rows)
    whole = weighted.astype(BF)
    hi[...] = whole
    low[...] = (weighted - whole.astype(F32)).astype(BF)

    n_rows = n_ex * hc

    def fill_y(p):
        @pl.loop(0, nd, unroll=4)
        def _(j):
            cols = pl.ds(pl.multiple_of(j * dtile, dtile), dtile)
            y_send[p, :, :, cols] = (
                jnp.dot(
                    pick[p * n_rows : (p + 1) * n_rows, :],
                    cot_ref[:, cols],
                    preferred_element_type=F32,
                )
                .astype(BF)
                .reshape(n_ex, hc, dtile)
            )

    loads[0].wait()
    fill_y(0)
    pl.semaphore_wait(barrier, n_dp + n_ex - 2)
    y_start(0)

    shift = slot.bit_length() - 1
    seqs = dest_ref.shape[1]
    srow, scol = iota((n_dp * slot, rows), 0), iota((n_dp * slot, rows), 1)
    same_place = (srow & (slot - 1)) == (scol & (slot - 1))
    mine = dest_ref[...] == iota((n_dp, seqs), 0)
    len_to = jnp.sum(jnp.where(mine, len_ref[...].astype(F32), 0.0), axis=1, keepdims=True)
    adv_to = jnp.sum(jnp.where(mine, adv_ref[...].astype(F32), 0.0), axis=1, keepdims=True)
    line = iota((n_dp, 8, 128), 1)
    meta_send[...] = jnp.where(line == 0, len_to[:, :, None], adv_to[:, :, None])
    seq_lanes = ((iota((seqs, rows), 1) >> shift) == iota((seqs, rows), 0)).astype(F32)
    mine_lanes = jnp.dot(mine.astype(F32), seq_lanes, preferred_element_type=F32)
    spread = jnp.broadcast_to(mine_lanes[:, None, :], (n_dp, slot, rows)).reshape(n_dp * slot, rows)
    spread = jnp.where(same_place, spread, 0.0).astype(BF)
    meta_start()
    loads[1].wait()

    for h in range(2):

        @pl.loop(0, nd // 2)
        def _(j):
            cols = pl.ds(pl.multiple_of(j * dtile, dtile), dtile)
            from_cols = pl.ds(pl.multiple_of(h * mid + j * dtile, dtile), dtile)
            seq_send[h, :, :, cols] = (
                jnp.dot(spread, gen_ref[:, from_cols], preferred_element_type=F32)
                .astype(BF)
                .reshape(n_dp, slot, dtile)
            )

        seqs_of[h][0]()

    fill_y(1)
    y_start(1)
    meta_wait()

    got_len = meta_recv[:, 0, :]
    got_adv = meta_recv[:, 1, :]
    alive = (got_len > 0.0).astype(BF)
    lower = (iota((n_dp, n_dp), 1) < iota((n_dp, n_dp), 0)).astype(BF)
    arrival = jnp.dot(lower, alive, preferred_element_type=F32)
    arrival = jnp.where(got_len > 0.0, arrival, -1.0)
    per_len = got_adv / jnp.maximum(got_len, 1.0)

    def widen(v):
        return jnp.broadcast_to(v[:, None, :rows], (n_dp, slot, rows)).reshape(n_dp * slot, rows)

    placed = (widen(arrival) == (scol >> shift).astype(F32)) & same_place
    within = (srow & (slot - 1)).astype(F32) < widen(got_len)
    tok_scale = jnp.sum(
        jnp.where(placed & within, widen(per_len), 0.0), axis=0, keepdims=True
    )
    row_scale = jnp.sum(
        jnp.where(hit, (gate_of * tok_scale)[None, :, None, :], 0.0), axis=3, keepdims=True
    )
    lane_of = iota((2, n_ex, hc, lanes), 0) * hc + iota((2, n_ex, hc, lanes), 2)
    on_lane = lane_of == iota((2, n_ex, hc, lanes), 3)
    spread_scale = jnp.where(on_lane, row_scale, 0.0)
    spread_scale = jnp.sum(spread_scale[0] + spread_scale[1], axis=1, keepdims=True)
    scale_send[0] = jnp.broadcast_to(spread_scale, (n_ex, 8, lanes))
    v_start(0)
    fetch = contract(picked, placed.astype(BF), 1, 1).astype(BF)
    def fill_x(h, p):
        here = slice(p * n_rows, (p + 1) * n_rows)

        @pl.loop(0, nd // 2)
        def _(j):
            cols = pl.ds(pl.multiple_of(j * dtile, dtile), dtile)
            to_cols = pl.ds(pl.multiple_of(h * mid + j * dtile, dtile), dtile)
            source = seq_recv[h, :, :, cols].reshape(n_dp * slot, dtile)
            x_send[p, :, :, to_cols] = (
                jnp.dot(fetch[here, :], source, preferred_element_type=F32)
                .astype(BF)
                .reshape(n_ex, hc, dtile)
            )

        x_of[h][0](p)

    for h in range(2):
        seqs_of[h][1]()
        fill_x(h, 0)
        fill_x(h, 1)

    y_wait(0)
    y_wait(1)
    v_wait(0)
    scale = jnp.sum(
        jnp.where(on_lane, scale_recv[:, :, 0:1, :], 0.0), axis=3, keepdims=True
    ).reshape(slots, 1)

    @pl.loop(0, nd)
    def _(j):
        cols = pl.ds(pl.multiple_of(j * dtile, dtile), dtile)
        y_recv[:, :, :, cols] = (
            (y_recv[:, :, :, cols].reshape(slots, dtile).astype(F32) * scale)
            .astype(BF)
            .reshape(2, n_ex, hc, dtile)
        )

    for copy in loads[2:]:
        copy.wait()

    @pl.loop(0, nf)
    def _(j):
        cols = pl.ds(pl.multiple_of(j * ftile, ftile), ftile)
        hidden_grad[:, cols] = contract(y_recv[...].reshape(slots, width), wd[cols, :], 1, 1)

    def first_products():
        x_of[0][1](0)
        x_of[0][1](1)

        @pl.loop(0, nf)
        def _(j):
            cols = pl.ds(pl.multiple_of(j * ftile, ftile), ftile)
            x_some = x_recv[:, :, :, :mid].reshape(slots, mid)
            gate_part[:, cols] = jnp.dot(x_some, wg[:mid, cols], preferred_element_type=F32)
            up_part[:, cols] = jnp.dot(x_some, wu[:mid, cols], preferred_element_type=F32)

    def hidden_units(p):
        here = pl.ds(p * n_rows, n_rows)

        @pl.loop(0, nf, unroll=True)
        def _(j):
            cols = pl.ds(pl.multiple_of(j * ftile, ftile), ftile)
            x_some = x_recv[p, :, :, mid:].reshape(n_rows, mid)
            gate_pre = gate_part[here, cols] + jnp.dot(
                x_some, wg[mid:, cols], preferred_element_type=F32
            )
            up_pre = up_part[here, cols] + jnp.dot(
                x_some, wu[mid:, cols], preferred_element_type=F32
            )
            sig = jax.nn.sigmoid(gate_pre)
            act = gate_pre * sig
            hid[here, cols] = (act * up_pre).astype(BF)
            down = hidden_grad[here, cols]
            both[here, cols] = (
                down * up_pre * sig * (1.0 + gate_pre * (1.0 - sig))
            ).astype(BF)
            ups = pl.ds(pl.multiple_of(ff + j * ftile, ftile), ftile)
            both[here, ups] = (down * act).astype(BF)

    def output_rows(p):
        here = pl.ds(p * n_rows, n_rows)

        @pl.loop(0, nd)
        def _(j):
            cols = pl.ds(pl.multiple_of(j * dtile, dtile), dtile)
            o_send[p, :, :, cols] = (
                jnp.dot(hid[here, :], wd[:, cols], preferred_element_type=F32)
                .astype(BF)
                .reshape(n_ex, hc, dtile)
            )

    def input_rows(lo, hi):
        @pl.loop(lo, hi)
        def _(j):
            cols = pl.ds(pl.multiple_of(j * dtile, dtile), dtile)
            b_send[:, :, :, cols] = (
                (
                    contract(both[:, :ff], wg[cols, :], 1, 1)
                    + contract(both[:, ff:], wu[cols, :], 1, 1)
                )
                .astype(BF)
                .reshape(2, n_ex, hc, dtile)
            )

    grads = ((grad_d, twin_d, ring_d, gd_out), (grad_g, twin_g, ring_g, gg_out), (grad_u, twin_u, ring_u, gu_out))

    def block(i, b, c):
        part = grads[i][1].shape[1]
        return pl.ds(pl.multiple_of((b * 2 + c) * part, part), part)

    def twin_copy(i, b):
        return pltpu.make_async_remote_copy(
            src_ref=grads[i][0].at[block(i, b, 1 - core)],
            dst_ref=grads[i][1].at[b],
            send_sem=twin_ss.at[i],
            recv_sem=twin_rs.at[i, b],
            device_id={"dp": g + 1 - 2 * core},
            device_id_type=MESH,
        )

    def ring_copy(i, way, s):
        grad, _, ring, _ = grads[i]
        mid = grad.shape[1] // 2
        if s == 0:
            b = lax.rem(z + half, n_z)
            cols = pl.ds(way * mid, mid)
        else:
            b = lax.rem(z + (half - s) * (1 - 2 * way) + n_z, n_z)
            cols = pl.ds(0, 2 * mid)
        return pltpu.make_async_remote_copy(
            src_ref=grad.at[block(i, b, core), cols],
            dst_ref=ring.at[way, s, :, cols],
            send_sem=ring_ss.at[i],
            recv_sem=ring_rs.at[i, way, s],
            device_id={"dp": lax.rem(g + 2 * (1 - 2 * way) + n_dp, n_dp)},
            device_id_type=MESH,
        )

    def ring_step(i, s):
        grad, twin, ring, _ = grads[i]
        mid = grad.shape[1] // 2
        if s == 0:
            b = lax.rem(z + half, n_z)
            here = block(i, b, core)
            twin_copy(i, b).wait_recv()
            grad[here, :] = (grad[here, :].astype(F32) + twin[b].astype(F32)).astype(BF)
            ring_copy(i, 0, 0).start()
            ring_copy(i, 1, 0).start()
            return
        for way in range(2):
            b = lax.rem(z + (half - s) * (1 - 2 * way) + n_z, n_z)
            here = block(i, b, core)
            twin_copy(i, b).wait_recv()
            ring_copy(i, way, s - 1).wait_recv()
            if s == 1:
                near, far = pl.ds(way * mid, mid), pl.ds((1 - way) * mid, mid)
                grad[here, near] = (
                    grad[here, near].astype(F32)
                    + twin[b, :, near].astype(F32)
                    + ring[way, 0, :, near].astype(F32)
                ).astype(BF)
                grad[here, far] = (
                    grad[here, far].astype(F32) + twin[b, :, far].astype(F32)
                ).astype(BF)
            else:
                grad[here, :] = (
                    grad[here, :].astype(F32)
                    + twin[b].astype(F32)
                    + ring[way, s - 1].astype(F32)
                ).astype(BF)
            ring_copy(i, way, s).start()

    def ring_last(i):
        grad, twin, ring, out = grads[i]
        twin_copy(i, z).wait_recv()
        ring_copy(i, 0, half - 1).wait_recv()
        ring_copy(i, 1, half - 1).wait_recv()
        here = block(i, z, core)
        out[...] = (
            grad[here, :].astype(F32)
            + twin[z].astype(F32)
            + ring[0, half - 1].astype(F32)
            + ring[1, half - 1].astype(F32)
        ).astype(BF)

    pair = width // n_z

    def ring_order(k):
        d = half - lax.div(k + 1, 2)
        way = 2 * lax.rem(k, 2) - 1
        return lax.rem(z + way * d + n_z, n_z)

    def gate_up(lo, hi):
        @pl.loop(lo, hi)
        def _(k):
            b = ring_order(k)
            cols = pl.ds(pl.multiple_of(b * pair, pair), pair)
            x_part = x_recv[:, :, :, cols].reshape(slots, pair)
            sums = contract(x_part, both[...], 0, 0).astype(BF)
            grad_g[cols, :] = sums[:, :ff]
            grad_u[cols, :] = sums[:, ff:]
            twin_copy(1, b).start()
            twin_copy(2, b).start()

    wide = min(WIDE, width)

    def down_units(lo, hi):
        per = width // wide

        @pl.loop(lo * per, hi * per)
        def _(j):
            units = pl.ds(pl.multiple_of(lax.div(j, per) * ftile, ftile), ftile)
            cols = pl.ds(pl.multiple_of(lax.rem(j, per) * wide, wide), wide)
            grad_d[units, cols] = contract(
                hid[:, units], y_recv[:, :, :, cols].reshape(slots, wide), 0, 0
            ).astype(BF)

    def tokens_out():
        o_wait(0)
        o_wait(1)

        @pl.loop(0, nd)
        def _(j):
            cols = pl.ds(pl.multiple_of(j * dtile, dtile), dtile)
            back = o_recv[:, :, :, cols].reshape(slots, dtile)
            out_ref[:, cols] = (
                contract(hi[...], back, 0, 0) + contract(low[...], back, 0, 0)
            ).astype(BF)

    def tokens_dx(p):
        b_wait(p)

        @pl.loop(0, nd, unroll=2)
        def _(j):
            cols = pl.ds(pl.multiple_of(j * dtile, dtile), dtile)
            back = contract(
                pick[p * n_rows : (p + 1) * n_rows, :],
                b_recv[p, :, :, cols].reshape(n_rows, dtile),
                0,
                0,
            )
            if p == 0:
                dx_half[:, cols] = back
            else:
                dx_ref[:, cols] = (dx_half[:, cols] + back).astype(BF)

    cut1 = nf // 3

    first_products()
    x_of[1][1](0)
    hidden_units(0)
    output_rows(0)
    x_of[1][1](1)
    o_start(0)
    hidden_units(1)
    gate_up(0, 1)
    down_units(0, cut1)
    gate_up(1, 2)
    ring_step(1, 0)
    ring_step(2, 0)
    down_units(cut1, nf)

    @pl.loop(0, n_z)
    def _(k):
        twin_copy(0, ring_order(k)).start()

    gate_up(2, 3)
    ring_step(0, 0)
    output_rows(1)
    o_start(1)
    ring_step(1, 1)
    ring_step(2, 1)
    gate_up(3, min(5, n_z))
    ring_step(0, 1)
    input_rows(0, nd)
    b_start(0)
    b_start(1)
    if half > 2:
        ring_step(1, 2)
    if n_z > 5:
        gate_up(5, n_z)
    if half > 2:
        ring_step(2, 2)
        ring_step(0, 2)
    for s in range(3, half):
        for i in (1, 2, 0):
            ring_step(i, s)
    tokens_out()
    tokens_dx(0)
    tokens_dx(1)
    for i in (1, 2, 0):
        ring_last(i)

    for done in (
        meta_done,
        v_done,
        seqs_of[0][2],
        seqs_of[1][2],
        x_of[0][2],
        x_of[1][2],
        y_done,
        o_done,
        b_done,
    ):
        done()

    for i in range(3):
        grad, twin, _, _ = grads[i]
        part = twin.shape[1]
        for sem, count in ((twin_ss, n_z), (ring_ss, n_z - 1)):
            rows_sent = pl.ds(0, count * part)
            pltpu.make_async_remote_copy(
                src_ref=grad.at[rows_sent],
                dst_ref=grad.at[rows_sent],
                send_sem=sem.at[i],
                recv_sem=sem.at[i],
                device_id={"dp": g + 1 - 2 * core},
                device_id_type=MESH,
            ).wait_send()


def settle_kernel(*refs):
    n = (len(refs) - 1) // 2
    copies = [pltpu.make_async_copy(refs[i], refs[n + i], refs[2 * n].at[i]) for i in range(n)]
    for copy in copies:
        copy.start()
    for copy in copies:
        copy.wait()


def settle(arrays):
    n = len(arrays)
    return pl.pallas_call(
        settle_kernel,
        out_shape=[jax.ShapeDtypeStruct(a.shape, a.dtype) for a in arrays],
        in_specs=[pl.BlockSpec(memory_space=pltpu.VMEM)] * n,
        out_specs=[pl.BlockSpec(memory_space=pl.ANY)] * n,
        scratch_shapes=[pltpu.SemaphoreType.DMA((n,))],
        compiler_params=pltpu.CompilerParams(vmem_limit_bytes=4 * 1024 * 1024),
    )(*[pltpu.with_memory_space_constraint(a, pltpu.VMEM) for a in arrays])


def on_device(
    n_dp,
    n_ex,
    gen_rows,
    gen_lengths,
    gen_adv,
    destination,
    expert_ids,
    gate_values,
    cotangent,
    w_gate,
    w_up,
    w_down,
):
    rows, width = gen_rows.shape
    seqs = destination.shape[2]
    slot = rows // seqs
    ff = w_gate.shape[2]
    cap = 2 * rows * expert_ids.shape[1] // n_ex
    slots = n_ex * cap
    n_z = n_dp // 2
    lanes = max(cap, 128)
    vmem = pl.BlockSpec(memory_space=pltpu.VMEM)
    hbm = pl.BlockSpec(memory_space=pl.ANY)
    dma = pltpu.SemaphoreType.DMA
    part, part_d = width // n_dp, ff // n_dp
    buffers = [pltpu.VMEM((2, n_ex, cap // 2, width), BF)] * 8
    ring = [
        pltpu.VMEM((2, n_z // 2, p, c), BF) for p, c in ((part, ff), (part, ff), (part_d, width))
    ]
    twin = [pltpu.VMEM((n_z, p, c), BF) for p, c in ((part, ff), (part, ff), (part_d, width))]
    outs = pl.pallas_call(
        functools.partial(step_kernel, n_dp, n_ex, slot, cap),
        out_shape=(
            pltpu.VMEM((rows, width), BF),
            pltpu.VMEM((rows, width), BF),
            pltpu.VMEM((part, ff), BF),
            pltpu.VMEM((part, ff), BF),
            pltpu.VMEM((part_d, width), BF),
        ),
        in_specs=[vmem] * 5 + [hbm] * 5,
        out_specs=[vmem] * 5,
        scratch_shapes=[
            pltpu.VMEM((rows, width), BF),
            pltpu.VMEM((rows, width), BF),
            pltpu.VMEM((width, ff), BF),
            pltpu.VMEM((width, ff), BF),
            pltpu.VMEM((ff, width), BF),
            pltpu.VMEM((n_dp, 8, 128), F32),
            pltpu.VMEM((n_dp, 8, 128), F32),
            pltpu.VMEM((1, n_ex, 8, lanes), F32),
            pltpu.VMEM((1, n_ex, 8, lanes), F32),
            pltpu.VMEM((2, n_dp, slot, width // 2), BF),
            pltpu.VMEM((2, n_dp, slot, width // 2), BF),
            *buffers,
            pltpu.VMEM((slots, rows), BF),
            pltpu.VMEM((slots, rows), BF),
            pltpu.VMEM((slots, rows), BF),
            pltpu.VMEM((rows, width), F32),
            pltpu.VMEM((slots, ff), F32),
            pltpu.VMEM((slots, ff), F32),
            pltpu.VMEM((slots, ff), F32),
            pltpu.VMEM((slots, ff), BF),
            pltpu.VMEM((slots, 2 * ff), BF),
            pltpu.VMEM((width, ff), BF),
            pltpu.VMEM((width, ff), BF),
            pltpu.VMEM((ff, width), BF),
            *twin,
            *ring,
            dma((5,)),
            dma((3,)),
            dma((1, 3)),
            dma((2, 3)),
            dma((2, 2, 3)),
            *([dma((2, 3))] * 3),
            dma((3,)),
            dma((3, n_z)),
            dma((3,)),
            dma((3, 2, n_z // 2)),
        ],
        compiler_params=pltpu.CompilerParams(
            collective_id=0, has_side_effects=True, vmem_limit_bytes=62 * 1024 * 1024
        ),
    )(
        destination[0],
        gen_lengths[0],
        gen_adv[0],
        expert_ids.T,
        gate_values.T,
        gen_rows,
        cotangent,
        w_gate[0],
        w_up[0],
        w_down[0],
    )
    outs = settle(outs)
    return outs[0], outs[1], outs[2][None], outs[3][None], outs[4][None]


def solution(mesh):
    n_dp, n_ex = mesh.shape["dp"], mesh.shape["expert"]
    in_specs = (
        P(("dp", "expert"), None),
        P("dp", "expert", None),
        P("dp", "expert", None),
        P("dp", "expert", None),
        P(("dp", "expert"), None),
        P(("dp", "expert"), None),
        P(("dp", "expert"), None),
        P("expert", None, None),
        P("expert", None, None),
        P("expert", None, None),
    )
    out_specs = (
        P(("dp", "expert"), None),
        P(("dp", "expert"), None),
        P("expert", "dp", None),
        P("expert", "dp", None),
        P("expert", "dp", None),
    )
    return jax.shard_map(
        functools.partial(on_device, n_dp, n_ex),
        mesh=mesh,
        in_specs=in_specs,
        out_specs=out_specs,
        check_vma=False,
    )
```

```python
import functools

import jax
import jax.numpy as jnp
from jax import lax
from jax.experimental import pallas as pl
from jax.experimental.pallas import tpu as pltpu
from jax.sharding import PartitionSpec as P

MESH = pl.DeviceIdType.MESH
BF = jnp.bfloat16
F32 = jnp.float32
WIDE = 1024


def contract(left, right, left_dim, right_dim):
    return lax.dot_general(
        left, right, (((left_dim,), (right_dim,)), ((), ())), preferred_element_type=F32
    )


def iota(shape, dim):
    return lax.broadcasted_iota(jnp.int32, shape, dim)


def step_kernel(
    n_dp,
    n_ex,
    slot,
    cap,
    dest_ref,
    len_ref,
    adv_ref,
    ids_ref,
    gate_ref,
    gen_hbm,
    cot_hbm,
    wg_hbm,
    wu_hbm,
    wd_hbm,
    out_ref,
    dx_ref,
    gg_out,
    gu_out,
    gd_out,
    gen_ref,
    cot_ref,
    wg,
    wu,
    wd,
    meta_send,
    meta_recv,
    scale_send,
    scale_recv,
    seq_send,
    seq_recv,
    x_send,
    x_recv,
    y_send,
    y_recv,
    o_send,
    o_recv,
    b_send,
    b_recv,
    pick,
    hi,
    low,
    dx_half,
    gate_part,
    up_part,
    hidden_grad,
    hid,
    both,
    grad_g,
    grad_u,
    grad_d,
    twin_g,
    twin_u,
    twin_d,
    ring_g,
    ring_u,
    ring_d,
    w_sem,
    meta_sem,
    scale_sem,
    seq_sem,
    x_sem,
    y_sem,
    o_sem,
    b_sem,
    twin_ss,
    twin_rs,
    ring_ss,
    ring_rs,
):
    g = lax.axis_index("dp")
    e = lax.axis_index("expert")
    core = lax.rem(g, 2)
    z = lax.div(g, 2)
    n_z = n_dp // 2
    half = n_z // 2
    rows = gen_ref.shape[0]
    width = gen_ref.shape[1]
    ff = wg.shape[1]
    mid = width // 2
    slots = n_ex * cap
    hc = cap // 2
    lanes = max(cap, 128)
    dtile = min(256, width)
    ftile = min(256, ff)
    nd, nf = width // dtile, ff // ftile

    nx = 1
    while (nx * 2) * (nx * 2) <= n_ex:
        nx *= 2
    ny = n_ex // nx
    ex, ey = lax.rem(e, nx), lax.div(e, nx)

    def far(d, n):
        return min(d, n - d)

    tokens = sorted(
        ((dy, dx) for dy in range(ny) for dx in range(nx)),
        key=lambda d: -(far(d[0], ny) + far(d[1], nx)),
    )
    trainers = sorted(
        ((dz, dc) for dz in range(n_z) for dc in range(2)), key=lambda d: -(far(d[0], n_z) + d[1])
    )

    def expert_to(i, sign=1):
        dy, dx = tokens[i]
        return lax.rem(ey + sign * dy + ny, ny) * nx + lax.rem(ex + sign * dx + nx, nx)

    def trainer_to(i):
        dz, dc = trainers[i]
        return lax.rem(z + dz, n_z) * 2 + lax.rem(core + dc, 2)

    loads = [
        pltpu.make_async_copy(src, dst, w_sem.at[i])
        for i, (src, dst) in enumerate(
            ((cot_hbm, cot_ref), (gen_hbm, gen_ref), (wg_hbm, wg), (wu_hbm, wu), (wd_hbm, wd))
        )
    ]
    for copy in loads:
        copy.start()

    barrier = pltpu.get_barrier_semaphore()

    for i in range(max(n_dp, n_ex) - 1):
        if i < n_dp - 1:
            pl.semaphore_signal(
                barrier, 1, device_id={"dp": trainer_to(i)}, device_id_type=MESH
            )
        if i < n_ex - 1:
            pl.semaphore_signal(
                barrier, 1, device_id={"expert": expert_to(i)}, device_id_type=MESH
            )

    def dp_exchange(send, recv, sems):
        def copy(src, dst, peer):
            return pltpu.make_async_remote_copy(
                src_ref=src,
                dst_ref=dst,
                send_sem=sems.at[0],
                recv_sem=sems.at[1],
                device_id={"dp": peer},
                device_id_type=MESH,
            )

        own = pltpu.make_async_copy(send.at[g], recv.at[g], sems.at[2])
        others = pl.ds(0, n_dp - 1)
        every = copy(send.at[others], recv.at[others], trainer_to(0))

        def start():
            for i in range(n_dp - 1):
                peer = trainer_to(i)
                copy(send.at[peer], recv.at[g], peer).start()
            own.start()

        def wait_recv():
            own.wait()
            every.wait_recv()

        return start, wait_recv, every.wait_send

    def token_exchange(sign, send, recv, sems):
        def copy(p, i):
            return pltpu.make_async_remote_copy(
                src_ref=send.at[p, i],
                dst_ref=recv.at[p, i],
                send_sem=sems.at[p, 0],
                recv_sem=sems.at[p, 1],
                device_id={"expert": expert_to(0 if isinstance(i, pl.Slice) else i, sign)},
                device_id_type=MESH,
            )

        last = n_ex - 1

        def own(p):
            return pltpu.make_async_copy(send.at[p, last], recv.at[p, last], sems.at[p, 2])

        def start(p):
            for i in range(last):
                copy(p, i).start()
            own(p).start()

        def wait_recv(p):
            own(p).wait()
            copy(p, pl.ds(0, last)).wait_recv()

        def wait_send():
            for p in range(sems.shape[0]):
                copy(p, pl.ds(0, last)).wait_send()

        return start, wait_recv, wait_send

    meta_start, meta_wait, meta_done = dp_exchange(meta_send, meta_recv, meta_sem)
    seqs_of = [dp_exchange(seq_send.at[h], seq_recv.at[h], seq_sem.at[h]) for h in range(2)]
    halves = [pl.ds(h * mid, mid) for h in range(2)]
    x_of = [
        token_exchange(
            1,
            x_send.at[:, :, :, halves[h]],
            x_recv.at[:, :, :, halves[h]],
            x_sem.at[h],
        )
        for h in range(2)
    ]
    y_start, y_wait, y_done = token_exchange(1, y_send, y_recv, y_sem)
    v_start, v_wait, v_done = token_exchange(1, scale_send, scale_recv, scale_sem)
    o_start, o_wait, o_done = token_exchange(-1, o_send, o_recv, o_sem)
    b_start, b_wait, b_done = token_exchange(-1, b_send, b_recv, b_sem)

    names = jnp.zeros((n_ex, rows), jnp.int32)
    for i in range(n_ex):
        names = jnp.where(iota((n_ex, rows), 0) == i, expert_to(i), names)
    hit0, hit1 = ids_ref[0:1, :] == names, ids_ref[1:2, :] == names
    routed = hit0 | hit1
    gate_of = jnp.where(hit0, gate_ref[0:1, :], 0.0) + jnp.where(hit1, gate_ref[1:2, :], 0.0)
    before = (iota((rows, rows), 0) < iota((rows, rows), 1)).astype(BF)
    pos = jnp.dot(routed.astype(BF), before, preferred_element_type=F32)
    code = jnp.where(routed, pos, -1.0)
    place = iota((2, n_ex, hc, rows), 0) * hc + iota((2, n_ex, hc, rows), 2)
    hit = code[None, :, None, :] == place.astype(F32)
    picked = hit.astype(BF).reshape(slots, rows)
    pick[...] = picked
    weighted = jnp.where(hit, gate_of[None, :, None, :], 0.0).reshape(slots, rows)
    whole = weighted.astype(BF)
    hi[...] = whole
    low[...] = (weighted - whole.astype(F32)).astype(BF)

    n_rows = n_ex * hc

    def fill_y(p):
        @pl.loop(0, nd, unroll=4)
        def _(j):
            cols = pl.ds(pl.multiple_of(j * dtile, dtile), dtile)
            y_send[p, :, :, cols] = (
                jnp.dot(
                    pick[p * n_rows : (p + 1) * n_rows, :],
                    cot_ref[:, cols],
                    preferred_element_type=F32,
                )
                .astype(BF)
                .reshape(n_ex, hc, dtile)
            )

    loads[0].wait()
    fill_y(0)
    pl.semaphore_wait(barrier, n_dp + n_ex - 2)
    y_start(0)

    shift = slot.bit_length() - 1
    seqs = dest_ref.shape[1]
    srow, scol = iota((n_dp * slot, rows), 0), iota((n_dp * slot, rows), 1)
    same_place = (srow & (slot - 1)) == (scol & (slot - 1))
    mine = dest_ref[...] == iota((n_dp, seqs), 0)
    len_to = jnp.sum(jnp.where(mine, len_ref[...].astype(F32), 0.0), axis=1, keepdims=True)
    adv_to = jnp.sum(jnp.where(mine, adv_ref[...].astype(F32), 0.0), axis=1, keepdims=True)
    line = iota((n_dp, 8, 128), 1)
    meta_send[...] = jnp.where(line == 0, len_to[:, :, None], adv_to[:, :, None])
    seq_lanes = ((iota((seqs, rows), 1) >> shift) == iota((seqs, rows), 0)).astype(F32)
    mine_lanes = jnp.dot(mine.astype(F32), seq_lanes, preferred_element_type=F32)
    spread = jnp.broadcast_to(mine_lanes[:, None, :], (n_dp, slot, rows)).reshape(n_dp * slot, rows)
    spread = jnp.where(same_place, spread, 0.0).astype(BF)
    meta_start()
    loads[1].wait()

    for h in range(2):

        @pl.loop(0, nd // 2)
        def _(j):
            cols = pl.ds(pl.multiple_of(j * dtile, dtile), dtile)
            from_cols = pl.ds(pl.multiple_of(h * mid + j * dtile, dtile), dtile)
            seq_send[h, :, :, cols] = (
                jnp.dot(spread, gen_ref[:, from_cols], preferred_element_type=F32)
                .astype(BF)
                .reshape(n_dp, slot, dtile)
            )

        seqs_of[h][0]()

    fill_y(1)
    y_start(1)
    meta_wait()

    got_len = meta_recv[:, 0, :]
    got_adv = meta_recv[:, 1, :]
    alive = (got_len > 0.0).astype(BF)
    lower = (iota((n_dp, n_dp), 1) < iota((n_dp, n_dp), 0)).astype(BF)
    arrival = jnp.dot(lower, alive, preferred_element_type=F32)
    arrival = jnp.where(got_len > 0.0, arrival, -1.0)
    per_len = got_adv / jnp.maximum(got_len, 1.0)

    def widen(v):
        return jnp.broadcast_to(v[:, None, :rows], (n_dp, slot, rows)).reshape(n_dp * slot, rows)

    placed = (widen(arrival) == (scol >> shift).astype(F32)) & same_place
    within = (srow & (slot - 1)).astype(F32) < widen(got_len)
    tok_scale = jnp.sum(
        jnp.where(placed & within, widen(per_len), 0.0), axis=0, keepdims=True
    )
    row_scale = jnp.sum(
        jnp.where(hit, (gate_of * tok_scale)[None, :, None, :], 0.0), axis=3, keepdims=True
    )
    lane_of = iota((2, n_ex, hc, lanes), 0) * hc + iota((2, n_ex, hc, lanes), 2)
    on_lane = lane_of == iota((2, n_ex, hc, lanes), 3)
    spread_scale = jnp.where(on_lane, row_scale, 0.0)
    spread_scale = jnp.sum(spread_scale[0] + spread_scale[1], axis=1, keepdims=True)
    scale_send[0] = jnp.broadcast_to(spread_scale, (n_ex, 8, lanes))
    v_start(0)
    fetch = contract(picked, placed.astype(BF), 1, 1).astype(BF)
    def fill_x(h, p):
        here = slice(p * n_rows, (p + 1) * n_rows)

        @pl.loop(0, nd // 2, unroll=2)
        def _(j):
            cols = pl.ds(pl.multiple_of(j * dtile, dtile), dtile)
            to_cols = pl.ds(pl.multiple_of(h * mid + j * dtile, dtile), dtile)
            source = seq_recv[h, :, :, cols].reshape(n_dp * slot, dtile)
            x_send[p, :, :, to_cols] = (
                jnp.dot(fetch[here, :], source, preferred_element_type=F32)
                .astype(BF)
                .reshape(n_ex, hc, dtile)
            )

        x_of[h][0](p)

    for h in range(2):
        seqs_of[h][1]()
        fill_x(h, 0)
        fill_x(h, 1)

    y_wait(0)
    y_wait(1)
    v_wait(0)
    scale = jnp.sum(
        jnp.where(on_lane, scale_recv[:, :, 0:1, :], 0.0), axis=3, keepdims=True
    ).reshape(slots, 1)

    @pl.loop(0, nd)
    def _(j):
        cols = pl.ds(pl.multiple_of(j * dtile, dtile), dtile)
        y_recv[:, :, :, cols] = (
            (y_recv[:, :, :, cols].reshape(slots, dtile).astype(F32) * scale)
            .astype(BF)
            .reshape(2, n_ex, hc, dtile)
        )

    for copy in loads[2:]:
        copy.wait()

    @pl.loop(0, nf)
    def _(j):
        cols = pl.ds(pl.multiple_of(j * ftile, ftile), ftile)
        hidden_grad[:, cols] = contract(y_recv[...].reshape(slots, width), wd[cols, :], 1, 1)

    def first_products():
        x_of[0][1](0)
        x_of[0][1](1)

        @pl.loop(0, nf, unroll=True)
        def _(j):
            cols = pl.ds(pl.multiple_of(j * ftile, ftile), ftile)
            x_some = x_recv[:, :, :, :mid].reshape(slots, mid)
            gate_part[:, cols] = jnp.dot(x_some, wg[:mid, cols], preferred_element_type=F32)
            up_part[:, cols] = jnp.dot(x_some, wu[:mid, cols], preferred_element_type=F32)

    def hidden_units(p):
        here = pl.ds(p * n_rows, n_rows)

        @pl.loop(0, nf, unroll=True)
        def _(j):
            cols = pl.ds(pl.multiple_of(j * ftile, ftile), ftile)
            x_some = x_recv[p, :, :, mid:].reshape(n_rows, mid)
            gate_pre = gate_part[here, cols] + jnp.dot(
                x_some, wg[mid:, cols], preferred_element_type=F32
            )
            up_pre = up_part[here, cols] + jnp.dot(
                x_some, wu[mid:, cols], preferred_element_type=F32
            )
            sig = jax.nn.sigmoid(gate_pre)
            act = gate_pre * sig
            hid[here, cols] = (act * up_pre).astype(BF)
            down = hidden_grad[here, cols]
            both[here, cols] = (
                down * up_pre * sig * (1.0 + gate_pre * (1.0 - sig))
            ).astype(BF)
            ups = pl.ds(pl.multiple_of(ff + j * ftile, ftile), ftile)
            both[here, ups] = (down * act).astype(BF)

    def output_rows(p):
        here = pl.ds(p * n_rows, n_rows)

        @pl.loop(0, nd, unroll=4)
        def _(j):
            cols = pl.ds(pl.multiple_of(j * dtile, dtile), dtile)
            o_send[p, :, :, cols] = (
                jnp.dot(hid[here, :], wd[:, cols], preferred_element_type=F32)
                .astype(BF)
                .reshape(n_ex, hc, dtile)
            )

    def input_rows(lo, hi):
        @pl.loop(lo, hi, unroll=2)
        def _(j):
            cols = pl.ds(pl.multiple_of(j * dtile, dtile), dtile)
            b_send[:, :, :, cols] = (
                (
                    contract(both[:, :ff], wg[cols, :], 1, 1)
                    + contract(both[:, ff:], wu[cols, :], 1, 1)
                )
                .astype(BF)
                .reshape(2, n_ex, hc, dtile)
            )

    grads = ((grad_d, twin_d, ring_d, gd_out), (grad_g, twin_g, ring_g, gg_out), (grad_u, twin_u, ring_u, gu_out))

    def block(i, b, c):
        part = grads[i][1].shape[1]
        return pl.ds(pl.multiple_of((b * 2 + c) * part, part), part)

    def twin_copy(i, b):
        return pltpu.make_async_remote_copy(
            src_ref=grads[i][0].at[block(i, b, 1 - core)],
            dst_ref=grads[i][1].at[b],
            send_sem=twin_ss.at[i],
            recv_sem=twin_rs.at[i, b],
            device_id={"dp": g + 1 - 2 * core},
            device_id_type=MESH,
        )

    def ring_copy(i, way, s):
        grad, _, ring, _ = grads[i]
        mid = grad.shape[1] // 2
        if s == 0:
            b = lax.rem(z + half, n_z)
            cols = pl.ds(way * mid, mid)
        else:
            b = lax.rem(z + (half - s) * (1 - 2 * way) + n_z, n_z)
            cols = pl.ds(0, 2 * mid)
        return pltpu.make_async_remote_copy(
            src_ref=grad.at[block(i, b, core), cols],
            dst_ref=ring.at[way, s, :, cols],
            send_sem=ring_ss.at[i],
            recv_sem=ring_rs.at[i, way, s],
            device_id={"dp": lax.rem(g + 2 * (1 - 2 * way) + n_dp, n_dp)},
            device_id_type=MESH,
        )

    def ring_step(i, s):
        grad, twin, ring, _ = grads[i]
        mid = grad.shape[1] // 2
        if s == 0:
            b = lax.rem(z + half, n_z)
            here = block(i, b, core)
            twin_copy(i, b).wait_recv()
            grad[here, :] = (grad[here, :].astype(F32) + twin[b].astype(F32)).astype(BF)
            ring_copy(i, 0, 0).start()
            ring_copy(i, 1, 0).start()
            return
        for way in range(2):
            b = lax.rem(z + (half - s) * (1 - 2 * way) + n_z, n_z)
            here = block(i, b, core)
            twin_copy(i, b).wait_recv()
            ring_copy(i, way, s - 1).wait_recv()
            if s == 1:
                near, far = pl.ds(way * mid, mid), pl.ds((1 - way) * mid, mid)
                grad[here, near] = (
                    grad[here, near].astype(F32)
                    + twin[b, :, near].astype(F32)
                    + ring[way, 0, :, near].astype(F32)
                ).astype(BF)
                grad[here, far] = (
                    grad[here, far].astype(F32) + twin[b, :, far].astype(F32)
                ).astype(BF)
            else:
                grad[here, :] = (
                    grad[here, :].astype(F32)
                    + twin[b].astype(F32)
                    + ring[way, s - 1].astype(F32)
                ).astype(BF)
            ring_copy(i, way, s).start()

    def ring_last(i):
        grad, twin, ring, out = grads[i]
        twin_copy(i, z).wait_recv()
        ring_copy(i, 0, half - 1).wait_recv()
        ring_copy(i, 1, half - 1).wait_recv()
        here = block(i, z, core)
        out[...] = (
            grad[here, :].astype(F32)
            + twin[z].astype(F32)
            + ring[0, half - 1].astype(F32)
            + ring[1, half - 1].astype(F32)
        ).astype(BF)

    pair = width // n_z

    def ring_order(k):
        d = half - lax.div(k + 1, 2)
        way = 2 * lax.rem(k, 2) - 1
        return lax.rem(z + way * d + n_z, n_z)

    def gate_up(lo, hi):
        @pl.loop(lo, hi)
        def _(k):
            b = ring_order(k)
            cols = pl.ds(pl.multiple_of(b * pair, pair), pair)
            x_part = x_recv[:, :, :, cols].reshape(slots, pair)
            sums = contract(x_part, both[...], 0, 0).astype(BF)
            grad_g[cols, :] = sums[:, :ff]
            grad_u[cols, :] = sums[:, ff:]
            twin_copy(1, b).start()
            twin_copy(2, b).start()

    wide = min(WIDE, width)

    def down_units(lo, hi):
        per = width // wide

        @pl.loop(lo * per, hi * per)
        def _(j):
            units = pl.ds(pl.multiple_of(lax.div(j, per) * ftile, ftile), ftile)
            cols = pl.ds(pl.multiple_of(lax.rem(j, per) * wide, wide), wide)
            grad_d[units, cols] = contract(
                hid[:, units], y_recv[:, :, :, cols].reshape(slots, wide), 0, 0
            ).astype(BF)

    def tokens_out():
        o_wait(0)
        o_wait(1)

        @pl.loop(0, nd, unroll=2)
        def _(j):
            cols = pl.ds(pl.multiple_of(j * dtile, dtile), dtile)
            back = o_recv[:, :, :, cols].reshape(slots, dtile)
            out_ref[:, cols] = (
                contract(hi[...], back, 0, 0) + contract(low[...], back, 0, 0)
            ).astype(BF)

    def tokens_dx(p):
        b_wait(p)

        @pl.loop(0, nd, unroll=2)
        def _(j):
            cols = pl.ds(pl.multiple_of(j * dtile, dtile), dtile)
            back = contract(
                pick[p * n_rows : (p + 1) * n_rows, :],
                b_recv[p, :, :, cols].reshape(n_rows, dtile),
                0,
                0,
            )
            if p == 0:
                dx_half[:, cols] = back
            else:
                dx_ref[:, cols] = (dx_half[:, cols] + back).astype(BF)

    cut1 = nf // 3

    first_products()
    x_of[1][1](0)
    hidden_units(0)
    output_rows(0)
    x_of[1][1](1)
    o_start(0)
    hidden_units(1)
    gate_up(0, 1)
    down_units(0, cut1)
    gate_up(1, 2)
    ring_step(1, 0)
    ring_step(2, 0)
    down_units(cut1, nf)

    @pl.loop(0, n_z)
    def _(k):
        twin_copy(0, ring_order(k)).start()

    gate_up(2, 3)
    ring_step(0, 0)
    output_rows(1)
    o_start(1)
    ring_step(1, 1)
    ring_step(2, 1)
    gate_up(3, min(5, n_z))
    ring_step(0, 1)
    input_rows(0, nd)
    b_start(0)
    b_start(1)
    if half > 2:
        ring_step(1, 2)
    if n_z > 5:
        gate_up(5, n_z)
    if half > 2:
        ring_step(2, 2)
        ring_step(0, 2)
    for s in range(3, half):
        for i in (1, 2, 0):
            ring_step(i, s)
    tokens_out()
    tokens_dx(0)
    tokens_dx(1)
    for i in (1, 2, 0):
        ring_last(i)

    for done in (
        meta_done,
        v_done,
        seqs_of[0][2],
        seqs_of[1][2],
        x_of[0][2],
        x_of[1][2],
        y_done,
        o_done,
        b_done,
    ):
        done()

    for i in range(3):
        grad, twin, _, _ = grads[i]
        part = twin.shape[1]
        for sem, count in ((twin_ss, n_z), (ring_ss, n_z - 1)):
            rows_sent = pl.ds(0, count * part)
            pltpu.make_async_remote_copy(
                src_ref=grad.at[rows_sent],
                dst_ref=grad.at[rows_sent],
                send_sem=sem.at[i],
                recv_sem=sem.at[i],
                device_id={"dp": g + 1 - 2 * core},
                device_id_type=MESH,
            ).wait_send()


def settle_kernel(*refs):
    n = (len(refs) - 1) // 2
    copies = [pltpu.make_async_copy(refs[i], refs[n + i], refs[2 * n].at[i]) for i in range(n)]
    for copy in copies:
        copy.start()
    for copy in copies:
        copy.wait()


def settle(arrays):
    n = len(arrays)
    return pl.pallas_call(
        settle_kernel,
        out_shape=[jax.ShapeDtypeStruct(a.shape, a.dtype) for a in arrays],
        in_specs=[pl.BlockSpec(memory_space=pltpu.VMEM)] * n,
        out_specs=[pl.BlockSpec(memory_space=pl.ANY)] * n,
        scratch_shapes=[pltpu.SemaphoreType.DMA((n,))],
        compiler_params=pltpu.CompilerParams(vmem_limit_bytes=4 * 1024 * 1024),
    )(*[pltpu.with_memory_space_constraint(a, pltpu.VMEM) for a in arrays])


def on_device(
    n_dp,
    n_ex,
    gen_rows,
    gen_lengths,
    gen_adv,
    destination,
    expert_ids,
    gate_values,
    cotangent,
    w_gate,
    w_up,
    w_down,
):
    rows, width = gen_rows.shape
    seqs = destination.shape[2]
    slot = rows // seqs
    ff = w_gate.shape[2]
    cap = 2 * rows * expert_ids.shape[1] // n_ex
    slots = n_ex * cap
    n_z = n_dp // 2
    lanes = max(cap, 128)
    vmem = pl.BlockSpec(memory_space=pltpu.VMEM)
    hbm = pl.BlockSpec(memory_space=pl.ANY)
    dma = pltpu.SemaphoreType.DMA
    part, part_d = width // n_dp, ff // n_dp
    buffers = [pltpu.VMEM((2, n_ex, cap // 2, width), BF)] * 8
    ring = [
        pltpu.VMEM((2, n_z // 2, p, c), BF) for p, c in ((part, ff), (part, ff), (part_d, width))
    ]
    twin = [pltpu.VMEM((n_z, p, c), BF) for p, c in ((part, ff), (part, ff), (part_d, width))]
    outs = pl.pallas_call(
        functools.partial(step_kernel, n_dp, n_ex, slot, cap),
        out_shape=(
            pltpu.VMEM((rows, width), BF),
            pltpu.VMEM((rows, width), BF),
            pltpu.VMEM((part, ff), BF),
            pltpu.VMEM((part, ff), BF),
            pltpu.VMEM((part_d, width), BF),
        ),
        in_specs=[vmem] * 5 + [hbm] * 5,
        out_specs=[vmem] * 5,
        scratch_shapes=[
            pltpu.VMEM((rows, width), BF),
            pltpu.VMEM((rows, width), BF),
            pltpu.VMEM((width, ff), BF),
            pltpu.VMEM((width, ff), BF),
            pltpu.VMEM((ff, width), BF),
            pltpu.VMEM((n_dp, 8, 128), F32),
            pltpu.VMEM((n_dp, 8, 128), F32),
            pltpu.VMEM((1, n_ex, 8, lanes), F32),
            pltpu.VMEM((1, n_ex, 8, lanes), F32),
            pltpu.VMEM((2, n_dp, slot, width // 2), BF),
            pltpu.VMEM((2, n_dp, slot, width // 2), BF),
            *buffers,
            pltpu.VMEM((slots, rows), BF),
            pltpu.VMEM((slots, rows), BF),
            pltpu.VMEM((slots, rows), BF),
            pltpu.VMEM((rows, width), F32),
            pltpu.VMEM((slots, ff), F32),
            pltpu.VMEM((slots, ff), F32),
            pltpu.VMEM((slots, ff), F32),
            pltpu.VMEM((slots, ff), BF),
            pltpu.VMEM((slots, 2 * ff), BF),
            pltpu.VMEM((width, ff), BF),
            pltpu.VMEM((width, ff), BF),
            pltpu.VMEM((ff, width), BF),
            *twin,
            *ring,
            dma((5,)),
            dma((3,)),
            dma((1, 3)),
            dma((2, 3)),
            dma((2, 2, 3)),
            *([dma((2, 3))] * 3),
            dma((3,)),
            dma((3, n_z)),
            dma((3,)),
            dma((3, 2, n_z // 2)),
        ],
        compiler_params=pltpu.CompilerParams(
            collective_id=0, has_side_effects=True, vmem_limit_bytes=62 * 1024 * 1024
        ),
    )(
        destination[0],
        gen_lengths[0],
        gen_adv[0],
        expert_ids.T,
        gate_values.T,
        gen_rows,
        cotangent,
        w_gate[0],
        w_up[0],
        w_down[0],
    )
    outs = settle(outs)
    return outs[0], outs[1], outs[2][None], outs[3][None], outs[4][None]


def solution(mesh):
    n_dp, n_ex = mesh.shape["dp"], mesh.shape["expert"]
    in_specs = (
        P(("dp", "expert"), None),
        P("dp", "expert", None),
        P("dp", "expert", None),
        P("dp", "expert", None),
        P(("dp", "expert"), None),
        P(("dp", "expert"), None),
        P(("dp", "expert"), None),
        P("expert", None, None),
        P("expert", None, None),
        P("expert", None, None),
    )
    out_specs = (
        P(("dp", "expert"), None),
        P(("dp", "expert"), None),
        P("expert", "dp", None),
        P("expert", "dp", None),
        P("expert", "dp", None),
    )
    return jax.shard_map(
        functools.partial(on_device, n_dp, n_ex),
        mesh=mesh,
        in_specs=in_specs,
        out_specs=out_specs,
        check_vma=False,
    )
```

```python
import functools

import jax
import jax.numpy as jnp
from jax import lax
from jax.experimental import pallas as pl
from jax.experimental.pallas import tpu as pltpu
from jax.sharding import PartitionSpec as P

MESH = pl.DeviceIdType.MESH
BF = jnp.bfloat16
F32 = jnp.float32
WIDE = 1024


def contract(left, right, left_dim, right_dim):
    return lax.dot_general(
        left, right, (((left_dim,), (right_dim,)), ((), ())), preferred_element_type=F32
    )


def iota(shape, dim):
    return lax.broadcasted_iota(jnp.int32, shape, dim)


def step_kernel(
    n_dp,
    n_ex,
    slot,
    cap,
    dest_ref,
    len_ref,
    adv_ref,
    ids_ref,
    gate_ref,
    gen_hbm,
    cot_hbm,
    wg_hbm,
    wu_hbm,
    wd_hbm,
    out_ref,
    dx_ref,
    gg_out,
    gu_out,
    gd_out,
    gen_ref,
    cot_ref,
    wg,
    wu,
    wd,
    meta_send,
    meta_recv,
    scale_send,
    scale_recv,
    seq_send,
    seq_recv,
    x_send,
    x_recv,
    y_send,
    y_recv,
    o_send,
    o_recv,
    b_send,
    b_recv,
    pick,
    hi,
    low,
    dx_half,
    gate_part,
    up_part,
    hidden_grad,
    hid,
    both,
    grad_g,
    grad_u,
    grad_d,
    twin_g,
    twin_u,
    twin_d,
    ring_g,
    ring_u,
    ring_d,
    w_sem,
    meta_sem,
    scale_sem,
    seq_sem,
    x_sem,
    y_sem,
    o_sem,
    b_sem,
    twin_ss,
    twin_rs,
    ring_ss,
    ring_rs,
):
    g = lax.axis_index("dp")
    e = lax.axis_index("expert")
    core = lax.rem(g, 2)
    z = lax.div(g, 2)
    n_z = n_dp // 2
    half = n_z // 2
    rows = gen_ref.shape[0]
    width = gen_ref.shape[1]
    ff = wg.shape[1]
    mid = width // 2
    slots = n_ex * cap
    hc = cap // 2
    lanes = max(cap, 128)
    dtile = min(256, width)
    ftile = min(256, ff)
    nd, nf = width // dtile, ff // ftile

    nx = 1
    while (nx * 2) * (nx * 2) <= n_ex:
        nx *= 2
    ny = n_ex // nx
    ex, ey = lax.rem(e, nx), lax.div(e, nx)

    def far(d, n):
        return min(d, n - d)

    tokens = sorted(
        ((dy, dx) for dy in range(ny) for dx in range(nx)),
        key=lambda d: -(far(d[0], ny) + far(d[1], nx)),
    )
    trainers = sorted(
        ((dz, dc) for dz in range(n_z) for dc in range(2)), key=lambda d: -(far(d[0], n_z) + d[1])
    )

    def expert_to(i, sign=1):
        dy, dx = tokens[i]
        return lax.rem(ey + sign * dy + ny, ny) * nx + lax.rem(ex + sign * dx + nx, nx)

    def trainer_to(i):
        dz, dc = trainers[i]
        return lax.rem(z + dz, n_z) * 2 + lax.rem(core + dc, 2)

    loads = [
        pltpu.make_async_copy(src, dst, w_sem.at[i])
        for i, (src, dst) in enumerate(
            ((cot_hbm, cot_ref), (gen_hbm, gen_ref), (wg_hbm, wg), (wu_hbm, wu), (wd_hbm, wd))
        )
    ]
    for copy in loads:
        copy.start()

    barrier = pltpu.get_barrier_semaphore()

    for i in range(max(n_dp, n_ex) - 1):
        if i < n_dp - 1:
            pl.semaphore_signal(
                barrier, 1, device_id={"dp": trainer_to(i)}, device_id_type=MESH
            )
        if i < n_ex - 1:
            pl.semaphore_signal(
                barrier, 1, device_id={"expert": expert_to(i)}, device_id_type=MESH
            )

    def dp_exchange(send, recv, sems):
        def copy(src, dst, peer):
            return pltpu.make_async_remote_copy(
                src_ref=src,
                dst_ref=dst,
                send_sem=sems.at[0],
                recv_sem=sems.at[1],
                device_id={"dp": peer},
                device_id_type=MESH,
            )

        own = pltpu.make_async_copy(send.at[g], recv.at[g], sems.at[2])
        others = pl.ds(0, n_dp - 1)
        every = copy(send.at[others], recv.at[others], trainer_to(0))

        def start():
            for i in range(n_dp - 1):
                peer = trainer_to(i)
                copy(send.at[peer], recv.at[g], peer).start()
            own.start()

        def wait_recv():
            own.wait()
            every.wait_recv()

        return start, wait_recv, every.wait_send

    def token_exchange(sign, send, recv, sems):
        def copy(p, i):
            return pltpu.make_async_remote_copy(
                src_ref=send.at[p, i],
                dst_ref=recv.at[p, i],
                send_sem=sems.at[p, 0],
                recv_sem=sems.at[p, 1],
                device_id={"expert": expert_to(0 if isinstance(i, pl.Slice) else i, sign)},
                device_id_type=MESH,
            )

        last = n_ex - 1

        def own(p):
            return pltpu.make_async_copy(send.at[p, last], recv.at[p, last], sems.at[p, 2])

        def start(p):
            for i in range(last):
                copy(p, i).start()
            own(p).start()

        def wait_recv(p):
            own(p).wait()
            copy(p, pl.ds(0, last)).wait_recv()

        def wait_send():
            for p in range(sems.shape[0]):
                copy(p, pl.ds(0, last)).wait_send()

        return start, wait_recv, wait_send

    meta_start, meta_wait, meta_done = dp_exchange(meta_send, meta_recv, meta_sem)
    seqs_of = [dp_exchange(seq_send.at[h], seq_recv.at[h], seq_sem.at[h]) for h in range(2)]
    halves = [pl.ds(h * mid, mid) for h in range(2)]
    x_of = [
        token_exchange(
            1,
            x_send.at[:, :, :, halves[h]],
            x_recv.at[:, :, :, halves[h]],
            x_sem.at[h],
        )
        for h in range(2)
    ]
    y_start, y_wait, y_done = token_exchange(1, y_send, y_recv, y_sem)
    v_start, v_wait, v_done = token_exchange(1, scale_send, scale_recv, scale_sem)
    o_start, o_wait, o_done = token_exchange(-1, o_send, o_recv, o_sem)
    b_start, b_wait, b_done = token_exchange(-1, b_send, b_recv, b_sem)

    names = jnp.zeros((n_ex, rows), jnp.int32)
    for i in range(n_ex):
        names = jnp.where(iota((n_ex, rows), 0) == i, expert_to(i), names)
    hit0, hit1 = ids_ref[0:1, :] == names, ids_ref[1:2, :] == names
    routed = hit0 | hit1
    gate_of = jnp.where(hit0, gate_ref[0:1, :], 0.0) + jnp.where(hit1, gate_ref[1:2, :], 0.0)
    before = (iota((rows, rows), 0) < iota((rows, rows), 1)).astype(BF)
    pos = jnp.dot(routed.astype(BF), before, preferred_element_type=F32)
    code = jnp.where(routed, pos, -1.0)
    place = iota((2, n_ex, hc, rows), 0) * hc + iota((2, n_ex, hc, rows), 2)
    hit = code[None, :, None, :] == place.astype(F32)
    picked = hit.astype(BF).reshape(slots, rows)
    pick[...] = picked
    weighted = jnp.where(hit, gate_of[None, :, None, :], 0.0).reshape(slots, rows)
    whole = weighted.astype(BF)
    hi[...] = whole
    low[...] = (weighted - whole.astype(F32)).astype(BF)

    n_rows = n_ex * hc

    def fill_y(p):
        @pl.loop(0, nd, unroll=4)
        def _(j):
            cols = pl.ds(pl.multiple_of(j * dtile, dtile), dtile)
            y_send[p, :, :, cols] = (
                jnp.dot(
                    pick[p * n_rows : (p + 1) * n_rows, :],
                    cot_ref[:, cols],
                    preferred_element_type=F32,
                )
                .astype(BF)
                .reshape(n_ex, hc, dtile)
            )

    loads[0].wait()
    fill_y(0)
    pl.semaphore_wait(barrier, n_dp + n_ex - 2)
    y_start(0)

    shift = slot.bit_length() - 1
    seqs = dest_ref.shape[1]
    srow, scol = iota((n_dp * slot, rows), 0), iota((n_dp * slot, rows), 1)
    same_place = (srow & (slot - 1)) == (scol & (slot - 1))
    mine = dest_ref[...] == iota((n_dp, seqs), 0)
    len_to = jnp.sum(jnp.where(mine, len_ref[...].astype(F32), 0.0), axis=1, keepdims=True)
    adv_to = jnp.sum(jnp.where(mine, adv_ref[...].astype(F32), 0.0), axis=1, keepdims=True)
    line = iota((n_dp, 8, 128), 1)
    meta_send[...] = jnp.where(line == 0, len_to[:, :, None], adv_to[:, :, None])
    seq_lanes = ((iota((seqs, rows), 1) >> shift) == iota((seqs, rows), 0)).astype(F32)
    mine_lanes = jnp.dot(mine.astype(F32), seq_lanes, preferred_element_type=F32)
    spread = jnp.broadcast_to(mine_lanes[:, None, :], (n_dp, slot, rows)).reshape(n_dp * slot, rows)
    spread = jnp.where(same_place, spread, 0.0).astype(BF)
    meta_start()
    loads[1].wait()

    for h in range(2):

        @pl.loop(0, nd // 2)
        def _(j):
            cols = pl.ds(pl.multiple_of(j * dtile, dtile), dtile)
            from_cols = pl.ds(pl.multiple_of(h * mid + j * dtile, dtile), dtile)
            seq_send[h, :, :, cols] = (
                jnp.dot(spread, gen_ref[:, from_cols], preferred_element_type=F32)
                .astype(BF)
                .reshape(n_dp, slot, dtile)
            )

        seqs_of[h][0]()

    fill_y(1)
    y_start(1)
    meta_wait()

    got_len = meta_recv[:, 0, :]
    got_adv = meta_recv[:, 1, :]
    alive = (got_len > 0.0).astype(BF)
    lower = (iota((n_dp, n_dp), 1) < iota((n_dp, n_dp), 0)).astype(BF)
    arrival = jnp.dot(lower, alive, preferred_element_type=F32)
    arrival = jnp.where(got_len > 0.0, arrival, -1.0)
    per_len = got_adv / jnp.maximum(got_len, 1.0)

    def widen(v):
        return jnp.broadcast_to(v[:, None, :rows], (n_dp, slot, rows)).reshape(n_dp * slot, rows)

    placed = (widen(arrival) == (scol >> shift).astype(F32)) & same_place
    within = (srow & (slot - 1)).astype(F32) < widen(got_len)
    tok_scale = jnp.sum(
        jnp.where(placed & within, widen(per_len), 0.0), axis=0, keepdims=True
    )
    row_scale = jnp.sum(
        jnp.where(hit, (gate_of * tok_scale)[None, :, None, :], 0.0), axis=3, keepdims=True
    )
    lane_of = iota((2, n_ex, hc, lanes), 0) * hc + iota((2, n_ex, hc, lanes), 2)
    on_lane = lane_of == iota((2, n_ex, hc, lanes), 3)
    spread_scale = jnp.where(on_lane, row_scale, 0.0)
    spread_scale = jnp.sum(spread_scale[0] + spread_scale[1], axis=1, keepdims=True)
    scale_send[0] = jnp.broadcast_to(spread_scale, (n_ex, 8, lanes))
    v_start(0)
    fetch = contract(picked, placed.astype(BF), 1, 1).astype(BF)
    def fill_x(h, p):
        here = slice(p * n_rows, (p + 1) * n_rows)

        @pl.loop(0, nd // 2, unroll=2)
        def _(j):
            cols = pl.ds(pl.multiple_of(j * dtile, dtile), dtile)
            to_cols = pl.ds(pl.multiple_of(h * mid + j * dtile, dtile), dtile)
            source = seq_recv[h, :, :, cols].reshape(n_dp * slot, dtile)
            x_send[p, :, :, to_cols] = (
                jnp.dot(fetch[here, :], source, preferred_element_type=F32)
                .astype(BF)
                .reshape(n_ex, hc, dtile)
            )

        x_of[h][0](p)

    for h in range(2):
        seqs_of[h][1]()
        fill_x(h, 0)
        fill_x(h, 1)

    y_wait(0)
    y_wait(1)
    v_wait(0)
    scale = jnp.sum(
        jnp.where(on_lane, scale_recv[:, :, 0:1, :], 0.0), axis=3, keepdims=True
    ).reshape(slots, 1)

    @pl.loop(0, nd)
    def _(j):
        cols = pl.ds(pl.multiple_of(j * dtile, dtile), dtile)
        y_recv[:, :, :, cols] = (
            (y_recv[:, :, :, cols].reshape(slots, dtile).astype(F32) * scale)
            .astype(BF)
            .reshape(2, n_ex, hc, dtile)
        )

    for copy in loads[2:]:
        copy.wait()

    @pl.loop(0, nf, unroll=True)
    def _(j):
        cols = pl.ds(pl.multiple_of(j * ftile, ftile), ftile)
        hidden_grad[:, cols] = contract(y_recv[...].reshape(slots, width), wd[cols, :], 1, 1)

    def first_products():
        x_of[0][1](0)
        x_of[0][1](1)

        @pl.loop(0, nf, unroll=True)
        def _(j):
            cols = pl.ds(pl.multiple_of(j * ftile, ftile), ftile)
            x_some = x_recv[:, :, :, :mid].reshape(slots, mid)
            gate_part[:, cols] = jnp.dot(x_some, wg[:mid, cols], preferred_element_type=F32)
            up_part[:, cols] = jnp.dot(x_some, wu[:mid, cols], preferred_element_type=F32)

    def hidden_units(p):
        here = pl.ds(p * n_rows, n_rows)

        @pl.loop(0, nf, unroll=True)
        def _(j):
            cols = pl.ds(pl.multiple_of(j * ftile, ftile), ftile)
            x_some = x_recv[p, :, :, mid:].reshape(n_rows, mid)
            gate_pre = gate_part[here, cols] + jnp.dot(
                x_some, wg[mid:, cols], preferred_element_type=F32
            )
            up_pre = up_part[here, cols] + jnp.dot(
                x_some, wu[mid:, cols], preferred_element_type=F32
            )
            sig = jax.nn.sigmoid(gate_pre)
            act = gate_pre * sig
            hid[here, cols] = (act * up_pre).astype(BF)
            down = hidden_grad[here, cols]
            both[here, cols] = (
                down * up_pre * sig * (1.0 + gate_pre * (1.0 - sig))
            ).astype(BF)
            ups = pl.ds(pl.multiple_of(ff + j * ftile, ftile), ftile)
            both[here, ups] = (down * act).astype(BF)

    def output_rows(p):
        here = pl.ds(p * n_rows, n_rows)

        @pl.loop(0, nd, unroll=4)
        def _(j):
            cols = pl.ds(pl.multiple_of(j * dtile, dtile), dtile)
            o_send[p, :, :, cols] = (
                jnp.dot(hid[here, :], wd[:, cols], preferred_element_type=F32)
                .astype(BF)
                .reshape(n_ex, hc, dtile)
            )

    def input_rows(lo, hi):
        @pl.loop(lo, hi, unroll=2)
        def _(j):
            cols = pl.ds(pl.multiple_of(j * dtile, dtile), dtile)
            b_send[:, :, :, cols] = (
                (
                    contract(both[:, :ff], wg[cols, :], 1, 1)
                    + contract(both[:, ff:], wu[cols, :], 1, 1)
                )
                .astype(BF)
                .reshape(2, n_ex, hc, dtile)
            )

    grads = ((grad_d, twin_d, ring_d, gd_out), (grad_g, twin_g, ring_g, gg_out), (grad_u, twin_u, ring_u, gu_out))

    def block(i, b, c):
        part = grads[i][1].shape[1]
        return pl.ds(pl.multiple_of((b * 2 + c) * part, part), part)

    def twin_copy(i, b):
        return pltpu.make_async_remote_copy(
            src_ref=grads[i][0].at[block(i, b, 1 - core)],
            dst_ref=grads[i][1].at[b],
            send_sem=twin_ss.at[i],
            recv_sem=twin_rs.at[i, b],
            device_id={"dp": g + 1 - 2 * core},
            device_id_type=MESH,
        )

    def ring_copy(i, way, s):
        grad, _, ring, _ = grads[i]
        mid = grad.shape[1] // 2
        if s == 0:
            b = lax.rem(z + half, n_z)
            cols = pl.ds(way * mid, mid)
        else:
            b = lax.rem(z + (half - s) * (1 - 2 * way) + n_z, n_z)
            cols = pl.ds(0, 2 * mid)
        return pltpu.make_async_remote_copy(
            src_ref=grad.at[block(i, b, core), cols],
            dst_ref=ring.at[way, s, :, cols],
            send_sem=ring_ss.at[i],
            recv_sem=ring_rs.at[i, way, s],
            device_id={"dp": lax.rem(g + 2 * (1 - 2 * way) + n_dp, n_dp)},
            device_id_type=MESH,
        )

    def ring_step(i, s):
        grad, twin, ring, _ = grads[i]
        mid = grad.shape[1] // 2
        if s == 0:
            b = lax.rem(z + half, n_z)
            here = block(i, b, core)
            twin_copy(i, b).wait_recv()
            grad[here, :] = (grad[here, :].astype(F32) + twin[b].astype(F32)).astype(BF)
            ring_copy(i, 0, 0).start()
            ring_copy(i, 1, 0).start()
            return
        for way in range(2):
            b = lax.rem(z + (half - s) * (1 - 2 * way) + n_z, n_z)
            here = block(i, b, core)
            twin_copy(i, b).wait_recv()
            ring_copy(i, way, s - 1).wait_recv()
            if s == 1:
                near, far = pl.ds(way * mid, mid), pl.ds((1 - way) * mid, mid)
                grad[here, near] = (
                    grad[here, near].astype(F32)
                    + twin[b, :, near].astype(F32)
                    + ring[way, 0, :, near].astype(F32)
                ).astype(BF)
                grad[here, far] = (
                    grad[here, far].astype(F32) + twin[b, :, far].astype(F32)
                ).astype(BF)
            else:
                grad[here, :] = (
                    grad[here, :].astype(F32)
                    + twin[b].astype(F32)
                    + ring[way, s - 1].astype(F32)
                ).astype(BF)
            ring_copy(i, way, s).start()

    def ring_last(i):
        grad, twin, ring, out = grads[i]
        twin_copy(i, z).wait_recv()
        ring_copy(i, 0, half - 1).wait_recv()
        ring_copy(i, 1, half - 1).wait_recv()
        here = block(i, z, core)
        out[...] = (
            grad[here, :].astype(F32)
            + twin[z].astype(F32)
            + ring[0, half - 1].astype(F32)
            + ring[1, half - 1].astype(F32)
        ).astype(BF)

    pair = width // n_z

    def ring_order(k):
        d = half - lax.div(k + 1, 2)
        way = 2 * lax.rem(k, 2) - 1
        return lax.rem(z + way * d + n_z, n_z)

    def gate_up(lo, hi):
        @pl.loop(lo, hi)
        def _(k):
            b = ring_order(k)
            cols = pl.ds(pl.multiple_of(b * pair, pair), pair)
            x_part = x_recv[:, :, :, cols].reshape(slots, pair)
            sums = contract(x_part, both[...], 0, 0).astype(BF)
            grad_g[cols, :] = sums[:, :ff]
            grad_u[cols, :] = sums[:, ff:]
            twin_copy(1, b).start()
            twin_copy(2, b).start()

    wide = min(WIDE, width)

    def down_units(lo, hi):
        per = width // wide

        @pl.loop(lo * per, hi * per, unroll=2)
        def _(j):
            units = pl.ds(pl.multiple_of(lax.div(j, per) * ftile, ftile), ftile)
            cols = pl.ds(pl.multiple_of(lax.rem(j, per) * wide, wide), wide)
            grad_d[units, cols] = contract(
                hid[:, units], y_recv[:, :, :, cols].reshape(slots, wide), 0, 0
            ).astype(BF)

    def tokens_out():
        o_wait(0)
        o_wait(1)

        @pl.loop(0, nd, unroll=2)
        def _(j):
            cols = pl.ds(pl.multiple_of(j * dtile, dtile), dtile)
            back = o_recv[:, :, :, cols].reshape(slots, dtile)
            out_ref[:, cols] = (
                contract(hi[...], back, 0, 0) + contract(low[...], back, 0, 0)
            ).astype(BF)

    def tokens_dx(p):
        b_wait(p)

        @pl.loop(0, nd, unroll=2)
        def _(j):
            cols = pl.ds(pl.multiple_of(j * dtile, dtile), dtile)
            back = contract(
                pick[p * n_rows : (p + 1) * n_rows, :],
                b_recv[p, :, :, cols].reshape(n_rows, dtile),
                0,
                0,
            )
            if p == 0:
                dx_half[:, cols] = back
            else:
                dx_ref[:, cols] = (dx_half[:, cols] + back).astype(BF)

    cut1 = nf // 3

    first_products()
    x_of[1][1](0)
    hidden_units(0)
    output_rows(0)
    x_of[1][1](1)
    o_start(0)
    hidden_units(1)
    gate_up(0, 1)
    down_units(0, cut1)
    gate_up(1, 2)
    ring_step(1, 0)
    ring_step(2, 0)
    down_units(cut1, nf)

    @pl.loop(0, n_z)
    def _(k):
        twin_copy(0, ring_order(k)).start()

    gate_up(2, 3)
    ring_step(0, 0)
    output_rows(1)
    o_start(1)
    ring_step(1, 1)
    ring_step(2, 1)
    gate_up(3, min(5, n_z))
    ring_step(0, 1)
    input_rows(0, nd)
    b_start(0)
    b_start(1)
    if half > 2:
        ring_step(1, 2)
    if n_z > 5:
        gate_up(5, n_z)
    if half > 2:
        ring_step(2, 2)
        ring_step(0, 2)
    for s in range(3, half):
        for i in (1, 2, 0):
            ring_step(i, s)
    tokens_out()
    tokens_dx(0)
    tokens_dx(1)
    for i in (1, 2, 0):
        ring_last(i)

    for done in (
        meta_done,
        v_done,
        seqs_of[0][2],
        seqs_of[1][2],
        x_of[0][2],
        x_of[1][2],
        y_done,
        o_done,
        b_done,
    ):
        done()

    for i in range(3):
        grad, twin, _, _ = grads[i]
        part = twin.shape[1]
        for sem, count in ((twin_ss, n_z), (ring_ss, n_z - 1)):
            rows_sent = pl.ds(0, count * part)
            pltpu.make_async_remote_copy(
                src_ref=grad.at[rows_sent],
                dst_ref=grad.at[rows_sent],
                send_sem=sem.at[i],
                recv_sem=sem.at[i],
                device_id={"dp": g + 1 - 2 * core},
                device_id_type=MESH,
            ).wait_send()


def settle_kernel(*refs):
    n = (len(refs) - 1) // 2
    copies = [pltpu.make_async_copy(refs[i], refs[n + i], refs[2 * n].at[i]) for i in range(n)]
    for copy in copies:
        copy.start()
    for copy in copies:
        copy.wait()


def settle(arrays):
    n = len(arrays)
    return pl.pallas_call(
        settle_kernel,
        out_shape=[jax.ShapeDtypeStruct(a.shape, a.dtype) for a in arrays],
        in_specs=[pl.BlockSpec(memory_space=pltpu.VMEM)] * n,
        out_specs=[pl.BlockSpec(memory_space=pl.ANY)] * n,
        scratch_shapes=[pltpu.SemaphoreType.DMA((n,))],
        compiler_params=pltpu.CompilerParams(vmem_limit_bytes=4 * 1024 * 1024),
    )(*[pltpu.with_memory_space_constraint(a, pltpu.VMEM) for a in arrays])


def on_device(
    n_dp,
    n_ex,
    gen_rows,
    gen_lengths,
    gen_adv,
    destination,
    expert_ids,
    gate_values,
    cotangent,
    w_gate,
    w_up,
    w_down,
):
    rows, width = gen_rows.shape
    seqs = destination.shape[2]
    slot = rows // seqs
    ff = w_gate.shape[2]
    cap = 2 * rows * expert_ids.shape[1] // n_ex
    slots = n_ex * cap
    n_z = n_dp // 2
    lanes = max(cap, 128)
    vmem = pl.BlockSpec(memory_space=pltpu.VMEM)
    hbm = pl.BlockSpec(memory_space=pl.ANY)
    dma = pltpu.SemaphoreType.DMA
    part, part_d = width // n_dp, ff // n_dp
    buffers = [pltpu.VMEM((2, n_ex, cap // 2, width), BF)] * 8
    ring = [
        pltpu.VMEM((2, n_z // 2, p, c), BF) for p, c in ((part, ff), (part, ff), (part_d, width))
    ]
    twin = [pltpu.VMEM((n_z, p, c), BF) for p, c in ((part, ff), (part, ff), (part_d, width))]
    outs = pl.pallas_call(
        functools.partial(step_kernel, n_dp, n_ex, slot, cap),
        out_shape=(
            pltpu.VMEM((rows, width), BF),
            pltpu.VMEM((rows, width), BF),
            pltpu.VMEM((part, ff), BF),
            pltpu.VMEM((part, ff), BF),
            pltpu.VMEM((part_d, width), BF),
        ),
        in_specs=[vmem] * 5 + [hbm] * 5,
        out_specs=[vmem] * 5,
        scratch_shapes=[
            pltpu.VMEM((rows, width), BF),
            pltpu.VMEM((rows, width), BF),
            pltpu.VMEM((width, ff), BF),
            pltpu.VMEM((width, ff), BF),
            pltpu.VMEM((ff, width), BF),
            pltpu.VMEM((n_dp, 8, 128), F32),
            pltpu.VMEM((n_dp, 8, 128), F32),
            pltpu.VMEM((1, n_ex, 8, lanes), F32),
            pltpu.VMEM((1, n_ex, 8, lanes), F32),
            pltpu.VMEM((2, n_dp, slot, width // 2), BF),
            pltpu.VMEM((2, n_dp, slot, width // 2), BF),
            *buffers,
            pltpu.VMEM((slots, rows), BF),
            pltpu.VMEM((slots, rows), BF),
            pltpu.VMEM((slots, rows), BF),
            pltpu.VMEM((rows, width), F32),
            pltpu.VMEM((slots, ff), F32),
            pltpu.VMEM((slots, ff), F32),
            pltpu.VMEM((slots, ff), F32),
            pltpu.VMEM((slots, ff), BF),
            pltpu.VMEM((slots, 2 * ff), BF),
            pltpu.VMEM((width, ff), BF),
            pltpu.VMEM((width, ff), BF),
            pltpu.VMEM((ff, width), BF),
            *twin,
            *ring,
            dma((5,)),
            dma((3,)),
            dma((1, 3)),
            dma((2, 3)),
            dma((2, 2, 3)),
            *([dma((2, 3))] * 3),
            dma((3,)),
            dma((3, n_z)),
            dma((3,)),
            dma((3, 2, n_z // 2)),
        ],
        compiler_params=pltpu.CompilerParams(
            collective_id=0, has_side_effects=True, vmem_limit_bytes=62 * 1024 * 1024
        ),
    )(
        destination[0],
        gen_lengths[0],
        gen_adv[0],
        expert_ids.T,
        gate_values.T,
        gen_rows,
        cotangent,
        w_gate[0],
        w_up[0],
        w_down[0],
    )
    outs = settle(outs)
    return outs[0], outs[1], outs[2][None], outs[3][None], outs[4][None]


def solution(mesh):
    n_dp, n_ex = mesh.shape["dp"], mesh.shape["expert"]
    in_specs = (
        P(("dp", "expert"), None),
        P("dp", "expert", None),
        P("dp", "expert", None),
        P("dp", "expert", None),
        P(("dp", "expert"), None),
        P(("dp", "expert"), None),
        P(("dp", "expert"), None),
        P("expert", None, None),
        P("expert", None, None),
        P("expert", None, None),
    )
    out_specs = (
        P(("dp", "expert"), None),
        P(("dp", "expert"), None),
        P("expert", "dp", None),
        P("expert", "dp", None),
        P("expert", "dp", None),
    )
    return jax.shard_map(
        functools.partial(on_device, n_dp, n_ex),
        mesh=mesh,
        in_specs=in_specs,
        out_specs=out_specs,
        check_vma=False,
    )
```
